32 devices in a mesh: gx: 16 (over z, y, core), gy: 2 (over x).
Axes of the slice: x: 2, y: 2, z: 4, core: 2. Of those that a mesh axis runs over, the one named last changes fastest.
Arguments:
- target: float32 [256, 128, 256], P('gx', None, 'gy'), may hold values from -6 to 6
- plane_xy: float32 [32, 256, 256], P(None, 'gx', 'gy'), may hold values from 0.4 to 1.6
- plane_xz: float32 [32, 256, 128], P(None, 'gx', 'gy'), may hold values from 0.4 to 1.6
- plane_yz: float32 [32, 128, 256], P(None, 'gx', 'gy'), may hold values from 0.4 to 1.6
- first_xy: float32 [32, 256, 256], P(None, 'gx', 'gy'), may hold values from -6 to 6
- first_xz: float32 [32, 256, 128], P(None, 'gx', 'gy'), may hold values from -6 to 6
- first_yz: float32 [32, 128, 256], P(None, 'gx', 'gy'), may hold values from -6 to 6
- second_xy: float32 [32, 256, 256], P(None, 'gx', 'gy'), may hold values from 0.5 to 8
- second_xz: float32 [32, 256, 128], P(None, 'gx', 'gy'), may hold values from 0.5 to 8
- second_yz: float32 [32, 128, 256], P(None, 'gx', 'gy'), may hold values from 0.5 to 8
- w_hidden: bfloat16 [32, 32], replicated, may hold values from -1 to 1
- b_hidden: float32 [32], replicated, may hold values from -3 to 3
- w_output: bfloat16 [32], replicated, may hold values from -1 to 1
- b_output: float32 [1], replicated, may hold values from -3 to 3
Outputs:
- updated_xy: float32 [32, 256, 256], P(None, 'gx', 'gy')
- updated_xz: float32 [32, 256, 128], P(None, 'gx', 'gy')
- updated_yz: float32 [32, 128, 256], P(None, 'gx', 'gy')
- mean_xy: float32 [32, 256, 256], P(None, 'gx', 'gy')
- mean_xz: float32 [32, 256, 128], P(None, 'gx', 'gy')
- mean_yz: float32 [32, 128, 256], P(None, 'gx', 'gy')
- square_xy: float32 [32, 256, 256], P(None, 'gx', 'gy')
- square_xz: float32 [32, 256, 128], P(None, 'gx', 'gy')
- square_yz: float32 [32, 128, 256], P(None, 'gx', 'gy')
The draws below stay inside these ranges and needn't reach their ends.
All inputs are finite; a program needn't handle non-finite values.
Results may differ from the reference program's by a relative error of at most 0.00053.
Values sent between devices are 32-bit elements; how exact they have to be, the bound alone decides.
No kernel may reach another device: no remote copies, remote signals or barrier semaphores. Data moves between devices by JAX's collectives and lax.ppermute only.
A program may use at most 64 MiB of HBM per device.

```python
import math
import jax
import jax.numpy as jnp
from jax import lax

C = 32
HIDDEN_SIZE = 32
Z = 128
STEPS = 2
START = 20
X = 256
Y = 256


def shard_levels(key, extent, shards, least, top_value):
    gain = 1.0
    for dim, parts in shards:
        steps = jax.random.uniform(jax.random.fold_in(jax.random.fold_in(key, 6), dim), (parts,), jnp.float32, least / len(shards), top_value / len(shards))
        gain = gain * jnp.repeat(jnp.exp(steps), extent[dim] // parts).reshape((-1,) + (1,) * (len(extent) - 1 - dim))
    return gain


def centred(key, dims, width, limit, pieces=(), kind=jnp.bfloat16):
    array = width * jax.random.normal(key, dims, jnp.float32)
    if pieces:
        array = array * shard_levels(key, dims, pieces, -0.22, 0.18)
    return jnp.clip(array, -limit, limit).astype(kind)


def setup_inputs(seed: int = 0) -> dict:
    key_of = jax.random.split(jax.random.key(seed), 15)
    return {
        "target": centred(key_of[0], (X, Z, Y), 1.0, 6.0, ((0, 16), (2, 2)), jnp.float32),
        "plane_xy": jnp.clip(0.4 + 1.2 * jax.random.uniform(key_of[1], (C, X, Y), jnp.float32) ** shard_levels(key_of[1], (C, X, Y), ((1, 16), (2, 2)), -0.2, 0.2), 0.4, 1.6),
        "plane_xz": jnp.clip(0.4 + 1.2 * jax.random.uniform(key_of[2], (C, X, Z), jnp.float32) ** shard_levels(key_of[2], (C, X, Z), ((1, 16), (2, 2)), -0.2, 0.2), 0.4, 1.6),
        "plane_yz": jnp.clip(0.4 + 1.2 * jax.random.uniform(key_of[3], (C, Z, Y), jnp.float32) ** shard_levels(key_of[3], (C, Z, Y), ((1, 16), (2, 2)), -0.2, 0.2), 0.4, 1.6),
        "first_xy": centred(key_of[4], (C, X, Y), 1.0, 6.0, ((1, 16), (2, 2)), jnp.float32),
        "first_xz": centred(key_of[5], (C, X, Z), 1.0, 6.0, ((1, 16), (2, 2)), jnp.float32),
        "first_yz": centred(key_of[6], (C, Z, Y), 1.0, 6.0, ((1, 16), (2, 2)), jnp.float32),
        "second_xy": jnp.clip(jnp.exp(math.log(8.0) - 2.7725887 * jax.random.uniform(key_of[7], (C, X, Y), jnp.float32) ** shard_levels(key_of[7], (C, X, Y), ((1, 16), (2, 2)), -0.2, 0.2)), 0.5, 8.0),
        "second_xz": jnp.clip(jnp.exp(math.log(8.0) - 2.7725887 * jax.random.uniform(key_of[8], (C, X, Z), jnp.float32) ** shard_levels(key_of[8], (C, X, Z), ((1, 16), (2, 2)), -0.2, 0.2)), 0.5, 8.0),
        "second_yz": jnp.clip(jnp.exp(math.log(8.0) - 2.7725887 * jax.random.uniform(key_of[9], (C, Z, Y), jnp.float32) ** shard_levels(key_of[9], (C, Z, Y), ((1, 16), (2, 2)), -0.2, 0.2)), 0.5, 8.0),
        "w_hidden": centred(key_of[10], (C, HIDDEN_SIZE), C ** -0.5, 1.0),
        "b_hidden": centred(key_of[11], (HIDDEN_SIZE,), 0.5, 3.0, (), jnp.float32),
        "w_output": centred(key_of[12], (HIDDEN_SIZE,), HIDDEN_SIZE ** -0.5, 1.0),
        "b_output": centred(key_of[13], (1,), 0.5, 3.0, (), jnp.float32),
    }


SMOOTHING = 0.5
BETA_ONE = 0.9
BETA_TWO = 0.99
LEARN_RATE = 0.01
EPSILON = 1e-08

def rounded(values):
    return lax.optimization_barrier(values.astype(jnp.bfloat16)).astype(jnp.float32)

def smooth(plane):
    down = plane[:, 1:, :] - plane[:, :-1, :]
    down = jnp.pad(down, ((0, 0), (1, 1), (0, 0)))
    across = plane[:, :, 1:] - plane[:, :, :-1]
    across = jnp.pad(across, ((0, 0), (0, 0), (1, 1)))
    return 2.0 * SMOOTHING * (down[:, :-1, :] - down[:, 1:, :] + across[:, :, :-1] - across[:, :, 1:])

def data_grads(target, plane_xy, plane_xz, plane_yz, w_hidden, b_hidden, w_output, b_output):
    weights_in = w_hidden.astype(jnp.float32)
    weights_out = w_output.astype(jnp.float32)

    def one_row(running, inputs):
        target_row, row_xy, row_xz = inputs
        cross = row_xz[:, :, None] * plane_yz
        features = rounded(row_xy[:, None, :] * cross)
        preact = jnp.einsum('ch,czy->hzy', weights_in, features) + b_hidden[:, None, None]
        sigma = jax.nn.sigmoid(preact)
        hidden = rounded(preact * sigma)
        output = jnp.einsum('h,hzy->zy', weights_out, hidden) + b_output[0]
        residual = output - target_row
        back_hidden = rounded(weights_out[:, None, None] * residual[None] * (sigma * (1.0 + preact * (1.0 - sigma))))
        back_feature = jnp.einsum('ch,hzy->czy', weights_in, back_hidden)
        grad_row_xy = lax.optimization_barrier(jnp.sum(back_feature * cross, axis=1))
        with_xy = back_feature * row_xy[:, None, :]
        grad_row_xz = lax.optimization_barrier(jnp.sum(with_xy * plane_yz, axis=2))
        running = running + with_xy * row_xz[:, :, None]
        return (running, (grad_row_xy, grad_row_xz))
    start = jnp.zeros(plane_yz.shape, jnp.float32)
    grad_yz, (rows_xy, rows_xz) = lax.scan(one_row, start, (target, jnp.moveaxis(plane_xy, 1, 0), jnp.moveaxis(plane_xz, 1, 0)))
    return (jnp.moveaxis(rows_xy, 0, 1), jnp.moveaxis(rows_xz, 0, 1), grad_yz)

def adam(plane, first, second, grads, count):
    first = BETA_ONE * first + (1.0 - BETA_ONE) * grads
    second = BETA_TWO * second + (1.0 - BETA_TWO) * grads * grads
    corr_one = 1.0 - BETA_ONE ** count
    corr_two = 1.0 - BETA_TWO ** count
    plane = plane - LEARN_RATE * (first / corr_one) / (jnp.sqrt(second / corr_two) + EPSILON)
    return (plane, first, second)

def reference(target, plane_xy, plane_xz, plane_yz, first_xy, first_xz, first_yz, second_xy, second_xz, second_yz, w_hidden, b_hidden, w_output, b_output):
    for iteration in range(STEPS):
        grad_xy, grad_xz, grad_yz = data_grads(target, plane_xy, plane_xz, plane_yz, w_hidden, b_hidden, w_output, b_output)
        grad_xy = grad_xy + smooth(plane_xy)
        grad_xz = grad_xz + smooth(plane_xz)
        grad_yz = grad_yz + smooth(plane_yz)
        count = START + iteration + 1
        plane_xy, first_xy, second_xy = adam(plane_xy, first_xy, second_xy, grad_xy, count)
        plane_xz, first_xz, second_xz = adam(plane_xz, first_xz, second_xz, grad_xz, count)
        plane_yz, first_yz, second_yz = adam(plane_yz, first_yz, second_yz, grad_yz, count)
    return (plane_xy, plane_xz, plane_yz, first_xy, first_xz, first_yz, second_xy, second_xz, second_yz)
```

```python
import functools
import jax
import jax.numpy as jnp
from jax import lax
from jax.experimental import pallas as pl
from jax.experimental.pallas import tpu as pltpu
from jax.sharding import PartitionSpec as P

STEPS = 2
START = 20


SMOOTHING = 0.5
BETA_ONE = 0.9
BETA_TWO = 0.99
LEARN_RATE = 0.01
EPSILON = 1e-08

LANES = 128
BLOCK = 256
ROWS = 16
BOTH = ("gx", "gy")
f32 = jnp.float32
bf16 = jnp.bfloat16


def ring_order(chips):
    return list(range(0, chips, 2)) + list(range(chips - 1, 0, -2))


def send(x, move):
    n, peers = lax.axis_size("gx"), lax.axis_size("gy")
    pairs = []
    for g in range(n):
        for y in range(peers):
            to = move(g // 2, g % 2, y)
            if to is not None:
                pairs.append((g * peers + y, (to[0] * 2 + to[1]) * peers + to[2]))
    return lax.ppermute(x, BOTH, pairs)


def to_core(x):
    return send(x, lambda k, c, y: (k, 1 - c, y))


def to_ring(x, step):
    chips = lax.axis_size("gx") // 2
    order = ring_order(chips)
    at = {k: i for i, k in enumerate(order)}
    return send(x, lambda k, c, y: (order[(at[k] + step) % chips], c, y))


def to_gy(x, step):
    peers = lax.axis_size("gy")
    return send(x, lambda k, c, y: (k, c, (y + step) % peers))


def grads_kernel(
    slot_yz, slot_xz, w_in, w_out, w_back, bias, scale, target, xy, xza, xzb, yza, yzb, gxy, gxz, gyz
):
    p = pl.program_id(0)
    x_count, y_count, _ = xy.shape
    z_count = target.shape[2] // 2
    block_yz = jnp.concatenate([yza[0], yzb[0]], axis=1)

    @pl.when(p == 0)
    def _():
        gxy[...] = jnp.zeros_like(gxy)

    gyz[...] = jnp.zeros_like(gyz)
    row = lax.broadcasted_iota(jnp.int32, (2 * z_count, BLOCK), 0) % z_count
    col = lax.broadcasted_iota(jnp.int32, (2 * z_count, BLOCK), 1) // 32
    pick = jnp.where(row == p * 8 + col, -1.0, 0.0).astype(bf16)
    w_res = jnp.concatenate([w_out[...], pick], axis=0)

    def some_rows(i, carry):
        xs = [i * ROWS + j for j in range(ROWS)]
        xzs = [
            jnp.concatenate([xza[0, pl.ds(x, 1), :], xzb[0, pl.ds(x, 1), :]], axis=1) for x in xs
        ]
        xys = [jnp.concatenate([xy[x], xy[x]], axis=1) for x in xs]
        features = jnp.concatenate(
            [(a * block_yz * r).astype(bf16) for a, r in zip(xys, xzs)], axis=0
        )
        half = jnp.dot(features, w_in[...], preferred_element_type=f32) + bias[...]
        t = jnp.tanh(half)
        up = 1.0 + t
        hidden = half * up
        slope = (up + hidden * (1.0 - t)) * scale[...]
        wanted = jnp.concatenate([target[x] for x in xs], axis=0)
        residual = jnp.dot(
            jnp.concatenate([hidden.astype(bf16), wanted], axis=1),
            w_res,
            preferred_element_type=f32,
        )
        back_hidden = (residual * slope).astype(bf16)
        back = jnp.dot(back_hidden, w_back[...], preferred_element_type=f32)
        total = None
        for j, x in enumerate(xs):
            b = back[j * y_count : (j + 1) * y_count]
            e = b * xzs[j]
            k = e * block_yz
            gxy[x] += k[:, :LANES] + k[:, LANES:]
            part = e * xys[j]
            total = part if total is None else total + part
            line = jnp.sum(b * (xys[j] * block_yz), axis=0, keepdims=True)
            gxz[0, pl.ds(x, 1), :] = line[:, :LANES]
            gxz[1, pl.ds(x, 1), :] = line[:, LANES:]
        gyz[0] += total[:, :LANES]
        gyz[1] += total[:, LANES:]
        return carry

    lax.fori_loop(0, x_count // ROWS, some_rows, 0)


def block_grads(slot_yz, slot_xz, weights, target, xy, xz, yz):
    tiles = yz.shape[0]
    x_count, y_count, _ = xy.shape

    def whole(a):
        return pl.BlockSpec(a.shape, lambda p, *_: (0,) * a.ndim)

    def tile_of(which, half, rows):
        return pl.BlockSpec(
            (1, rows, LANES), lambda p, sy, sx: ((sy, sx)[which][2 * p + half], 0, 0)
        )

    flops = 3 * 2 * x_count * y_count * tiles * LANES * BLOCK
    return pl.pallas_call(
        grads_kernel,
        grid_spec=pltpu.PrefetchScalarGridSpec(
            num_scalar_prefetch=2,
            grid=(tiles // 2,),
            in_specs=[whole(w) for w in weights]
            + [
                whole(target),
                whole(xy),
                tile_of(1, 0, x_count),
                tile_of(1, 1, x_count),
                tile_of(0, 0, y_count),
                tile_of(0, 1, y_count),
            ],
            out_specs=[
                whole(xy),
                pl.BlockSpec((2, x_count, LANES), lambda p, *_: (p, 0, 0)),
                pl.BlockSpec((2, y_count, LANES), lambda p, *_: (p, 0, 0)),
            ],
        ),
        out_shape=[
            jax.ShapeDtypeStruct(xy.shape, f32),
            jax.ShapeDtypeStruct((tiles, x_count, LANES), f32),
            jax.ShapeDtypeStruct((tiles, y_count, LANES), f32),
        ],
        compiler_params=pltpu.CompilerParams(vmem_limit_bytes=58 * 2**20),
        cost_estimate=pl.CostEstimate(flops=flops, bytes_accessed=16 * 2**20, transcendentals=0),
    )(slot_yz, slot_xz, *weights, target, xy, xz, xz, yz, yz)


def lanes_xy(plane):
    return jnp.tile(plane.transpose(1, 2, 0), (1, 1, LANES // plane.shape[0]))


def lanes_xz(plane):
    c, x, z = plane.shape
    per = LANES // c
    return plane.reshape(c, x, z // per, per).transpose(2, 1, 3, 0).reshape(z // per, x, LANES)


def plane_xz_of(tiles, c):
    z, x, _ = tiles.shape
    per = LANES // c
    return tiles.reshape(z, x, per, c).transpose(3, 1, 0, 2).reshape(c, x, z * per)


def lanes_yz(plane):
    c, z, y = plane.shape
    per = LANES // c
    return plane.reshape(c, z // per, per, y).transpose(1, 3, 2, 0).reshape(z // per, y, LANES)


def plane_yz_of(tiles, c):
    z, y, _ = tiles.shape
    per = LANES // c
    return tiles.reshape(z, y, per, c).transpose(3, 0, 2, 1).reshape(c, z * per, y)


def gather_ring(own):
    steps = lax.axis_size("gx") // 4
    middle = own.shape[1] // 2
    slots = [own]
    left, right = own, own
    for d in range(1, steps):
        left, right = to_ring(left, 1), to_ring(right, -1)
        slots += [left, right]
    first, second = to_ring(left[:, :middle], 1), to_ring(right[:, middle:], -1)
    slots.append(jnp.concatenate([first, second], axis=1))
    return jnp.concatenate(slots, axis=0)


def ring_tables(chips):
    order = ring_order(chips)
    at = {k: i for i, k in enumerate(order)}
    slots, owners = [], []
    for k in range(chips):
        row = []
        for other in range(chips):
            o = (at[other] - at[k]) % chips
            row.append(2 * o if o < chips // 2 else 2 * (chips - o) - 1)
        slots.append(row)
        owners.append([order[(at[k] + o) % chips] for o in range(chips)])
    return jnp.array(slots, jnp.int32), jnp.array(owners, jnp.int32)


def scatter_ring(tiles, owners, per):
    chips = lax.axis_size("gx") // 2
    middle = tiles.shape[1] // 2

    def chunk(o):
        return lax.dynamic_slice_in_dim(tiles, owners[o % chips] * per, per, axis=0)

    far = chunk(chips // 2)
    ahead, behind = to_ring(far[:, :middle], 1), to_ring(far[:, middle:], -1)
    for d in range(chips // 2 - 1, 0, -1):
        a, b = chunk(d), chunk(-d)
        if d == chips // 2 - 1:
            a = jnp.concatenate([a[:, :middle] + ahead, a[:, middle:]], axis=1)
            b = jnp.concatenate([b[:, :middle], b[:, middle:] + behind], axis=1)
        else:
            a, b = a + ahead, b + behind
        ahead, behind = to_ring(a, 1), to_ring(b, -1)
    return chunk(0) + ahead + behind


def borders(planes):
    n, peers = lax.axis_size("gx"), lax.axis_size("gy")
    up = [(i, i + 1) for i in range(n - 1)]
    last = jnp.concatenate([p[:, -1, :] for p in planes], axis=1)
    first = jnp.concatenate([p[:, 0, :] for p in planes], axis=1)
    above = lax.ppermute(last, "gx", up)
    below = lax.ppermute(first, "gx", [(j, i) for i, j in up])
    last = jnp.concatenate([p[:, :, -1] for p in planes], axis=1)
    first = jnp.concatenate([p[:, :, 0] for p in planes], axis=1)
    if peers == 2:
        left = right = lax.ppermute(
            jnp.where(lax.axis_index("gy") == 0, last, first), "gy", [(0, 1), (1, 0)]
        )
    else:
        up = [(i, i + 1) for i in range(peers - 1)]
        left = lax.ppermute(last, "gy", up)
        right = lax.ppermute(first, "gy", [(j, i) for i, j in up])
    out = []
    row, col = 0, 0
    for p in planes:
        a, b = p.shape[1:]
        out.append(
            (
                above[:, None, col : col + b],
                below[:, None, col : col + b],
                left[:, row : row + a, None],
                right[:, row : row + a, None],
            )
        )
        row, col = row + a, col + b
    return out


def smooth(plane, around):
    above, below, left, right = around
    rows = jnp.concatenate([above, plane, below], axis=1)
    cols = jnp.concatenate([left, plane, right], axis=2)
    down = rows[:, 1:, :] - rows[:, :-1, :]
    across = cols[:, :, 1:] - cols[:, :, :-1]
    row_count = down.shape[1]
    col_count = across.shape[2]
    row_places = jnp.arange(row_count)
    col_places = jnp.arange(col_count)
    lowest_x = lax.axis_index("gx") == 0
    highest_x = lax.axis_index("gx") == lax.axis_size("gx") - 1
    lowest_y = lax.axis_index("gy") == 0
    highest_y = lax.axis_index("gy") == lax.axis_size("gy") - 1
    row_keeps = jnp.where(
        (row_places == 0) & lowest_x | (row_places == row_count - 1) & highest_x, 0.0, 1.0
    )
    col_keeps = jnp.where(
        (col_places == 0) & lowest_y | (col_places == col_count - 1) & highest_y, 0.0, 1.0
    )
    down = down * row_keeps[None, :, None]
    across = across * col_keeps[None, None, :]
    return (
        2.0 * SMOOTHING * (down[:, :-1, :] - down[:, 1:, :] + across[:, :, :-1] - across[:, :, 1:])
    )


def adam(plane, first, second, grads, count):
    first = BETA_ONE * first + (1.0 - BETA_ONE) * grads
    second = BETA_TWO * second + (1.0 - BETA_TWO) * grads * grads
    corr_one = 1.0 - BETA_ONE**count
    corr_two = 1.0 - BETA_TWO**count
    plane = plane - LEARN_RATE * (first / corr_one) / (jnp.sqrt(second / corr_two) + EPSILON)
    return (plane, first, second)


def split_cores(x, axis, zl):
    c = lax.axis_index("gx") % 2
    shape = x.shape[:axis] + (x.shape[axis] // (2 * zl), 2, zl) + x.shape[axis + 1 :]
    half = x.shape[:axis] + (x.shape[axis] // 2,) + x.shape[axis + 1 :]
    x = x.reshape(shape)
    mine = lax.dynamic_index_in_dim(x, c, axis + 1, keepdims=False)
    other = lax.dynamic_index_in_dim(x, 1 - c, axis + 1, keepdims=False)
    return mine.reshape(half), other.reshape(half)


def make_weights(w_hidden, b_hidden, w_output):
    h = w_hidden.shape[1]
    times = BLOCK // h
    eye = jnp.eye(times, dtype=f32)
    wide = w_hidden.astype(f32)
    out = w_output.astype(f32)
    return (
        jnp.kron(eye, 0.5 * wide).astype(bf16),
        jnp.kron(eye, jnp.broadcast_to(out[:, None], (h, h))).astype(bf16),
        jnp.kron(eye, wide.T).astype(bf16),
        jnp.tile(0.5 * b_hidden, times)[None],
        jnp.tile(0.5 * out, times)[None],
    )


def per_device(
    target,
    plane_xy,
    plane_xz,
    plane_yz,
    first_xy,
    first_xz,
    first_yz,
    second_xy,
    second_xz,
    second_yz,
    w_hidden,
    b_hidden,
    w_output,
    b_output,
):
    n, peers = lax.axis_size("gx"), lax.axis_size("gy")
    chips = n // 2
    gx, gy = lax.axis_index("gx"), lax.axis_index("gy")
    channels, x_count, y_count = plane_xy.shape
    zl, zs = plane_yz.shape[1], plane_xz.shape[2]
    z_per = LANES // channels
    per = zl // z_per
    tiles = chips * per
    tiles_gy = tiles // peers

    slot_table, owner_table = ring_tables(chips)
    slots = lax.dynamic_index_in_dim(slot_table, gx // 2, 0, keepdims=False)
    owners = lax.dynamic_index_in_dim(owner_table, gx // 2, 0, keepdims=False)
    tile = jnp.arange(tiles, dtype=jnp.int32)
    slot_yz = jnp.repeat(slots, per) * per + tile % per
    slot_xz = (gy - tile // tiles_gy) % peers * tiles_gy + tile % tiles_gy

    weights = make_weights(w_hidden, b_hidden, w_output)
    mine, other = split_cores(target - b_output[0], 1, zl)
    wanted = jnp.concatenate([mine, to_core(other)], axis=0).transpose(0, 2, 1)
    high = lax.reduce_precision(wanted, 8, 7)
    wanted = jnp.concatenate([high.astype(bf16), (wanted - high).astype(bf16)], axis=2)

    for iteration in range(STEPS):
        yz = gather_ring(lanes_yz(plane_yz))
        xy = jnp.concatenate([lanes_xy(plane_xy), lanes_xy(to_core(plane_xy))], axis=0)
        mine, other = split_cores(plane_xz, 2, zl)
        own = lanes_xz(jnp.concatenate([mine, to_core(other)], axis=1))
        xz = jnp.concatenate([own] + [to_gy(own, s) for s in range(1, peers)], axis=0)
        around = borders((plane_xy, plane_xz, plane_yz))

        part_xy, part_xz, part_yz = block_grads(slot_yz, slot_xz, weights, wanted, xy, xz, yz)

        part_xy = part_xy.reshape(2 * x_count, y_count, z_per, channels).sum(2).transpose(2, 0, 1)
        grad_xy = part_xy[:, :x_count] + to_core(part_xy[:, x_count:])

        def piece(s):
            return lax.dynamic_slice_in_dim(part_xz, (gy + s) % peers * tiles_gy, tiles_gy, axis=0)

        total = piece(0)
        for s in range(1, peers):
            total = total + to_gy(piece(s), s)
        total = plane_xz_of(total, channels)
        mine, other = total[:, :x_count], to_core(total[:, x_count:])
        even = jnp.where(gx % 2 == 0, mine, other)
        odd = jnp.where(gx % 2 == 0, other, mine)
        shape = (channels, x_count, zs // (2 * zl), zl)
        grad_xz = jnp.stack([even.reshape(shape), odd.reshape(shape)], axis=3).reshape(plane_xz.shape)

        grad_yz = plane_yz_of(scatter_ring(part_yz, owners, per), channels)

        grad_xy = grad_xy + smooth(plane_xy, around[0])
        grad_xz = grad_xz + smooth(plane_xz, around[1])
        grad_yz = grad_yz + smooth(plane_yz, around[2])
        count = START + iteration + 1
        plane_xy, first_xy, second_xy = adam(plane_xy, first_xy, second_xy, grad_xy, count)
        plane_xz, first_xz, second_xz = adam(plane_xz, first_xz, second_xz, grad_xz, count)
        plane_yz, first_yz, second_yz = adam(plane_yz, first_yz, second_yz, grad_yz, count)
    return (
        plane_xy,
        plane_xz,
        plane_yz,
        first_xy,
        first_xz,
        first_yz,
        second_xy,
        second_xz,
        second_yz,
    )


def solution(mesh):
    return jax.shard_map(
        per_device,
        mesh=mesh,
        in_specs=(
            P("gx", None, "gy"),
            P(None, "gx", "gy"),
            P(None, "gx", "gy"),
            P(None, "gx", "gy"),
            P(None, "gx", "gy"),
            P(None, "gx", "gy"),
            P(None, "gx", "gy"),
            P(None, "gx", "gy"),
            P(None, "gx", "gy"),
            P(None, "gx", "gy"),
            P(),
            P(),
            P(),
            P(),
        ),
        out_specs=(
            P(None, "gx", "gy"),
            P(None, "gx", "gy"),
            P(None, "gx", "gy"),
            P(None, "gx", "gy"),
            P(None, "gx", "gy"),
            P(None, "gx", "gy"),
            P(None, "gx", "gy"),
            P(None, "gx", "gy"),
            P(None, "gx", "gy"),
        ),
        check_vma=False,
    )
```

```python
import functools
import jax
import jax.numpy as jnp
from jax import lax
from jax.experimental import pallas as pl
from jax.experimental.pallas import tpu as pltpu
from jax.sharding import PartitionSpec as P

STEPS = 2
START = 20


SMOOTHING = 0.5
BETA_ONE = 0.9
BETA_TWO = 0.99
LEARN_RATE = 0.01
EPSILON = 1e-08

LANES = 128
ROWS = 16
BOTH = ("gx", "gy")
f32 = jnp.float32
bf16 = jnp.bfloat16


def ring_order(chips):
    return list(range(0, chips, 2)) + list(range(chips - 1, 0, -2))


def send(x, move):
    n, peers = lax.axis_size("gx"), lax.axis_size("gy")
    pairs = []
    for g in range(n):
        for y in range(peers):
            to = move(g // 2, g % 2, y)
            if to is not None:
                pairs.append((g * peers + y, (to[0] * 2 + to[1]) * peers + to[2]))
    return lax.ppermute(x, BOTH, pairs)


def to_core(x):
    return send(x, lambda k, c, y: (k, 1 - c, y))


def to_ring(x, step):
    chips = lax.axis_size("gx") // 2
    order = ring_order(chips)
    at = {k: i for i, k in enumerate(order)}
    return send(x, lambda k, c, y: (order[(at[k] + step) % chips], c, y))


def to_gy(x, step):
    peers = lax.axis_size("gy")
    return send(x, lambda k, c, y: (k, c, (y + step) % peers))


def offsets(chips):
    out = [0]
    for d in range(1, chips // 2):
        out += [-d, d]
    return out + [chips // 2]


def chip_in_slot(gx, slot, chips):
    k = gx // 2
    at = jnp.where(k % 2 == 0, k // 2, chips - 1 - k // 2)
    i = (at + offsets(chips)[slot] + chips) % chips
    return jnp.where(i < chips // 2, 2 * i, 2 * chips - 1 - 2 * i)


def vmem(count):
    return [pl.BlockSpec(memory_space=pltpu.VMEM)] * count


SCALARS = pl.BlockSpec(memory_space=pltpu.SMEM)


def cost(flops, size):
    return pl.CostEstimate(flops=flops, bytes_accessed=size, transcendentals=0)


def diagonal(small, times):
    size = small.shape[0] * times
    wide = jnp.concatenate([small.astype(f32)] * times, axis=1)
    full = jnp.concatenate([wide] * times, axis=0)
    row = lax.broadcasted_iota(jnp.int32, (size, size), 0) // small.shape[0]
    col = lax.broadcasted_iota(jnp.int32, (size, size), 1) // small.shape[0]
    return jnp.where(row == col, full, 0.0)


def fixed_kernel(
    chips, zl, info, b_output, target_a, target_b, w, w_t, w_o, b, o, wanted, w_in, w_out, w_back, bias, scale
):
    gx = info[0]
    x_count = target_a.shape[0]
    starts = [
        pl.multiple_of((2 * chip_in_slot(gx, s, chips) + gx % 2) * zl, zl) for s in range(chips)
    ]
    for side, ref in enumerate((target_a, target_b)):

        def one(x, carry):
            rows = jnp.concatenate([ref[x, pl.ds(z, zl), :] for z in starts], axis=0)
            rows = rows - b_output[0]
            high = rows.astype(bf16).astype(f32)
            both = jnp.concatenate([high, rows - high], axis=0)
            wanted[side * x_count + x] = both.T.astype(bf16)
            return carry

        lax.fori_loop(0, x_count, one, 0)
    times = w_in.shape[0] // w.shape[0]
    w_in[...] = diagonal(0.5 * w[...].astype(f32), times).astype(bf16)
    w_out[...] = diagonal(w_o[...], times).astype(bf16)
    w_back[...] = diagonal(w_t[...], times).astype(bf16)
    bias[...] = jnp.concatenate([0.5 * b[...]] * times, axis=1)
    scale[...] = jnp.concatenate([0.5 * o[...]] * times, axis=1)


def fixed_parts(info, target, target_b, zl, w_hidden, b_hidden, w_output, b_output):
    chips = lax.axis_size("gx") // 2
    x_count, z_count, y_count = target.shape
    hidden = w_hidden.shape[1]
    width = zl * hidden
    square = jax.ShapeDtypeStruct((width, width), bf16)
    line = jax.ShapeDtypeStruct((1, width), f32)
    return pl.pallas_call(
        functools.partial(fixed_kernel, chips, zl),
        in_specs=[SCALARS, SCALARS] + vmem(7),
        out_specs=vmem(6),
        out_shape=[
            jax.ShapeDtypeStruct((2 * x_count, y_count, z_count), bf16),
            square,
            square,
            square,
            line,
            line,
        ],
        cost_estimate=cost(0, 4 * 2**20),
    )(
        info,
        b_output,
        target,
        target_b,
        w_hidden,
        w_hidden.T,
        jnp.broadcast_to(w_output[:, None], (hidden, hidden)),
        b_hidden[None],
        w_output.astype(f32)[None],
    )


def lanes_kernel(plane, out):
    c, zl, _ = plane.shape
    per = LANES // c
    for t in range(zl // per):
        rows = jnp.concatenate([plane[:, t * per + j, :] for j in range(per)], axis=0)
        out[:, t * LANES : (t + 1) * LANES] = rows.T


def lanes_yz(plane):
    c, zl, y = plane.shape
    return pl.pallas_call(
        lanes_kernel,
        in_specs=vmem(1),
        out_specs=vmem(1)[0],
        out_shape=jax.ShapeDtypeStruct((y, zl * c), f32),
        cost_estimate=cost(0, 2**18),
    )(plane)


def natural_kernel(a, b, d, out):
    c, zl, _ = out.shape
    per = LANES // c
    for t in range(zl // per):
        at = slice(t * LANES, (t + 1) * LANES)
        rows = (a[:, at] + b[:, at] + d[:, at]).T
        for j in range(per):
            out[:, t * per + j, :] = rows[j * c : (j + 1) * c]


def natural_yz(a, b, d, shape):
    return pl.pallas_call(
        natural_kernel,
        in_specs=vmem(3),
        out_specs=vmem(1)[0],
        out_shape=jax.ShapeDtypeStruct(shape, f32),
        cost_estimate=cost(0, 2**19),
    )(a, b, d)


def z_places(gx, gy, slot, chips, peers, zl, zs):
    z = (2 * chip_in_slot(gx, slot, chips) + gx % 2) * zl
    return (gy - z // zs + peers) % peers * zs + z % zs


def spread_kernel(chips, peers, zl, info, xy_a, xy_b, *refs):
    xzs, (xy, xz, held) = refs[: 2 * peers], refs[2 * peers :]
    c, x_count, _ = xy_a.shape
    zs = xzs[0].shape[2]
    for side, ref in enumerate((xy_a, xy_b)):
        for x in range(x_count):
            xy[side * x_count + x] = jnp.concatenate([ref[:, x, :]] * (LANES // c), axis=0).T
    for s in range(peers):
        for side in range(2):
            for x in range(x_count):
                held[s * zs : (s + 1) * zs, side * x_count + x, :] = xzs[2 * s + side][:, x, :].T
    for p in range(chips):
        at = z_places(info[0], info[1], p, chips, peers, zl, zs)
        xz[p] = jnp.concatenate([held[at + j] for j in range(zl)], axis=1)


def spread(info, xy_a, xy_b, xzs, zl):
    peers, chips = lax.axis_size("gy"), lax.axis_size("gx") // 2
    c, x_count, y_count = xy_a.shape
    return pl.pallas_call(
        functools.partial(spread_kernel, chips, peers, zl),
        in_specs=[SCALARS] + vmem(2 + len(xzs)),
        out_specs=vmem(2),
        out_shape=[
            jax.ShapeDtypeStruct((2 * x_count, y_count, LANES), f32),
            jax.ShapeDtypeStruct((chips, 2 * x_count, zl * c), f32),
        ],
        scratch_shapes=[pltpu.VMEM((peers * xzs[0].shape[2], 2 * x_count, c), f32)],
        cost_estimate=cost(0, 4 * 2**20),
    )(info, xy_a, xy_b, *xzs)


def collect_kernel(chips, peers, zl, info, part_xy, part_xz, xy_a, xy_b, *refs):
    outs, held = refs[: 2 * peers], refs[2 * peers]
    c, x_count, _ = xy_a.shape
    zs = outs[0].shape[2]
    for side, ref in enumerate((xy_a, xy_b)):
        for x in range(x_count):
            rows = part_xy[side * x_count + x].T
            ref[:, x, :] = sum(rows[j * c : (j + 1) * c] for j in range(LANES // c))
    held[...] = jnp.zeros_like(held)
    for p in range(chips):
        at = z_places(info[0], info[1], p, chips, peers, zl, zs)
        rows = part_xz[p]
        for j in range(zl):
            held[at + j] = rows[:, j * c : (j + 1) * c]
    for s in range(peers):
        for side in range(2):
            for x in range(x_count):
                outs[2 * s + side][:, x, :] = held[s * zs : (s + 1) * zs, side * x_count + x, :].T


def collect(info, part_xy, part_xz, shape_xy, shape_xz, zl):
    peers, chips = lax.axis_size("gy"), lax.axis_size("gx") // 2
    c, x_count, _ = shape_xy
    outs = pl.pallas_call(
        functools.partial(collect_kernel, chips, peers, zl),
        in_specs=[SCALARS] + vmem(2),
        out_specs=vmem(2 + 2 * peers),
        out_shape=[jax.ShapeDtypeStruct(shape_xy, f32)] * 2
        + [jax.ShapeDtypeStruct(shape_xz, f32)] * (2 * peers),
        scratch_shapes=[pltpu.VMEM((peers * shape_xz[2], 2 * x_count, c), f32)],
        cost_estimate=cost(0, 4 * 2**20),
    )(info, part_xy, part_xz)
    return outs[0], outs[1], outs[2:]


def grads_kernel(count, w_in, w_out, w_back, bias, scale, wanted, xy, xz, *refs):
    yzs, (gxy, gxz), gyzs, (block_yz, total_yz) = (
        refs[:count],
        refs[count : count + 2],
        refs[count + 2 : 2 * count + 2],
        refs[2 * count + 2 :],
    )
    p = pl.program_id(0)
    x_count, y_count, _ = xy.shape
    width = w_in.shape[0]
    z_count = wanted.shape[2] // 2
    zl = z_count // count
    times = width // LANES

    @pl.when(p == 0)
    def _():
        gxy[...] = jnp.zeros_like(gxy)

    for j in range(count):

        @pl.when(p == j)
        def _():
            block_yz[...] = yzs[j][...]

    total_yz[...] = jnp.zeros_like(total_yz)
    row = lax.broadcasted_iota(jnp.int32, (2 * z_count, width), 0) % z_count
    col = lax.broadcasted_iota(jnp.int32, (2 * z_count, width), 1) // (width // zl)
    pick = jnp.where(row == p * zl + col, -1.0, 0.0).astype(bf16)
    w_res = jnp.concatenate([w_out[...], pick], axis=0)

    def some_rows(i, carry):
        xs = [i * ROWS + j for j in range(ROWS)]
        yz = block_yz[...]
        xzs = [xz[0, pl.ds(x, 1), :] for x in xs]
        xys = [jnp.concatenate([xy[x]] * times, axis=1) for x in xs]
        features = jnp.concatenate([(a * yz * r).astype(bf16) for a, r in zip(xys, xzs)], axis=0)
        half = jnp.dot(features, w_in[...], preferred_element_type=f32) + bias[...]
        t = jnp.tanh(half)
        up = 1.0 + t
        hidden = half * up
        slope = (up + hidden * (1.0 - t)) * scale[...]
        residual = jnp.dot(
            jnp.concatenate(
                [hidden.astype(bf16), jnp.concatenate([wanted[x] for x in xs], axis=0)], axis=1
            ),
            w_res,
            preferred_element_type=f32,
        )
        back_hidden = (residual * slope).astype(bf16)
        back = jnp.dot(back_hidden, w_back[...], preferred_element_type=f32)
        total = None
        for j, x in enumerate(xs):
            b = back[j * y_count : (j + 1) * y_count]
            e = b * xzs[j]
            k = e * yz
            gxy[x] += sum(k[:, h * LANES : (h + 1) * LANES] for h in range(times))
            part = e * xys[j]
            total = part if total is None else total + part
            gxz[0, pl.ds(x, 1), :] = jnp.sum(b * (xys[j] * yz), axis=0, keepdims=True)
        total_yz[...] += total
        return carry

    lax.fori_loop(0, x_count // ROWS, some_rows, 0)
    for j in range(count):

        @pl.when(p == j)
        def _():
            gyzs[j][...] = total_yz[...]


def block_grads(weights, wanted, xy, xz, yzs):
    count = len(yzs)
    x_count, y_count, _ = xy.shape
    width = yzs[0].shape[1]

    def whole(a):
        return pl.BlockSpec(a.shape, lambda p: (0,) * a.ndim)

    slot = pl.BlockSpec((1, x_count, width), lambda p: (p, 0, 0))
    outs = pl.pallas_call(
        functools.partial(grads_kernel, count),
        grid=(count,),
        in_specs=[whole(w) for w in weights] + [whole(wanted), whole(xy), slot] + [whole(a) for a in yzs],
        out_specs=[whole(xy), slot] + [whole(a) for a in yzs],
        out_shape=[jax.ShapeDtypeStruct(a.shape, f32) for a in (xy, xz, *yzs)],
        scratch_shapes=[pltpu.VMEM((y_count, width), f32)] * 2,
        compiler_params=pltpu.CompilerParams(vmem_limit_bytes=58 * 2**20),
        cost_estimate=cost(6 * x_count * y_count * count * width * width, 8 * 2**20),
    )(*weights, wanted, xy, xz, *yzs)
    return outs[0], outs[1], outs[2:]


def gather_ring(own):
    steps = lax.axis_size("gx") // 4
    middle = own.shape[0] // 2
    slots = [own]
    left, right = own, own
    for d in range(1, steps):
        left, right = to_ring(left, 1), to_ring(right, -1)
        slots += [left, right]
    first, second = to_ring(left[:middle], 1), to_ring(right[middle:], -1)
    slots.append(jnp.concatenate([first, second], axis=0))
    return slots


def scatter_ring(parts):
    chips = len(parts)
    slot = {o: s for s, o in enumerate(offsets(chips))}
    middle = parts[0].shape[0] // 2
    far = parts[slot[chips // 2]]
    ahead, behind = to_ring(far[:middle], 1), to_ring(far[middle:], -1)
    for d in range(chips // 2 - 1, 0, -1):
        if d == chips // 2 - 1:
            ahead = jnp.pad(ahead, ((0, middle), (0, 0)))
            behind = jnp.pad(behind, ((middle, 0), (0, 0)))
        ahead = to_ring(parts[slot[d]] + ahead, 1)
        behind = to_ring(parts[slot[-d]] + behind, -1)
    return parts[0], ahead, behind


def borders(planes):
    n, peers = lax.axis_size("gx"), lax.axis_size("gy")
    up = [(i, i + 1) for i in range(n - 1)]
    last = jnp.concatenate([p[:, -1, :] for p in planes], axis=1)
    first = jnp.concatenate([p[:, 0, :] for p in planes], axis=1)
    above = lax.ppermute(last, "gx", up)
    below = lax.ppermute(first, "gx", [(j, i) for i, j in up])
    last = jnp.concatenate([p[:, :, -1] for p in planes], axis=1)
    first = jnp.concatenate([p[:, :, 0] for p in planes], axis=1)
    if peers == 2:
        left = right = lax.ppermute(
            jnp.where(lax.axis_index("gy") == 0, last, first), "gy", [(0, 1), (1, 0)]
        )
    else:
        up = [(i, i + 1) for i in range(peers - 1)]
        left = lax.ppermute(last, "gy", up)
        right = lax.ppermute(first, "gy", [(j, i) for i, j in up])
    out = []
    row, col = 0, 0
    for p in planes:
        a, b = p.shape[1:]
        out.append(
            (
                above[:, None, col : col + b],
                below[:, None, col : col + b],
                left[:, row : row + a, None],
                right[:, row : row + a, None],
            )
        )
        row, col = row + a, col + b
    return out


def smooth(plane, around):
    above, below, left, right = around
    rows = jnp.concatenate([above, plane, below], axis=1)
    cols = jnp.concatenate([left, plane, right], axis=2)
    down = rows[:, 1:, :] - rows[:, :-1, :]
    across = cols[:, :, 1:] - cols[:, :, :-1]
    row_count = down.shape[1]
    col_count = across.shape[2]
    row_places = jnp.arange(row_count)
    col_places = jnp.arange(col_count)
    lowest_x = lax.axis_index("gx") == 0
    highest_x = lax.axis_index("gx") == lax.axis_size("gx") - 1
    lowest_y = lax.axis_index("gy") == 0
    highest_y = lax.axis_index("gy") == lax.axis_size("gy") - 1
    row_keeps = jnp.where(
        (row_places == 0) & lowest_x | (row_places == row_count - 1) & highest_x, 0.0, 1.0
    )
    col_keeps = jnp.where(
        (col_places == 0) & lowest_y | (col_places == col_count - 1) & highest_y, 0.0, 1.0
    )
    down = down * row_keeps[None, :, None]
    across = across * col_keeps[None, None, :]
    return (
        2.0 * SMOOTHING * (down[:, :-1, :] - down[:, 1:, :] + across[:, :, :-1] - across[:, :, 1:])
    )


def adam(plane, first, second, grads, count):
    first = BETA_ONE * first + (1.0 - BETA_ONE) * grads
    second = BETA_TWO * second + (1.0 - BETA_TWO) * grads * grads
    corr_one = 1.0 - BETA_ONE**count
    corr_two = 1.0 - BETA_TWO**count
    plane = plane - LEARN_RATE * (first / corr_one) / (jnp.sqrt(second / corr_two) + EPSILON)
    return (plane, first, second)


def per_device(
    target,
    plane_xy,
    plane_xz,
    plane_yz,
    first_xy,
    first_xz,
    first_yz,
    second_xy,
    second_xz,
    second_yz,
    w_hidden,
    b_hidden,
    w_output,
    b_output,
):
    peers = lax.axis_size("gy")
    info = jnp.stack([lax.axis_index("gx"), lax.axis_index("gy")]).astype(jnp.int32)
    zl = plane_yz.shape[1]
    lanes = lanes_yz(plane_yz)
    target_b = to_core(target)
    fixed = None

    for iteration in range(STEPS):
        yzs = gather_ring(lanes)
        xy_b, xz_b = to_core(plane_xy), to_core(plane_xz)
        xzs = [plane_xz, xz_b]
        for s in range(1, peers):
            xzs += [to_gy(plane_xz, s), to_gy(xz_b, s)]
        around = borders((plane_xy, plane_xz, plane_yz))
        if fixed is None:
            fixed = fixed_parts(info, target, target_b, zl, w_hidden, b_hidden, w_output, b_output)
        wanted, weights = fixed[0], fixed[1:]
        xy, xz = spread(info, plane_xy, xy_b, xzs, zl)

        part_xy, part_xz, part_yz = block_grads(weights, wanted, xy, xz, yzs)
        grad_xy, far_xy, parts_xz = collect(
            info, part_xy, part_xz, plane_xy.shape, plane_xz.shape, zl
        )
        grad_xy = grad_xy + to_core(far_xy)
        grad_xz, far_xz = parts_xz[:2]
        for s in range(1, peers):
            grad_xz = grad_xz + to_gy(parts_xz[2 * s], -s)
            far_xz = far_xz + to_gy(parts_xz[2 * s + 1], -s)
        grad_xz = grad_xz + to_core(far_xz)
        grad_yz = natural_yz(*scatter_ring(part_yz), plane_yz.shape)

        grad_xy = grad_xy + smooth(plane_xy, around[0])
        grad_xz = grad_xz + smooth(plane_xz, around[1])
        grad_yz = grad_yz + smooth(plane_yz, around[2])
        count = START + iteration + 1
        plane_yz, first_yz, second_yz = adam(plane_yz, first_yz, second_yz, grad_yz, count)
        if iteration + 1 < STEPS:
            lanes = lanes_yz(plane_yz)
        plane_xy, first_xy, second_xy = adam(plane_xy, first_xy, second_xy, grad_xy, count)
        plane_xz, first_xz, second_xz = adam(plane_xz, first_xz, second_xz, grad_xz, count)
    return (
        plane_xy,
        plane_xz,
        plane_yz,
        first_xy,
        first_xz,
        first_yz,
        second_xy,
        second_xz,
        second_yz,
    )


def solution(mesh):
    return jax.shard_map(
        per_device,
        mesh=mesh,
        in_specs=(
            P("gx", None, "gy"),
            P(None, "gx", "gy"),
            P(None, "gx", "gy"),
            P(None, "gx", "gy"),
            P(None, "gx", "gy"),
            P(None, "gx", "gy"),
            P(None, "gx", "gy"),
            P(None, "gx", "gy"),
            P(None, "gx", "gy"),
            P(None, "gx", "gy"),
            P(),
            P(),
            P(),
            P(),
        ),
        out_specs=(
            P(None, "gx", "gy"),
            P(None, "gx", "gy"),
            P(None, "gx", "gy"),
            P(None, "gx", "gy"),
            P(None, "gx", "gy"),
            P(None, "gx", "gy"),
            P(None, "gx", "gy"),
            P(None, "gx", "gy"),
            P(None, "gx", "gy"),
        ),
        check_vma=False,
    )
```

```python
import functools
import jax
import jax.numpy as jnp
from jax import lax
from jax.experimental import pallas as pl
from jax.experimental.pallas import tpu as pltpu
from jax.sharding import PartitionSpec as P


STEPS = 2
START = 20


SMOOTHING = 0.5
BETA_ONE = 0.9
BETA_TWO = 0.99
LEARN_RATE = 0.01
EPSILON = 1e-08

LANES = 128
CHANNELS = 32
BOTH = ("gx", "gy")
f32 = jnp.float32
bf16 = jnp.bfloat16


def ring_order(chips):
    return list(range(0, chips, 2)) + list(range(chips - 1, 0, -2))


def send(x, move):
    n, peers = lax.axis_size("gx"), lax.axis_size("gy")
    pairs = []
    for g in range(n):
        for y in range(peers):
            to = move(g // 2, g % 2, y)
            if to is not None:
                pairs.append((g * peers + y, (to[0] * 2 + to[1]) * peers + to[2]))
    return lax.ppermute(x, BOTH, pairs)


def to_core(x):
    return send(x, lambda k, c, y: (k, 1 - c, y))


def to_ring(x, step):
    chips = lax.axis_size("gx") // 2
    order = ring_order(chips)
    at = {k: i for i, k in enumerate(order)}
    return send(x, lambda k, c, y: (order[(at[k] + step) % chips], c, y))


def to_gy(x, step):
    peers = lax.axis_size("gy")
    return send(x, lambda k, c, y: (k, c, (y + step) % peers))


def offsets(chips):
    out = [0]
    for d in range(1, chips // 2):
        out += [-d, d]
    return out + [chips // 2]


def chip_in_slot(gx, slot, chips):
    k = gx // 2
    at = jnp.where(k % 2 == 0, k // 2, chips - 1 - k // 2)
    i = (at + offsets(chips)[slot] + chips) % chips
    return jnp.where(i < chips // 2, 2 * i, 2 * chips - 1 - 2 * i)


def vmem(count):
    return [pl.BlockSpec(memory_space=pltpu.VMEM)] * count


SCALARS = pl.BlockSpec(memory_space=pltpu.SMEM)
SMALL = pltpu.CompilerParams(vmem_limit_bytes=20 * 2**20)


def cost(flops, size):
    return pl.CostEstimate(flops=flops, bytes_accessed=size, transcendentals=0)


def diagonal(small, times):
    size = small.shape[0] * times
    wide = jnp.concatenate([small.astype(f32)] * times, axis=1)
    full = jnp.concatenate([wide] * times, axis=0)
    row = lax.broadcasted_iota(jnp.int32, (size, size), 0) // small.shape[0]
    col = lax.broadcasted_iota(jnp.int32, (size, size), 1) // small.shape[0]
    return jnp.where(row == col, full, 0.0)


def fixed_kernel(
    chips, zl, info, b_output, target_a, target_b, w, w_t, w_o, b, o, wanted, w_in, w_out, w_back, bias, scale
):
    gx = info[0]
    x_count = target_a.shape[0]
    starts = [
        pl.multiple_of((2 * chip_in_slot(gx, s, chips) + gx % 2) * zl, zl) for s in range(chips)
    ]
    for side, ref in enumerate((target_a, target_b)):

        def one(x, carry):
            rows = jnp.concatenate([ref[x, pl.ds(z, zl), :] for z in starts], axis=0)
            rows = rows - b_output[0]
            high = rows.astype(bf16).astype(f32)
            both = jnp.concatenate([high, rows - high], axis=0)
            wanted[side * x_count + x] = both.T.astype(bf16)
            return carry

        lax.fori_loop(0, x_count, one, 0)
    times = w_in.shape[0] // w.shape[0]
    w_in[...] = diagonal(0.5 * w[...].astype(f32), times).astype(bf16)
    w_out[...] = diagonal(w_o[...], times).astype(bf16)
    w_back[...] = diagonal(w_t[...], times).astype(bf16)
    bias[...] = jnp.concatenate([0.5 * b[...]] * times, axis=1)
    scale[...] = jnp.concatenate([0.5 * o[...]] * times, axis=1)


def fixed_parts(info, target, target_b, zl, w_hidden, b_hidden, w_output, b_output):
    chips = lax.axis_size("gx") // 2
    x_count, z_count, y_count = target.shape
    hidden = w_hidden.shape[1]
    width = zl * hidden
    square = jax.ShapeDtypeStruct((width, width), bf16)
    line = jax.ShapeDtypeStruct((1, width), f32)
    return pl.pallas_call(
        functools.partial(fixed_kernel, chips, zl),
        in_specs=[SCALARS, SCALARS] + vmem(7),
        out_specs=vmem(6),
        out_shape=[
            jax.ShapeDtypeStruct((2 * x_count, y_count, z_count), bf16),
            square,
            square,
            square,
            line,
            line,
        ],
        compiler_params=SMALL,
        cost_estimate=cost(0, 4 * 2**20),
    )(
        info,
        b_output,
        target,
        target_b,
        w_hidden,
        w_hidden.T,
        jnp.broadcast_to(w_output[:, None], (hidden, hidden)),
        b_hidden[None],
        w_output.astype(f32)[None],
    )


def lanes_kernel(plane, out):
    c, zl, _ = plane.shape
    per = LANES // c
    for t in range(zl // per):
        rows = jnp.concatenate([plane[:, t * per + j, :] for j in range(per)], axis=0)
        out[:, t * LANES : (t + 1) * LANES] = rows.T


def lanes_yz(plane):
    c, zl, y = plane.shape
    return pl.pallas_call(
        lanes_kernel,
        in_specs=vmem(1),
        out_specs=vmem(1)[0],
        out_shape=jax.ShapeDtypeStruct((y, zl * c), f32),
        compiler_params=SMALL,
        cost_estimate=cost(0, 2**18),
    )(plane)


def z_places(gx, gy, slot, chips, peers, zl, zs):
    z = (2 * chip_in_slot(gx, slot, chips) + gx % 2) * zl
    return (gy - z // zs + peers) % peers * zs + z % zs


def spread_kernel(chips, peers, zl, info, xy_a, xy_b, *refs):
    xzs, (xy, xz, held) = refs[: 2 * peers], refs[2 * peers :]
    c, x_count, _ = xy_a.shape
    zs = xzs[0].shape[2]
    for side, ref in enumerate((xy_a, xy_b)):
        for x in range(x_count):
            xy[side * x_count + x] = jnp.concatenate([ref[:, x, :]] * (LANES // c), axis=0).T
    for s in range(peers):
        for side in range(2):
            for x in range(x_count):
                held[s * zs : (s + 1) * zs, side * x_count + x, :] = xzs[2 * s + side][:, x, :].T
    for p in range(chips):
        at = z_places(info[0], info[1], p, chips, peers, zl, zs)
        xz[p] = jnp.concatenate([held[at + j] for j in range(zl)], axis=1)


def spread(info, xy_a, xy_b, xzs, zl):
    peers, chips = lax.axis_size("gy"), lax.axis_size("gx") // 2
    c, x_count, y_count = xy_a.shape
    return pl.pallas_call(
        functools.partial(spread_kernel, chips, peers, zl),
        in_specs=[SCALARS] + vmem(2 + len(xzs)),
        out_specs=vmem(2),
        out_shape=[
            jax.ShapeDtypeStruct((2 * x_count, y_count, LANES), f32),
            jax.ShapeDtypeStruct((chips, 2 * x_count, zl * c), f32),
        ],
        scratch_shapes=[pltpu.VMEM((peers * xzs[0].shape[2], 2 * x_count, c), f32)],
        compiler_params=SMALL,
        cost_estimate=cost(0, 4 * 2**20),
    )(info, xy_a, xy_b, *xzs)


def collect_kernel(chips, peers, zl, info, part_xy, xy_a, xy_b, *refs):
    parts, outs, held = refs[:chips], refs[chips : chips + 2 + 2 * peers], refs[chips + 2 + 2 * peers]
    c, x_count, _ = xy_a.shape
    outs_xz = outs[2:]
    zs = outs_xz[0].shape[2]
    for side, ref in enumerate((xy_a, xy_b)):
        for x in range(x_count):
            rows = part_xy[side * x_count + x].T
            total = sum(rows[j * c : (j + 1) * c] for j in range(LANES // c))
            outs[side][:, x, :] = total / ref[:, x, :]
    held[...] = jnp.zeros_like(held)
    for p in range(chips):
        at = z_places(info[0], info[1], p, chips, peers, zl, zs)
        rows = parts[p][...]
        for j in range(zl):
            held[at + j] = rows[:, j * c : (j + 1) * c]
    for s in range(peers):
        for side in range(2):
            for x in range(x_count):
                outs_xz[2 * s + side][:, x, :] = held[s * zs : (s + 1) * zs, side * x_count + x, :].T


def collect(info, part_xy, xy_a, xy_b, parts_xz, shape_xz, zl):
    peers, chips = lax.axis_size("gy"), lax.axis_size("gx") // 2
    c, x_count, _ = xy_a.shape
    outs = pl.pallas_call(
        functools.partial(collect_kernel, chips, peers, zl),
        in_specs=[SCALARS] + vmem(3 + chips),
        out_specs=vmem(2 + 2 * peers),
        out_shape=[jax.ShapeDtypeStruct(xy_a.shape, f32)] * 2
        + [jax.ShapeDtypeStruct(shape_xz, f32)] * (2 * peers),
        scratch_shapes=[pltpu.VMEM((peers * shape_xz[2], 2 * x_count, c), f32)],
        compiler_params=SMALL,
        cost_estimate=cost(0, 8 * 2**20),
    )(info, part_xy, xy_a, xy_b, *parts_xz)
    return outs[0], outs[1], outs[2:]


def grads_kernel(slots, first, w_in, w_out, w_back, bias, scale, wanted, xy, *refs):
    count = len(slots)
    refs = list(refs)
    take = lambda k: [refs.pop(0) for _ in range(k)]
    xzs, yzs = take(count), take(count)
    before = None if first else take(1)[0]
    gxy = take(1)[0]
    gxzs, gyzs, picks = take(count), take(count), take(count)
    step = pl.program_id(0)
    x_count, y_count, _ = xy.shape
    width = w_in.shape[0]
    z_count = wanted.shape[2] // 2
    zl = width // CHANNELS
    times = width // LANES

    @pl.when(step == 0)
    def _():
        row = lax.broadcasted_iota(jnp.int32, (2 * z_count, width), 0) % z_count
        col = lax.broadcasted_iota(jnp.int32, (2 * z_count, width), 1) // CHANNELS
        for s, pick, gyz in zip(slots, picks, gyzs):
            pick[:width] = w_out[...]
            pick[width:] = jnp.where(row == s * zl + col, -1.0, 0.0).astype(bf16)
            gyz[...] = jnp.zeros_like(gyz)

    for j in range(count):
        yz = yzs[j][...]
        lines = [xzs[j][0, x : x + 1, :] for x in range(x_count)]
        pairs = [jnp.concatenate([xy[x]] * times, axis=1) * yz for x in range(x_count)]
        features = jnp.concatenate([(g * r).astype(bf16) for g, r in zip(pairs, lines)], axis=0)
        half = jnp.dot(features, w_in[...], preferred_element_type=f32) + bias[...]
        t = jnp.tanh(half)
        up = 1.0 + t
        hidden = half * up
        slope = (up + hidden * (1.0 - t)) * scale[...]
        residual = jnp.dot(
            jnp.concatenate(
                [
                    hidden.astype(bf16),
                    jnp.concatenate([wanted[x] for x in range(x_count)], axis=0),
                ],
                axis=1,
            ),
            picks[j][...],
            preferred_element_type=f32,
        )
        back_hidden = (residual * slope).astype(bf16)
        back = jnp.dot(back_hidden, w_back[...], preferred_element_type=f32)
        total = None
        for x in range(x_count):
            b = back[x * y_count : (x + 1) * y_count] * pairs[x]
            gxzs[j][x : x + 1, :] = jnp.sum(b, axis=0, keepdims=True)
            e = b * lines[x]
            folded = sum(e[:, h * LANES : (h + 1) * LANES] for h in range(times))
            if j > 0:
                gxy[x] += folded
            elif first:
                gxy[x] = folded
            else:
                gxy[x] = before[x] + folded
            total = e if total is None else total + e
        gyzs[j][...] += total

    @pl.when(step == 1)
    def _():
        for gyz, ref in zip(gyzs, yzs):
            gyz[...] = gyz[...] / ref[...]


def block_grads(slots, weights, wanted, xy, xz, yzs, before):
    count = len(slots)
    rows, y_count, _ = xy.shape
    rows = rows // 2
    width = yzs[0].shape[1]

    def whole(a):
        return pl.BlockSpec(a.shape, lambda i: (0,) * a.ndim)

    side = pl.BlockSpec((rows, y_count, LANES), lambda i: (i, 0, 0))
    line = pl.BlockSpec((rows, width), lambda i: (i, 0))
    outs = pl.pallas_call(
        functools.partial(grads_kernel, slots, before is None),
        grid=(2,),
        in_specs=[whole(w) for w in weights]
        + [side, side]
        + [pl.BlockSpec((1, rows, width), lambda i, s=s: (s, i, 0)) for s in slots]
        + [whole(a) for a in yzs]
        + ([] if before is None else [side]),
        out_specs=[side] + [line] * count + [whole(a) for a in yzs],
        out_shape=[jax.ShapeDtypeStruct(xy.shape, f32)]
        + [jax.ShapeDtypeStruct((2 * rows, width), f32)] * count
        + [jax.ShapeDtypeStruct(a.shape, f32) for a in yzs],
        scratch_shapes=[pltpu.VMEM((width + wanted.shape[2], width), bf16)] * count,
        compiler_params=pltpu.CompilerParams(vmem_limit_bytes=44 * 2**20),
        cost_estimate=cost(12 * rows * y_count * count * width * width, count * 10 * 2**20),
    )(*weights, wanted, xy, *([xz] * count), *yzs, *([] if before is None else [before]))
    return outs[0], outs[1 : 1 + count], outs[1 + count :]


def near_sides(p, above, below, left, right):
    rows, cols = p.shape[1:]
    row = lax.broadcasted_iota(jnp.int32, p.shape, 1)
    col = lax.broadcasted_iota(jnp.int32, p.shape, 2)
    up = jnp.where(row == 0, above, pltpu.roll(p, 1, 1))
    down = jnp.where(row == rows - 1, below, pltpu.roll(p, rows - 1, 1))
    wide = p if cols % LANES == 0 else jnp.concatenate([p] * (LANES // cols), axis=2)
    back = pltpu.roll(wide, 1, 2)[:, :, :cols]
    ahead = pltpu.roll(wide, wide.shape[2] - 1, 2)[:, :, :cols]
    return up, down, jnp.where(col == 0, left, back), jnp.where(col == cols - 1, right, ahead)


def update(info, ends, count, plane, first, second, grad, borders, at_row, at_col, outs):
    above, below, left, right = borders
    p = plane[...]
    rows, cols = p.shape[1:]
    above = jnp.where(info[0] == 0, p[:, :1, :], above[:, :, at_row : at_row + cols])
    below = jnp.where(info[0] == ends[0], p[:, rows - 1 :, :], below[:, :, at_row : at_row + cols])
    left = jnp.where(info[1] == 0, p[:, :, :1], left[:, at_col : at_col + rows][:, :, None])
    right = jnp.where(info[1] == ends[1], p[:, :, cols - 1 :], right[:, at_col : at_col + rows][:, :, None])
    up, down, back, ahead = near_sides(p, above, below, left, right)
    grad = grad + 2.0 * SMOOTHING * ((p - up) + (p - down) + (p - back) + (p - ahead))
    m = BETA_ONE * first[...] + (1.0 - BETA_ONE) * grad
    v = BETA_TWO * second[...] + (1.0 - BETA_TWO) * grad * grad
    corr_one = 1.0 - BETA_ONE**count
    corr_two = 1.0 - BETA_TWO**count
    outs[1][...] = m
    outs[2][...] = v
    outs[0][...] = p - LEARN_RATE * (m / corr_one) / (jnp.sqrt(v / corr_two) + EPSILON)


def update_two_kernel(ends, count, info, above, below, left, right, *refs):
    borders = (above, below, left, right)
    xy, xz, outs = refs[:5], refs[5:10], refs[10:]
    width_y = xy[0].shape[2]
    rows = xy[0].shape[1]
    update(info, ends, count, *xy[:3], xy[3][...] + xy[4][...], borders, 0, 0, outs[:3])
    update(info, ends, count, *xz[:3], xz[3][...] + xz[4][...], borders, 2 * width_y, rows, outs[3:])


def update_two(info, count, borders, xy, xz):
    ends = (lax.axis_size("gx") - 1, lax.axis_size("gy") - 1)
    shapes = [jax.ShapeDtypeStruct(a.shape, f32) for a in (*xy[:3], *xz[:3])]
    outs = pl.pallas_call(
        functools.partial(update_two_kernel, ends, count),
        in_specs=[SCALARS] + vmem(14),
        out_specs=vmem(6),
        out_shape=shapes,
        compiler_params=SMALL,
        cost_estimate=cost(0, 4 * 2**20),
    )(info, *borders, *xy, *xz)
    return outs[:3], outs[3:]


def update_yz_kernel(ends, count, info, above, below, left, right, plane, first, second, a, b, d, *refs):
    outs, lanes, held = refs[:3], refs[3], refs[4]
    c, zl, width = plane.shape
    per = LANES // c
    for t in range(zl // per):
        at = slice(t * LANES, (t + 1) * LANES)
        rows = (a[:, at] + b[:, at] + d[:, at]).T
        for j in range(per):
            held[:, t * per + j, :] = rows[j * c : (j + 1) * c]
    borders = (above, below, left, right)
    at_col = left.shape[1] - zl
    update(info, ends, count, plane, first, second, held[...], borders, width, at_col, outs)
    lanes_kernel(outs[0], lanes)


def update_yz(info, count, borders, state, parts):
    ends = (lax.axis_size("gx") - 1, lax.axis_size("gy") - 1)
    outs = pl.pallas_call(
        functools.partial(update_yz_kernel, ends, count),
        in_specs=[SCALARS] + vmem(10),
        out_specs=vmem(4),
        out_shape=[jax.ShapeDtypeStruct(a.shape, f32) for a in (*state, parts[0])],
        scratch_shapes=[pltpu.VMEM(state[0].shape, f32)],
        compiler_params=SMALL,
        cost_estimate=cost(0, 2 * 2**20),
    )(info, *borders, *state, *parts)
    return outs[:3], outs[3]


def borders(planes):
    n, peers = lax.axis_size("gx"), lax.axis_size("gy")
    xy, xz, yz = planes
    up = [(i, i + 1) for i in range(n - 1)]
    last = jnp.concatenate([p[:, -1:, :] for p in (xy, yz, xz)], axis=2)
    first = jnp.concatenate([p[:, :1, :] for p in (xy, yz, xz)], axis=2)
    above = lax.ppermute(last, "gx", up)
    below = lax.ppermute(first, "gx", [(j, i) for i, j in up])
    last = jnp.concatenate([p[:, :, -1] for p in (xy, xz, yz)], axis=1)
    first = jnp.concatenate([p[:, :, 0] for p in (xy, xz, yz)], axis=1)
    if peers == 2:
        left = right = lax.ppermute(
            jnp.where(lax.axis_index("gy") == 0, last, first), "gy", [(0, 1), (1, 0)]
        )
    else:
        up = [(i, i + 1) for i in range(peers - 1)]
        left = lax.ppermute(last, "gy", up)
        right = lax.ppermute(first, "gy", [(j, i) for i, j in up])
    return above, below, left, right


def per_device(
    target,
    plane_xy,
    plane_xz,
    plane_yz,
    first_xy,
    first_xz,
    first_yz,
    second_xy,
    second_xz,
    second_yz,
    w_hidden,
    b_hidden,
    w_output,
    b_output,
):
    peers = lax.axis_size("gy")
    info = jnp.stack([lax.axis_index("gx"), lax.axis_index("gy")]).astype(jnp.int32)
    zl = plane_yz.shape[1]
    lanes = lanes_yz(plane_yz)
    target_b = to_core(target)
    fixed = None

    chips = lax.axis_size("gx") // 2
    half = chips // 2
    slot = {o: i for i, o in enumerate(offsets(chips))}
    middle = lanes.shape[0] // 2

    for iteration in range(STEPS):
        back, ahead = {0: lanes}, {0: lanes}
        for d in range(1, half):
            back[d], ahead[d] = to_ring(back[d - 1], 1), to_ring(ahead[d - 1], -1)
        parts = to_ring(back[half - 1][:middle], 1), to_ring(ahead[half - 1][middle:], -1)
        far = jnp.concatenate(parts, axis=0)
        yzs = {0: lanes, half: far}
        for d in range(1, half):
            yzs[-d], yzs[d] = back[d], ahead[d]
        xy_b, xz_b = to_core(plane_xy), to_core(plane_xz)
        xzs = [plane_xz, xz_b]
        for s in range(1, peers):
            xzs += [to_gy(plane_xz, s), to_gy(xz_b, s)]
        if fixed is None:
            fixed = fixed_parts(
                info, target, target_b, zl, w_hidden, b_hidden, w_output, b_output
            )
        wanted, weights = fixed[0], fixed[1:]
        xy, xz = spread(info, plane_xy, xy_b, xzs, zl)

        order = [(0,), (-1,), (1,), (half,)] + [(-d, d) for d in range(half - 1, 1, -1)]
        part_xy, parts_xz, parts_yz = None, {}, {}
        send_ahead, send_back = None, None
        for group in order:
            part_xy, lines, blocks = block_grads(
                [slot[o] for o in group], weights, wanted, xy, xz, [yzs[o] for o in group], part_xy
            )
            for o, line, block in zip(group, lines, blocks):
                parts_xz[slot[o]], parts_yz[o] = line, block
            if group == (0,):
                gated = lax.optimization_barrier((plane_xy, plane_xz, plane_yz, lines[0]))[:3]
                around = borders(gated)
        block = parts_yz[half]
        send_ahead, send_back = to_ring(block[:middle], 1), to_ring(block[middle:], -1)
        for d in range(half - 1, 0, -1):
            if d == half - 1:
                send_ahead = jnp.pad(send_ahead, ((0, middle), (0, 0)))
                send_back = jnp.pad(send_back, ((middle, 0), (0, 0)))
            send_ahead, send_back = parts_yz[d] + send_ahead, parts_yz[-d] + send_back
            send_ahead, send_back = to_ring(send_ahead, 1), to_ring(send_back, -1)

        grad_xy, far_xy, pieces = collect(
            info, part_xy, plane_xy, xy_b, [parts_xz[i] for i in range(chips)], plane_xz.shape, zl
        )
        grad_xz, far_xz = pieces[:2]
        for s in range(1, peers):
            grad_xz = grad_xz + to_gy(pieces[2 * s], -s)
            far_xz = far_xz + to_gy(pieces[2 * s + 1], -s)
        count = START + iteration + 1
        (plane_xy, first_xy, second_xy), (plane_xz, first_xz, second_xz) = update_two(
            info,
            count,
            around,
            (plane_xy, first_xy, second_xy, grad_xy, to_core(far_xy)),
            (plane_xz, first_xz, second_xz, grad_xz, to_core(far_xz)),
        )
        (plane_yz, first_yz, second_yz), lanes = update_yz(
            info, count, around, (plane_yz, first_yz, second_yz), (parts_yz[0], send_ahead, send_back)
        )
    return (
        plane_xy,
        plane_xz,
        plane_yz,
        first_xy,
        first_xz,
        first_yz,
        second_xy,
        second_xz,
        second_yz,
    )


def solution(mesh):
    return jax.shard_map(
        per_device,
        mesh=mesh,
        in_specs=(
            P("gx", None, "gy"),
            P(None, "gx", "gy"),
            P(None, "gx", "gy"),
            P(None, "gx", "gy"),
            P(None, "gx", "gy"),
            P(None, "gx", "gy"),
            P(None, "gx", "gy"),
            P(None, "gx", "gy"),
            P(None, "gx", "gy"),
            P(None, "gx", "gy"),
            P(),
            P(),
            P(),
            P(),
        ),
        out_specs=(
            P(None, "gx", "gy"),
            P(None, "gx", "gy"),
            P(None, "gx", "gy"),
            P(None, "gx", "gy"),
            P(None, "gx", "gy"),
            P(None, "gx", "gy"),
            P(None, "gx", "gy"),
            P(None, "gx", "gy"),
            P(None, "gx", "gy"),
        ),
        check_vma=False,
    )
```

```python
import functools
import jax
import jax.numpy as jnp
from jax import lax
from jax.experimental import pallas as pl
from jax.experimental.pallas import tpu as pltpu
from jax.sharding import PartitionSpec as P


STEPS = 2
START = 20


SMOOTHING = 0.5
BETA_ONE = 0.9
BETA_TWO = 0.99
LEARN_RATE = 0.01
EPSILON = 1e-08

LANES = 128
CHANNELS = 32
UNROLL = 4
GRADS_VMEM = 16 * 2**20
BOTH = ("gx", "gy")
f32 = jnp.float32
bf16 = jnp.bfloat16


def ring_order(chips):
    return list(range(0, chips, 2)) + list(range(chips - 1, 0, -2))


def send(x, move):
    n, peers = lax.axis_size("gx"), lax.axis_size("gy")
    pairs = []
    for g in range(n):
        for y in range(peers):
            to = move(g // 2, g % 2, y)
            if to is not None:
                pairs.append((g * peers + y, (to[0] * 2 + to[1]) * peers + to[2]))
    return lax.ppermute(x, BOTH, pairs)


def to_core(x):
    return send(x, lambda k, c, y: (k, 1 - c, y))


def to_ring(x, step):
    chips = lax.axis_size("gx") // 2
    order = ring_order(chips)
    at = {k: i for i, k in enumerate(order)}
    return send(x, lambda k, c, y: (order[(at[k] + step) % chips], c, y))


def to_gy(x, step):
    peers = lax.axis_size("gy")
    return send(x, lambda k, c, y: (k, c, (y + step) % peers))


def offsets(chips):
    out = [0]
    for d in range(1, chips // 2):
        out += [-d, d]
    return out + [chips // 2]


def chip_in_slot(gx, slot, chips):
    k = gx // 2
    at = jnp.where(k % 2 == 0, k // 2, chips - 1 - k // 2)
    i = (at + offsets(chips)[slot] + chips) % chips
    return jnp.where(i < chips // 2, 2 * i, 2 * chips - 1 - 2 * i)


def vmem(count):
    return [pl.BlockSpec(memory_space=pltpu.VMEM)] * count


SCALARS = pl.BlockSpec(memory_space=pltpu.SMEM)
SMALL = pltpu.CompilerParams(vmem_limit_bytes=20 * 2**20)


def cost(flops, size):
    return pl.CostEstimate(flops=flops, bytes_accessed=size, transcendentals=0)


def diagonal(small, times):
    size = small.shape[0] * times
    wide = jnp.concatenate([small.astype(f32)] * times, axis=1)
    full = jnp.concatenate([wide] * times, axis=0)
    row = lax.broadcasted_iota(jnp.int32, (size, size), 0) // small.shape[0]
    col = lax.broadcasted_iota(jnp.int32, (size, size), 1) // small.shape[0]
    return jnp.where(row == col, full, 0.0)


def fixed_kernel(
    chips, zl, info, b_output, target_a, target_b, w, w_t, w_o, b, o, wanted, w_in, w_out, w_back, bias, scale
):
    gx = info[0]
    x_count = target_a.shape[0]
    starts = [
        pl.multiple_of((2 * chip_in_slot(gx, s, chips) + gx % 2) * zl, zl) for s in range(chips)
    ]
    for side, ref in enumerate((target_a, target_b)):

        def one(x, carry):
            rows = jnp.concatenate([ref[x, pl.ds(z, zl), :] for z in starts], axis=0)
            rows = rows - b_output[0]
            high = rows.astype(bf16).astype(f32)
            both = jnp.concatenate([high, rows - high], axis=0)
            wanted[side * x_count + x] = both.T.astype(bf16)
            return carry

        lax.fori_loop(0, x_count, one, 0)
    times = w_in.shape[0] // w.shape[0]
    w_in[...] = diagonal(0.5 * w[...].astype(f32), times).astype(bf16)
    w_out[...] = diagonal(w_o[...], times).astype(bf16)
    w_back[...] = diagonal(w_t[...], times).astype(bf16)
    bias[...] = jnp.concatenate([0.5 * b[...]] * times, axis=1)
    scale[...] = jnp.concatenate([0.5 * o[...]] * times, axis=1)


def fixed_parts(info, target, target_b, zl, w_hidden, b_hidden, w_output, b_output):
    chips = lax.axis_size("gx") // 2
    x_count, z_count, y_count = target.shape
    hidden = w_hidden.shape[1]
    width = zl * hidden
    square = jax.ShapeDtypeStruct((width, width), bf16)
    line = jax.ShapeDtypeStruct((1, width), f32)
    return pl.pallas_call(
        functools.partial(fixed_kernel, chips, zl),
        in_specs=[SCALARS, SCALARS] + vmem(7),
        out_specs=vmem(6),
        out_shape=[
            jax.ShapeDtypeStruct((2 * x_count, y_count, z_count), bf16),
            square,
            square,
            square,
            line,
            line,
        ],
        compiler_params=SMALL,
        cost_estimate=cost(0, 4 * 2**20),
    )(
        info,
        b_output,
        target,
        target_b,
        w_hidden,
        w_hidden.T,
        jnp.broadcast_to(w_output[:, None], (hidden, hidden)),
        b_hidden[None],
        w_output.astype(f32)[None],
    )


def lanes_kernel(plane, out):
    c, zl, _ = plane.shape
    per = LANES // c
    for t in range(zl // per):
        rows = jnp.concatenate([plane[:, t * per + j, :] for j in range(per)], axis=0)
        out[:, t * LANES : (t + 1) * LANES] = rows.T


def lanes_yz(plane):
    c, zl, y = plane.shape
    return pl.pallas_call(
        lanes_kernel,
        in_specs=vmem(1),
        out_specs=vmem(1)[0],
        out_shape=jax.ShapeDtypeStruct((y, zl * c), f32),
        compiler_params=SMALL,
        cost_estimate=cost(0, 2**18),
    )(plane)


def z_places(gx, gy, slot, chips, peers, zl, zs):
    z = (2 * chip_in_slot(gx, slot, chips) + gx % 2) * zl
    return (gy - z // zs + peers) % peers * zs + z % zs


def spread_kernel(chips, peers, zl, info, xy_a, xy_b, *refs):
    xzs, xy, xz, held = refs[: 2 * peers], refs[2 * peers], refs[2 * peers + 1 : -1], refs[-1]
    c, x_count, _ = xy_a.shape
    zs = xzs[0].shape[2]

    def some(i, carry):
        for x in range(UNROLL):
            x += i * UNROLL
            for side, ref in enumerate((xy_a, xy_b)):
                xy[side * x_count + x] = jnp.concatenate([ref[:, x, :]] * (LANES // c), axis=0).T
            for s in range(peers):
                for side in range(2):
                    held[s * zs : (s + 1) * zs, side * x_count + x, :] = xzs[2 * s + side][:, x, :].T
        return carry

    lax.fori_loop(0, x_count // UNROLL, some, 0)

    for p in range(chips):
        at = z_places(info[0], info[1], p, chips, peers, zl, zs)
        xz[p][...] = jnp.concatenate([held[at + j] for j in range(zl)], axis=1)


def spread(info, xy_a, xy_b, xzs, zl):
    peers, chips = lax.axis_size("gy"), lax.axis_size("gx") // 2
    c, x_count, y_count = xy_a.shape
    return pl.pallas_call(
        functools.partial(spread_kernel, chips, peers, zl),
        in_specs=[SCALARS] + vmem(2 + len(xzs)),
        out_specs=vmem(1 + chips),
        out_shape=[jax.ShapeDtypeStruct((2 * x_count, y_count, LANES), f32)]
        + [jax.ShapeDtypeStruct((2 * x_count, zl * c), f32)] * chips,
        scratch_shapes=[pltpu.VMEM((peers * xzs[0].shape[2], 2 * x_count, c), f32)],
        compiler_params=SMALL,
        cost_estimate=cost(0, 4 * 2**20),
    )(info, xy_a, xy_b, *xzs)


def collect_kernel(chips, peers, zl, info, part_xy, xy_a, xy_b, *refs):
    parts, outs, held = refs[:chips], refs[chips : chips + 2 + 2 * peers], refs[chips + 2 + 2 * peers]
    c, x_count, _ = xy_a.shape
    outs_xz = outs[2:]
    zs = outs_xz[0].shape[2]
    held[...] = jnp.zeros_like(held)
    for p in range(chips):
        at = z_places(info[0], info[1], p, chips, peers, zl, zs)
        rows = parts[p][...]
        for j in range(zl):
            held[at + j] = rows[:, j * c : (j + 1) * c]

    def some(i, carry):
        for x in range(UNROLL):
            x += i * UNROLL
            for side, ref in enumerate((xy_a, xy_b)):
                rows = part_xy[side * x_count + x].T
                total = sum(rows[j * c : (j + 1) * c] for j in range(LANES // c))
                outs[side][:, x, :] = total / ref[:, x, :]
            for s in range(peers):
                for side in range(2):
                    outs_xz[2 * s + side][:, x, :] = held[
                        s * zs : (s + 1) * zs, side * x_count + x, :
                    ].T
        return carry

    lax.fori_loop(0, x_count // UNROLL, some, 0)


def collect(info, part_xy, xy_a, xy_b, parts_xz, shape_xz, zl):
    peers, chips = lax.axis_size("gy"), lax.axis_size("gx") // 2
    c, x_count, _ = xy_a.shape
    outs = pl.pallas_call(
        functools.partial(collect_kernel, chips, peers, zl),
        in_specs=[SCALARS] + vmem(3 + chips),
        out_specs=vmem(2 + 2 * peers),
        out_shape=[jax.ShapeDtypeStruct(xy_a.shape, f32)] * 2
        + [jax.ShapeDtypeStruct(shape_xz, f32)] * (2 * peers),
        scratch_shapes=[pltpu.VMEM((peers * shape_xz[2], 2 * x_count, c), f32)],
        compiler_params=SMALL,
        cost_estimate=cost(0, 8 * 2**20),
    )(info, part_xy, xy_a, xy_b, *parts_xz)
    return outs[0], outs[1], outs[2:]


def grads_kernel(count, first, slot, w_in, w_out, w_back, bias, scale, wanted, xy, *refs):
    refs = list(refs)
    take = lambda k: [refs.pop(0) for _ in range(k)]
    xzs, yzs = take(count), take(count)
    before = None if first else take(1)[0]
    gxy = take(1)[0]
    gxzs, gyzs = take(count), take(count)
    pick, xz, yzb, gxz, gyz = refs
    step = pl.program_id(0)
    x_count, y_count, _ = xy.shape
    width = w_in.shape[0]
    z_count = wanted.shape[2] // 2
    zl = width // CHANNELS
    times = width // LANES

    @pl.when(step == 0)
    def _():
        row = lax.broadcasted_iota(jnp.int32, (2 * z_count, width), 0) % z_count
        col = lax.broadcasted_iota(jnp.int32, (2 * z_count, width), 1) // CHANNELS
        for j in range(count):
            pick[j, :width] = w_out[...]
            pick[j, width:] = jnp.where(row == (slot[0] + j) * zl + col, -1.0, 0.0).astype(bf16)
            yzb[j] = yzs[j][...]
        gyz[...] = jnp.zeros_like(gyz)

    for j in range(count):
        xz[j] = xzs[j][...]
    if first:
        gxy[...] = jnp.zeros_like(gxy)
    else:
        gxy[...] = before[...]

    def one_block(j, carry):
        yz = yzb[j]
        lines = [xz[j, x : x + 1, :] for x in range(x_count)]
        pairs = [jnp.concatenate([xy[x]] * times, axis=1) * yz for x in range(x_count)]
        features = jnp.concatenate([(g * r).astype(bf16) for g, r in zip(pairs, lines)], axis=0)
        half = jnp.dot(features, w_in[...], preferred_element_type=f32) + bias[...]
        t = jnp.tanh(half)
        up = 1.0 + t
        hidden = half * up
        slope = (up + hidden * (1.0 - t)) * scale[...]
        residual = jnp.dot(
            jnp.concatenate(
                [
                    hidden.astype(bf16),
                    jnp.concatenate([wanted[x] for x in range(x_count)], axis=0),
                ],
                axis=1,
            ),
            pick[j],
            preferred_element_type=f32,
        )
        back_hidden = (residual * slope).astype(bf16)
        back = jnp.dot(back_hidden, w_back[...], preferred_element_type=f32)
        total = None
        for x in range(x_count):
            b = back[x * y_count : (x + 1) * y_count] * pairs[x]
            gxz[j, x : x + 1, :] = jnp.sum(b, axis=0, keepdims=True)
            e = b * lines[x]
            gxy[x] += sum(e[:, h * LANES : (h + 1) * LANES] for h in range(times))
            total = e if total is None else total + e
        gyz[j] += total
        return carry

    lax.fori_loop(0, count, one_block, 0)
    for j in range(count):
        gxzs[j][...] = gxz[j]

    @pl.when(step == 1)
    def _():
        for j in range(count):
            gyzs[j][...] = gyz[j] / yzb[j]


def block_grads(slots, weights, wanted, xy, xzs, yzs, before):
    count = len(slots)
    rows, y_count, _ = xy.shape
    rows = rows // 2
    width = yzs[0].shape[1]

    def whole(a):
        return pl.BlockSpec(a.shape, lambda i: (0,) * a.ndim)

    side = pl.BlockSpec((rows, y_count, LANES), lambda i: (i, 0, 0))
    line = pl.BlockSpec((rows, width), lambda i: (i, 0))
    outs = pl.pallas_call(
        functools.partial(grads_kernel, count, before is None),
        grid=(2,),
        in_specs=[SCALARS]
        + [whole(w) for w in weights]
        + [side, side]
        + [line] * count
        + [whole(a) for a in yzs]
        + ([] if before is None else [side]),
        out_specs=[side] + [line] * count + [whole(a) for a in yzs],
        out_shape=[jax.ShapeDtypeStruct(xy.shape, f32)]
        + [jax.ShapeDtypeStruct((2 * rows, width), f32)] * count
        + [jax.ShapeDtypeStruct(a.shape, f32) for a in yzs],
        scratch_shapes=[
            pltpu.VMEM((count, width + wanted.shape[2], width), bf16),
            pltpu.VMEM((count, rows, width), f32),
            pltpu.VMEM((count, y_count, width), f32),
            pltpu.VMEM((count, rows, width), f32),
            pltpu.VMEM((count, y_count, width), f32),
        ],
        compiler_params=pltpu.CompilerParams(vmem_limit_bytes=GRADS_VMEM),
        cost_estimate=cost(12 * rows * y_count * count * width * width, count * 10 * 2**20),
    )(
        jnp.array(slots[:1], jnp.int32),
        *weights,
        wanted,
        xy,
        *[xzs[s] for s in slots],
        *yzs,
        *([] if before is None else [before]),
    )
    return outs[0], outs[1 : 1 + count], outs[1 + count :]


def near_sides(p, above, below, left, right):
    rows, cols = p.shape[1:]
    row = lax.broadcasted_iota(jnp.int32, p.shape, 1)
    col = lax.broadcasted_iota(jnp.int32, p.shape, 2)
    up = jnp.where(row == 0, above, pltpu.roll(p, 1, 1))
    down = jnp.where(row == rows - 1, below, pltpu.roll(p, rows - 1, 1))
    wide = p if cols % LANES == 0 else jnp.concatenate([p] * (LANES // cols), axis=2)
    back = pltpu.roll(wide, 1, 2)[:, :, :cols]
    ahead = pltpu.roll(wide, wide.shape[2] - 1, 2)[:, :, :cols]
    return up, down, jnp.where(col == 0, left, back), jnp.where(col == cols - 1, right, ahead)


def upright(ref, at, shape):
    c, rows, cols = shape
    line = ref[:, at : at + c * rows]
    return jnp.broadcast_to(line, (cols, c * rows)).T.reshape(shape)


def update(info, ends, count, plane, first, second, grad, borders, at_row, at_col, outs):
    above, below, left, right = borders
    p = plane[...]
    rows, cols = p.shape[1:]
    above = jnp.where(info[0] == 0, p[:, :1, :], above[:, :, at_row : at_row + cols])
    below = jnp.where(info[0] == ends[0], p[:, rows - 1 :, :], below[:, :, at_row : at_row + cols])
    left = jnp.where(info[1] == 0, p, upright(left, at_col, p.shape))
    right = jnp.where(info[1] == ends[1], p, upright(right, at_col, p.shape))
    up, down, back, ahead = near_sides(p, above, below, left, right)
    grad = grad + 2.0 * SMOOTHING * ((p - up) + (p - down) + (p - back) + (p - ahead))
    m = BETA_ONE * first[...] + (1.0 - BETA_ONE) * grad
    v = BETA_TWO * second[...] + (1.0 - BETA_TWO) * grad * grad
    corr_one = 1.0 - BETA_ONE**count
    corr_two = 1.0 - BETA_TWO**count
    outs[1][...] = m
    outs[2][...] = v
    outs[0][...] = p - LEARN_RATE * (m / corr_one) / (jnp.sqrt(v / corr_two) + EPSILON)


def update_two_kernel(ends, count, info, above, below, left, right, *refs):
    borders = (above, below, left, right)
    xy, xz, outs = refs[:5], refs[5:11], refs[11:]
    width_y = xy[0].shape[2]
    rows = xy[0].shape[1]
    update(info, ends, count, *xy[:3], xy[3][...] + xy[4][...], borders, 0, 0, outs[:3])
    update(info, ends, count, *xz[:3], xz[3][...] + xz[4][...] + xz[5][...], borders, 2 * width_y, xy[0].shape[0] * rows, outs[3:])


def update_two(info, count, borders, xy, xz):
    ends = (lax.axis_size("gx") - 1, lax.axis_size("gy") - 1)
    shapes = [jax.ShapeDtypeStruct(a.shape, f32) for a in (*xy[:3], *xz[:3])]
    outs = pl.pallas_call(
        functools.partial(update_two_kernel, ends, count),
        in_specs=[SCALARS] + vmem(15),
        out_specs=vmem(6),
        out_shape=shapes,
        compiler_params=SMALL,
        cost_estimate=cost(0, 4 * 2**20),
    )(info, *borders, *xy, *xz)
    return outs[:3], outs[3:]


def update_yz_kernel(ends, count, info, above, below, left, right, plane, first, second, a, b, d, *refs):
    outs, lanes, held = refs[:3], refs[3], refs[4]
    c, zl, width = plane.shape
    per = LANES // c
    for t in range(zl // per):
        at = slice(t * LANES, (t + 1) * LANES)
        rows = (a[:, at] + b[:, at] + d[:, at]).T
        for j in range(per):
            held[:, t * per + j, :] = rows[j * c : (j + 1) * c]
    borders = (above, below, left, right)
    at_col = left.shape[1] - c * zl
    update(info, ends, count, plane, first, second, held[...], borders, width, at_col, outs)
    lanes_kernel(outs[0], lanes)


def update_yz(info, count, borders, state, parts):
    ends = (lax.axis_size("gx") - 1, lax.axis_size("gy") - 1)
    outs = pl.pallas_call(
        functools.partial(update_yz_kernel, ends, count),
        in_specs=[SCALARS] + vmem(10),
        out_specs=vmem(4),
        out_shape=[jax.ShapeDtypeStruct(a.shape, f32) for a in (*state, parts[0])],
        scratch_shapes=[pltpu.VMEM(state[0].shape, f32)],
        compiler_params=SMALL,
        cost_estimate=cost(0, 2 * 2**20),
    )(info, *borders, *state, *parts)
    return outs[:3], outs[3]


def edges_kernel(peers, info, xy, xz, yz, gate, *outs):
    width = xy.shape[2]
    for ref, at in ((xy, 0), (yz, width), (xz, 2 * width)):
        rows, cols = ref.shape[1:]
        outs[0][:, :, at : at + cols] = ref[:, rows - 1 :, :]
        outs[1][:, :, at : at + cols] = ref[:, :1, :]
    at = 0
    for ref in (xy, xz, yz):
        c, rows, cols = ref.shape
        flat = ref[...].reshape(c * rows, cols).T
        last, first = flat[cols - 1 :], flat[:1]
        here = slice(at, at + c * rows)
        if peers == 2:
            outs[2][:, here] = jnp.where(info[1] == 0, last, first)
        else:
            outs[2][:, here] = last
            outs[3][:, here] = first
        at += c * rows


def borders(info, planes, gate):
    n, peers = lax.axis_size("gx"), lax.axis_size("gy")
    c = planes[0].shape[0]
    row = jax.ShapeDtypeStruct((c, 1, sum(p.shape[2] for p in planes)), f32)
    col = jax.ShapeDtypeStruct((1, sum(c * p.shape[1] for p in planes)), f32)
    outs = pl.pallas_call(
        functools.partial(edges_kernel, peers),
        in_specs=[SCALARS] + vmem(3) + [pl.BlockSpec(memory_space=pl.ANY)],
        out_specs=vmem(3 if peers == 2 else 4),
        out_shape=[row, row] + [col] * (1 if peers == 2 else 2),
        compiler_params=SMALL,
        cost_estimate=cost(0, 2**20),
    )(info, *planes, gate)
    up = [(i, i + 1) for i in range(n - 1)]
    above = lax.ppermute(outs[0], "gx", up)
    below = lax.ppermute(outs[1], "gx", [(j, i) for i, j in up])
    if peers == 2:
        left = right = lax.ppermute(outs[2], "gy", [(0, 1), (1, 0)])
    else:
        up = [(i, i + 1) for i in range(peers - 1)]
        left = lax.ppermute(outs[2], "gy", up)
        right = lax.ppermute(outs[3], "gy", [(j, i) for i, j in up])
    return above, below, left, right


def per_device(
    target,
    plane_xy,
    plane_xz,
    plane_yz,
    first_xy,
    first_xz,
    first_yz,
    second_xy,
    second_xz,
    second_yz,
    w_hidden,
    b_hidden,
    w_output,
    b_output,
):
    peers = lax.axis_size("gy")
    info = jnp.stack([lax.axis_index("gx"), lax.axis_index("gy")]).astype(jnp.int32)
    zl = plane_yz.shape[1]
    lanes = lanes_yz(plane_yz)
    target_b = to_core(target)
    fixed = None

    chips = lax.axis_size("gx") // 2
    half = chips // 2
    slot = {o: i for i, o in enumerate(offsets(chips))}
    middle = lanes.shape[0] // 2

    for iteration in range(STEPS):
        back, ahead = {0: lanes}, {0: lanes}
        for d in range(1, half):
            back[d], ahead[d] = to_ring(back[d - 1], 1), to_ring(ahead[d - 1], -1)
        parts = to_ring(back[half - 1][:middle], 1), to_ring(ahead[half - 1][middle:], -1)
        far = jnp.concatenate(parts, axis=0)
        yzs = {0: lanes, half: far}
        for d in range(1, half):
            yzs[-d], yzs[d] = back[d], ahead[d]
        xy_b, xz_b = to_core(plane_xy), to_core(plane_xz)
        xzs = [plane_xz, xz_b]
        for s in range(1, peers):
            xz_y = to_gy(plane_xz, s)
            xzs += [xz_y, to_core(xz_y)]
        if fixed is None:
            fixed = fixed_parts(info, target, target_b, zl, w_hidden, b_hidden, w_output, b_output)
        wanted, weights = fixed[0], fixed[1:]
        xy, *xz = spread(info, plane_xy, xy_b, xzs, zl)

        order = [(0,), (-1,), (1,), (half,)] + [(-d, d) for d in range(half - 1, 1, -1)]
        part_xy, parts_xz, parts_yz = None, {}, {}
        send_ahead, send_back = None, None
        for group in order:
            part_xy, lines, blocks = block_grads(
                [slot[o] for o in group], weights, wanted, xy, xz, [yzs[o] for o in group], part_xy
            )
            for o, line, block in zip(group, lines, blocks):
                parts_xz[slot[o]], parts_yz[o] = line, block
            if group == (0,):
                around = borders(info, (plane_xy, plane_xz, plane_yz), lines[0])
        block = parts_yz[half]
        send_ahead, send_back = to_ring(block[:middle], 1), to_ring(block[middle:], -1)
        for d in range(half - 1, 0, -1):
            if d == half - 1:
                send_ahead = jnp.pad(send_ahead, ((0, middle), (0, 0)))
                send_back = jnp.pad(send_back, ((middle, 0), (0, 0)))
            send_ahead, send_back = parts_yz[d] + send_ahead, parts_yz[-d] + send_back
            send_ahead, send_back = to_ring(send_ahead, 1), to_ring(send_back, -1)

        grad_xy, far_xy, pieces = collect(
            info, part_xy, plane_xy, xy_b, [parts_xz[i] for i in range(chips)], plane_xz.shape, zl
        )
        sides = [pieces[2 * s] + to_core(pieces[2 * s + 1]) for s in range(1, peers)]
        grads_xz = [to_gy(side, -s) for s, side in enumerate(sides, 1)]
        near_xz, far_xz = pieces[0], to_core(pieces[1])
        for extra in grads_xz[1:]:
            near_xz = near_xz + extra
        count = START + iteration + 1
        (plane_xy, first_xy, second_xy), (plane_xz, first_xz, second_xz) = update_two(
            info,
            count,
            around,
            (plane_xy, first_xy, second_xy, grad_xy, to_core(far_xy)),
            (plane_xz, first_xz, second_xz, near_xz, far_xz, grads_xz[0]),
        )
        (plane_yz, first_yz, second_yz), lanes = update_yz(
            info, count, around, (plane_yz, first_yz, second_yz), (parts_yz[0], send_ahead, send_back)
        )
    return (
        plane_xy,
        plane_xz,
        plane_yz,
        first_xy,
        first_xz,
        first_yz,
        second_xy,
        second_xz,
        second_yz,
    )


def solution(mesh):
    return jax.shard_map(
        per_device,
        mesh=mesh,
        in_specs=(
            P("gx", None, "gy"),
            P(None, "gx", "gy"),
            P(None, "gx", "gy"),
            P(None, "gx", "gy"),
            P(None, "gx", "gy"),
            P(None, "gx", "gy"),
            P(None, "gx", "gy"),
            P(None, "gx", "gy"),
            P(None, "gx", "gy"),
            P(None, "gx", "gy"),
            P(),
            P(),
            P(),
            P(),
        ),
        out_specs=(
            P(None, "gx", "gy"),
            P(None, "gx", "gy"),
            P(None, "gx", "gy"),
            P(None, "gx", "gy"),
            P(None, "gx", "gy"),
            P(None, "gx", "gy"),
            P(None, "gx", "gy"),
            P(None, "gx", "gy"),
            P(None, "gx", "gy"),
        ),
        check_vma=False,
    )
```

```python
import functools
import jax
import jax.numpy as jnp
from jax import lax
from jax.experimental import pallas as pl
from jax.experimental.pallas import tpu as pltpu
from jax.sharding import PartitionSpec as P


STEPS = 2
START = 20


SMOOTHING = 0.5
BETA_ONE = 0.9
BETA_TWO = 0.99
LEARN_RATE = 0.01
EPSILON = 1e-08

LANES = 128
CHANNELS = 32
UNROLL = 4
GRADS_VMEM = 16 * 2**20
BOTH = ("gx", "gy")
f32 = jnp.float32
bf16 = jnp.bfloat16


def ring_order(chips):
    return list(range(0, chips, 2)) + list(range(chips - 1, 0, -2))


def send(x, move):
    n, peers = lax.axis_size("gx"), lax.axis_size("gy")
    pairs = []
    for g in range(n):
        for y in range(peers):
            to = move(g // 2, g % 2, y)
            if to is not None:
                pairs.append((g * peers + y, (to[0] * 2 + to[1]) * peers + to[2]))
    return lax.ppermute(x, BOTH, pairs)


def to_core(x):
    return send(x, lambda k, c, y: (k, 1 - c, y))


def to_ring(x, step):
    chips = lax.axis_size("gx") // 2
    order = ring_order(chips)
    at = {k: i for i, k in enumerate(order)}
    return send(x, lambda k, c, y: (order[(at[k] + step) % chips], c, y))


def to_gy(x, step):
    peers = lax.axis_size("gy")
    return send(x, lambda k, c, y: (k, c, (y + step) % peers))


def offsets(chips):
    out = [0]
    for d in range(1, chips // 2):
        out += [-d, d]
    return out + [chips // 2]


def chip_in_slot(gx, slot, chips):
    k = gx // 2
    at = jnp.where(k % 2 == 0, k // 2, chips - 1 - k // 2)
    i = (at + offsets(chips)[slot] + chips) % chips
    return jnp.where(i < chips // 2, 2 * i, 2 * chips - 1 - 2 * i)


def vmem(count):
    return [pl.BlockSpec(memory_space=pltpu.VMEM)] * count


SCALARS = pl.BlockSpec(memory_space=pltpu.SMEM)
SMALL = pltpu.CompilerParams(vmem_limit_bytes=20 * 2**20)


def cost(flops, size):
    return pl.CostEstimate(flops=flops, bytes_accessed=size, transcendentals=0)


def diagonal(small, times):
    size = small.shape[0] * times
    wide = jnp.concatenate([small.astype(f32)] * times, axis=1)
    full = jnp.concatenate([wide] * times, axis=0)
    row = lax.broadcasted_iota(jnp.int32, (size, size), 0) // small.shape[0]
    col = lax.broadcasted_iota(jnp.int32, (size, size), 1) // small.shape[0]
    return jnp.where(row == col, full, 0.0)


def fixed_kernel(
    chips, zl, info, b_output, target_a, target_b, w, b, o, wanted, w_in, w_out, w_back, bias, scale
):
    gx = info[0]
    x_count = target_a.shape[0]
    starts = [
        pl.multiple_of((2 * chip_in_slot(gx, s, chips) + gx % 2) * zl, zl) for s in range(chips)
    ]
    for side, ref in enumerate((target_a, target_b)):

        def one(x, carry):
            rows = jnp.concatenate([ref[x, pl.ds(z, zl), :] for z in starts], axis=0)
            rows = rows - b_output[0]
            high = rows.astype(bf16).astype(f32)
            both = jnp.concatenate([high, rows - high], axis=0)
            wanted[side * x_count + x] = both.T.astype(bf16)
            return carry

        lax.fori_loop(0, x_count, one, 0)
    times = w_in.shape[0] // w.shape[0]
    wide, line = w[...].astype(f32), o[...].astype(f32)
    w_in[...] = diagonal(0.5 * wide, times).astype(bf16)
    w_out[...] = diagonal(jnp.broadcast_to(line, wide.shape).T, times).astype(bf16)
    w_back[...] = diagonal(wide.T, times).astype(bf16)
    bias[...] = jnp.concatenate([0.5 * b[...]] * times, axis=1)
    scale[...] = jnp.concatenate([0.5 * line] * times, axis=1)


def fixed_parts(info, target, target_b, zl, w_hidden, b_hidden, w_output, b_output):
    chips = lax.axis_size("gx") // 2
    x_count, z_count, y_count = target.shape
    hidden = w_hidden.shape[1]
    width = zl * hidden
    square = jax.ShapeDtypeStruct((width, width), bf16)
    line = jax.ShapeDtypeStruct((1, width), f32)
    return pl.pallas_call(
        functools.partial(fixed_kernel, chips, zl),
        in_specs=[SCALARS, SCALARS] + vmem(5),
        out_specs=vmem(6),
        out_shape=[
            jax.ShapeDtypeStruct((2 * x_count, y_count, z_count), bf16),
            square,
            square,
            square,
            line,
            line,
        ],
        compiler_params=SMALL,
        cost_estimate=cost(0, 4 * 2**20),
    )(
        info,
        b_output,
        target,
        target_b,
        w_hidden,
        b_hidden[None],
        w_output[None],
    )


def lanes_kernel(plane, out):
    c, zl, _ = plane.shape
    per = LANES // c
    for t in range(zl // per):
        rows = jnp.concatenate([plane[:, t * per + j, :] for j in range(per)], axis=0)
        out[:, t * LANES : (t + 1) * LANES] = rows.T


def lanes_yz(plane):
    c, zl, y = plane.shape
    return pl.pallas_call(
        lanes_kernel,
        in_specs=vmem(1),
        out_specs=vmem(1)[0],
        out_shape=jax.ShapeDtypeStruct((y, zl * c), f32),
        compiler_params=SMALL,
        cost_estimate=cost(0, 2**18),
    )(plane)


def z_places(gx, gy, slot, chips, peers, zl, zs):
    z = (2 * chip_in_slot(gx, slot, chips) + gx % 2) * zl
    return (gy - z // zs + peers) % peers * zs + z % zs


def spread_kernel(chips, peers, zl, info, xy_a, xy_b, *refs):
    xzs, xy, xz, held = refs[: 2 * peers], refs[2 * peers], refs[2 * peers + 1 : -1], refs[-1]
    c, x_count, _ = xy_a.shape
    zs = xzs[0].shape[2]

    def some(i, carry):
        for x in range(UNROLL):
            x += i * UNROLL
            for side, ref in enumerate((xy_a, xy_b)):
                xy[side * x_count + x] = jnp.concatenate([ref[:, x, :]] * (LANES // c), axis=0).T
            for s in range(peers):
                for side in range(2):
                    held[s * zs : (s + 1) * zs, side * x_count + x, :] = xzs[2 * s + side][:, x, :].T
        return carry

    lax.fori_loop(0, x_count // UNROLL, some, 0)

    for p in range(chips):
        at = z_places(info[0], info[1], p, chips, peers, zl, zs)
        xz[p][...] = jnp.concatenate([held[at + j] for j in range(zl)], axis=1)


def spread(info, xy_a, xy_b, xzs, zl):
    peers, chips = lax.axis_size("gy"), lax.axis_size("gx") // 2
    c, x_count, y_count = xy_a.shape
    return pl.pallas_call(
        functools.partial(spread_kernel, chips, peers, zl),
        in_specs=[SCALARS] + vmem(2 + len(xzs)),
        out_specs=vmem(1 + chips),
        out_shape=[jax.ShapeDtypeStruct((2 * x_count, y_count, LANES), f32)]
        + [jax.ShapeDtypeStruct((2 * x_count, zl * c), f32)] * chips,
        scratch_shapes=[pltpu.VMEM((peers * xzs[0].shape[2], 2 * x_count, c), f32)],
        compiler_params=SMALL,
        cost_estimate=cost(0, 4 * 2**20),
    )(info, xy_a, xy_b, *xzs)


def collect_xy_kernel(part, xy_a, xy_b, *outs):
    c, x_count, _ = xy_a.shape

    def some(i, carry):
        for x in range(UNROLL):
            x += i * UNROLL
            for side, ref in enumerate((xy_a, xy_b)):
                rows = part[side * x_count + x].T
                total = sum(rows[j * c : (j + 1) * c] for j in range(LANES // c))
                outs[side][:, x, :] = total / ref[:, x, :]
        return carry

    lax.fori_loop(0, x_count // UNROLL, some, 0)


def collect_xy(part, xy_a, xy_b):
    return pl.pallas_call(
        collect_xy_kernel,
        in_specs=vmem(3),
        out_specs=vmem(2),
        out_shape=[jax.ShapeDtypeStruct(xy_a.shape, f32)] * 2,
        compiler_params=SMALL,
        cost_estimate=cost(0, 4 * 2**20),
    )(part, xy_a, xy_b)


def collect_xz_kernel(chips, peers, zl, info, *refs):
    parts, outs, held = refs[:chips], refs[chips : chips + 2 * peers], refs[chips + 2 * peers]
    c, x_count, zs = outs[0].shape
    held[...] = jnp.zeros_like(held)
    for p in range(chips):
        at = z_places(info[0], info[1], p, chips, peers, zl, zs)
        rows = parts[p][...]
        for j in range(zl):
            held[at + j] = rows[:, j * c : (j + 1) * c]

    def some(i, carry):
        for x in range(UNROLL):
            x += i * UNROLL
            for s in range(peers):
                for side in range(2):
                    outs[2 * s + side][:, x, :] = held[
                        s * zs : (s + 1) * zs, side * x_count + x, :
                    ].T
        return carry

    lax.fori_loop(0, x_count // UNROLL, some, 0)


def collect_xz(info, parts, shape, zl):
    peers, chips = lax.axis_size("gy"), lax.axis_size("gx") // 2
    c, x_count, zs = shape
    return pl.pallas_call(
        functools.partial(collect_xz_kernel, chips, peers, zl),
        in_specs=[SCALARS] + vmem(chips),
        out_specs=vmem(2 * peers),
        out_shape=[jax.ShapeDtypeStruct(shape, f32)] * (2 * peers),
        scratch_shapes=[pltpu.VMEM((peers * zs, 2 * x_count, c), f32)],
        compiler_params=SMALL,
        cost_estimate=cost(0, 4 * 2**20),
    )(info, *parts)


def grads_kernel(count, first, slot, w_in, w_out, w_back, bias, scale, wanted, xy, *refs):
    refs = list(refs)
    take = lambda k: [refs.pop(0) for _ in range(k)]
    xzs, yzs = take(count), take(count)
    before = None if first else take(1)[0]
    gxy = take(1)[0]
    gxzs, gyzs = take(count), take(count)
    pick, xz, yzb, gxz, gyz = refs
    step = pl.program_id(0)
    x_count, y_count, _ = xy.shape
    width = w_in.shape[0]
    z_count = wanted.shape[2] // 2
    zl = width // CHANNELS
    times = width // LANES

    @pl.when(step == 0)
    def _():
        row = lax.broadcasted_iota(jnp.int32, (2 * z_count, width), 0) % z_count
        col = lax.broadcasted_iota(jnp.int32, (2 * z_count, width), 1) // CHANNELS
        for j in range(count):
            pick[j, :width] = w_out[...]
            pick[j, width:] = jnp.where(row == (slot[0] + j) * zl + col, -1.0, 0.0).astype(bf16)
            yzb[j] = yzs[j][...]
        gyz[...] = jnp.zeros_like(gyz)

    for j in range(count):
        xz[j] = xzs[j][...]
    if first:
        gxy[...] = jnp.zeros_like(gxy)
    else:
        gxy[...] = before[...]

    def one_block(j, carry):
        yz = yzb[j]
        lines = [xz[j, x : x + 1, :] for x in range(x_count)]
        pairs = [jnp.concatenate([xy[x]] * times, axis=1) * yz for x in range(x_count)]
        features = jnp.concatenate([(g * r).astype(bf16) for g, r in zip(pairs, lines)], axis=0)
        half = jnp.dot(features, w_in[...], preferred_element_type=f32) + bias[...]
        t = jnp.tanh(half)
        up = 1.0 + t
        hidden = half * up
        slope = (up + hidden * (1.0 - t)) * scale[...]
        residual = jnp.dot(
            jnp.concatenate(
                [
                    hidden.astype(bf16),
                    jnp.concatenate([wanted[x] for x in range(x_count)], axis=0),
                ],
                axis=1,
            ),
            pick[j],
            preferred_element_type=f32,
        )
        back_hidden = (residual * slope).astype(bf16)
        back = jnp.dot(back_hidden, w_back[...], preferred_element_type=f32)
        total = None
        for x in range(x_count):
            b = back[x * y_count : (x + 1) * y_count] * pairs[x]
            gxz[j, x : x + 1, :] = jnp.sum(b, axis=0, keepdims=True)
            e = b * lines[x]
            gxy[x] += sum(e[:, h * LANES : (h + 1) * LANES] for h in range(times))
            total = e if total is None else total + e
        gyz[j] += total
        return carry

    lax.fori_loop(0, count, one_block, 0)
    for j in range(count):
        gxzs[j][...] = gxz[j]

    @pl.when(step == 1)
    def _():
        for j in range(count):
            gyzs[j][...] = gyz[j] / yzb[j]


def block_grads(slots, weights, wanted, xy, xzs, yzs, before):
    count = len(slots)
    rows, y_count, _ = xy.shape
    rows = rows // 2
    width = yzs[0].shape[1]

    def whole(a):
        return pl.BlockSpec(a.shape, lambda i: (0,) * a.ndim)

    side = pl.BlockSpec((rows, y_count, LANES), lambda i: (i, 0, 0))
    line = pl.BlockSpec((rows, width), lambda i: (i, 0))
    outs = pl.pallas_call(
        functools.partial(grads_kernel, count, before is None),
        grid=(2,),
        in_specs=[SCALARS]
        + [whole(w) for w in weights]
        + [side, side]
        + [line] * count
        + [whole(a) for a in yzs]
        + ([] if before is None else [side]),
        out_specs=[side] + [line] * count + [whole(a) for a in yzs],
        out_shape=[jax.ShapeDtypeStruct(xy.shape, f32)]
        + [jax.ShapeDtypeStruct((2 * rows, width), f32)] * count
        + [jax.ShapeDtypeStruct(a.shape, f32) for a in yzs],
        scratch_shapes=[
            pltpu.VMEM((count, width + wanted.shape[2], width), bf16),
            pltpu.VMEM((count, rows, width), f32),
            pltpu.VMEM((count, y_count, width), f32),
            pltpu.VMEM((count, rows, width), f32),
            pltpu.VMEM((count, y_count, width), f32),
        ],
        compiler_params=pltpu.CompilerParams(vmem_limit_bytes=GRADS_VMEM),
        cost_estimate=cost(12 * rows * y_count * count * width * width, count * 10 * 2**20),
    )(
        jnp.array(slots[:1], jnp.int32),
        *weights,
        wanted,
        xy,
        *[xzs[s] for s in slots],
        *yzs,
        *([] if before is None else [before]),
    )
    return outs[0], outs[1 : 1 + count], outs[1 + count :]


def near_sides(p, above, below, left, right):
    rows, cols = p.shape[1:]
    row = lax.broadcasted_iota(jnp.int32, p.shape, 1)
    col = lax.broadcasted_iota(jnp.int32, p.shape, 2)
    up = jnp.where(row == 0, above, pltpu.roll(p, 1, 1))
    down = jnp.where(row == rows - 1, below, pltpu.roll(p, rows - 1, 1))
    wide = p if cols % LANES == 0 else jnp.concatenate([p] * (LANES // cols), axis=2)
    back = pltpu.roll(wide, 1, 2)[:, :, :cols]
    ahead = pltpu.roll(wide, wide.shape[2] - 1, 2)[:, :, :cols]
    return up, down, jnp.where(col == 0, left, back), jnp.where(col == cols - 1, right, ahead)


def upright(ref, at, shape):
    c, rows, cols = shape
    line = ref[:, at : at + c * rows]
    return jnp.broadcast_to(line, (cols, c * rows)).T.reshape(shape)


def update(info, ends, count, plane, first, second, grad, borders, at_row, at_col, outs):
    above, below, left, right = borders
    p = plane[...]
    rows, cols = p.shape[1:]
    above = jnp.where(info[0] == 0, p[:, :1, :], above[:, :, at_row : at_row + cols])
    below = jnp.where(info[0] == ends[0], p[:, rows - 1 :, :], below[:, :, at_row : at_row + cols])
    left = jnp.where(info[1] == 0, p, upright(left, at_col, p.shape))
    right = jnp.where(info[1] == ends[1], p, upright(right, at_col, p.shape))
    up, down, back, ahead = near_sides(p, above, below, left, right)
    grad = grad + 2.0 * SMOOTHING * ((p - up) + (p - down) + (p - back) + (p - ahead))
    m = BETA_ONE * first[...] + (1.0 - BETA_ONE) * grad
    v = BETA_TWO * second[...] + (1.0 - BETA_TWO) * grad * grad
    corr_one = 1.0 - BETA_ONE**count
    corr_two = 1.0 - BETA_TWO**count
    outs[1][...] = m
    outs[2][...] = v
    outs[0][...] = p - LEARN_RATE * (m / corr_one) / (jnp.sqrt(v / corr_two) + EPSILON)


def update_two_kernel(ends, count, info, above, below, left, right, *refs):
    borders = (above, below, left, right)
    xy, xz, outs = refs[:5], refs[5:11], refs[11:]
    width_y = xy[0].shape[2]
    rows = xy[0].shape[1]
    update(info, ends, count, *xy[:3], xy[3][...] + xy[4][...], borders, 0, 0, outs[:3])
    update(info, ends, count, *xz[:3], xz[3][...] + xz[4][...] + xz[5][...], borders, 2 * width_y, xy[0].shape[0] * rows, outs[3:])


def update_two(info, count, borders, xy, xz):
    ends = (lax.axis_size("gx") - 1, lax.axis_size("gy") - 1)
    shapes = [jax.ShapeDtypeStruct(a.shape, f32) for a in (*xy[:3], *xz[:3])]
    outs = pl.pallas_call(
        functools.partial(update_two_kernel, ends, count),
        in_specs=[SCALARS] + vmem(15),
        out_specs=vmem(6),
        out_shape=shapes,
        compiler_params=SMALL,
        cost_estimate=cost(0, 4 * 2**20),
    )(info, *borders, *xy, *xz)
    return outs[:3], outs[3:]


def update_yz_kernel(ends, count, info, above, below, left, right, plane, first, second, a, b, d, *refs):
    outs, lanes, held = refs[:3], refs[3], refs[4]
    c, zl, width = plane.shape
    per = LANES // c
    for t in range(zl // per):
        at = slice(t * LANES, (t + 1) * LANES)
        rows = (a[:, at] + b[:, at] + d[:, at]).T
        for j in range(per):
            held[:, t * per + j, :] = rows[j * c : (j + 1) * c]
    borders = (above, below, left, right)
    at_col = left.shape[1] - c * zl
    update(info, ends, count, plane, first, second, held[...], borders, width, at_col, outs)
    lanes_kernel(outs[0], lanes)


def update_yz(info, count, borders, state, parts):
    ends = (lax.axis_size("gx") - 1, lax.axis_size("gy") - 1)
    outs = pl.pallas_call(
        functools.partial(update_yz_kernel, ends, count),
        in_specs=[SCALARS] + vmem(10),
        out_specs=vmem(4),
        out_shape=[jax.ShapeDtypeStruct(a.shape, f32) for a in (*state, parts[0])],
        scratch_shapes=[pltpu.VMEM(state[0].shape, f32)],
        compiler_params=SMALL,
        cost_estimate=cost(0, 2 * 2**20),
    )(info, *borders, *state, *parts)
    return outs[:3], outs[3]


def edges_kernel(peers, info, xy, xz, yz, gate, *outs):
    width = xy.shape[2]
    for ref, at in ((xy, 0), (yz, width), (xz, 2 * width)):
        rows, cols = ref.shape[1:]
        outs[0][:, :, at : at + cols] = ref[:, rows - 1 :, :]
        outs[1][:, :, at : at + cols] = ref[:, :1, :]
    at = 0
    for ref in (xy, xz, yz):
        c, rows, cols = ref.shape
        flat = ref[...].reshape(c * rows, cols).T
        last, first = flat[cols - 1 :], flat[:1]
        here = slice(at, at + c * rows)
        if peers == 2:
            outs[2][:, here] = jnp.where(info[1] == 0, last, first)
        else:
            outs[2][:, here] = last
            outs[3][:, here] = first
        at += c * rows


def borders(info, planes, gate):
    n, peers = lax.axis_size("gx"), lax.axis_size("gy")
    c = planes[0].shape[0]
    row = jax.ShapeDtypeStruct((c, 1, sum(p.shape[2] for p in planes)), f32)
    col = jax.ShapeDtypeStruct((1, sum(c * p.shape[1] for p in planes)), f32)
    outs = pl.pallas_call(
        functools.partial(edges_kernel, peers),
        in_specs=[SCALARS] + vmem(3) + [pl.BlockSpec(memory_space=pl.ANY)],
        out_specs=vmem(3 if peers == 2 else 4),
        out_shape=[row, row] + [col] * (1 if peers == 2 else 2),
        compiler_params=SMALL,
        cost_estimate=cost(0, 2**20),
    )(info, *planes, gate)
    up = [(i, i + 1) for i in range(n - 1)]
    above = lax.ppermute(outs[0], "gx", up)
    below = lax.ppermute(outs[1], "gx", [(j, i) for i, j in up])
    if peers == 2:
        left = right = lax.ppermute(outs[2], "gy", [(0, 1), (1, 0)])
    else:
        up = [(i, i + 1) for i in range(peers - 1)]
        left = lax.ppermute(outs[2], "gy", up)
        right = lax.ppermute(outs[3], "gy", [(j, i) for i, j in up])
    return above, below, left, right


def per_device(
    target,
    plane_xy,
    plane_xz,
    plane_yz,
    first_xy,
    first_xz,
    first_yz,
    second_xy,
    second_xz,
    second_yz,
    w_hidden,
    b_hidden,
    w_output,
    b_output,
):
    peers = lax.axis_size("gy")
    info = jnp.stack([lax.axis_index("gx"), lax.axis_index("gy")]).astype(jnp.int32)
    zl = plane_yz.shape[1]
    lanes = lanes_yz(plane_yz)
    target_b = to_core(target)
    fixed = None

    chips = lax.axis_size("gx") // 2
    half = chips // 2
    slot = {o: i for i, o in enumerate(offsets(chips))}
    middle = lanes.shape[0] // 2

    for iteration in range(STEPS):
        back, ahead = {0: lanes}, {0: lanes}
        for d in range(1, half):
            back[d], ahead[d] = to_ring(back[d - 1], 1), to_ring(ahead[d - 1], -1)
        parts = to_ring(back[half - 1][:middle], 1), to_ring(ahead[half - 1][middle:], -1)
        far = jnp.concatenate(parts, axis=0)
        yzs = {0: lanes, half: far}
        for d in range(1, half):
            yzs[-d], yzs[d] = back[d], ahead[d]
        xy_b, xz_b = to_core(plane_xy), to_core(plane_xz)
        xzs = [plane_xz, xz_b]
        for s in range(1, peers):
            xz_y = to_gy(plane_xz, s)
            xzs += [xz_y, to_core(xz_y)]
        if fixed is None:
            fixed = fixed_parts(info, target, target_b, zl, w_hidden, b_hidden, w_output, b_output)
        wanted, weights = fixed[0], fixed[1:]
        xy, *xz = spread(info, plane_xy, xy_b, xzs, zl)

        order = [(0,), (-1,), (1,), (half,)] + [(-d, d) for d in range(half - 1, 1, -1)]
        part_xy, parts_xz, parts_yz = None, {}, {}
        send_ahead, send_back = None, None
        for group in order:
            part_xy, lines, blocks = block_grads(
                [slot[o] for o in group], weights, wanted, xy, xz, [yzs[o] for o in group], part_xy
            )
            for o, line, block in zip(group, lines, blocks):
                parts_xz[slot[o]], parts_yz[o] = line, block
            if group == (1,):
                around = borders(info, (plane_xy, plane_xz, plane_yz), lines[0])
        block = parts_yz[half]
        send_ahead, send_back = to_ring(block[:middle], 1), to_ring(block[middle:], -1)
        for d in range(half - 1, 0, -1):
            if d == half - 1:
                send_ahead = jnp.pad(send_ahead, ((0, middle), (0, 0)))
                send_back = jnp.pad(send_back, ((middle, 0), (0, 0)))
            send_ahead, send_back = parts_yz[d] + send_ahead, parts_yz[-d] + send_back
            send_ahead, send_back = to_ring(send_ahead, 1), to_ring(send_back, -1)

        pieces = collect_xz(info, [parts_xz[i] for i in range(chips)], plane_xz.shape, zl)
        grad_xy, far_xy = collect_xy(part_xy, plane_xy, xy_b)
        sides = [pieces[2 * s] + to_core(pieces[2 * s + 1]) for s in range(1, peers)]
        grads_xz = [to_gy(side, -s) for s, side in enumerate(sides, 1)]
        near_xz, far_xz = pieces[0], to_core(pieces[1])
        for extra in grads_xz[1:]:
            near_xz = near_xz + extra
        count = START + iteration + 1
        (plane_xy, first_xy, second_xy), (plane_xz, first_xz, second_xz) = update_two(
            info,
            count,
            around,
            (plane_xy, first_xy, second_xy, grad_xy, to_core(far_xy)),
            (plane_xz, first_xz, second_xz, near_xz, far_xz, grads_xz[0]),
        )
        (plane_yz, first_yz, second_yz), lanes = update_yz(
            info, count, around, (plane_yz, first_yz, second_yz), (parts_yz[0], send_ahead, send_back)
        )
    return (
        plane_xy,
        plane_xz,
        plane_yz,
        first_xy,
        first_xz,
        first_yz,
        second_xy,
        second_xz,
        second_yz,
    )


def solution(mesh):
    return jax.shard_map(
        per_device,
        mesh=mesh,
        in_specs=(
            P("gx", None, "gy"),
            P(None, "gx", "gy"),
            P(None, "gx", "gy"),
            P(None, "gx", "gy"),
            P(None, "gx", "gy"),
            P(None, "gx", "gy"),
            P(None, "gx", "gy"),
            P(None, "gx", "gy"),
            P(None, "gx", "gy"),
            P(None, "gx", "gy"),
            P(),
            P(),
            P(),
            P(),
        ),
        out_specs=(
            P(None, "gx", "gy"),
            P(None, "gx", "gy"),
            P(None, "gx", "gy"),
            P(None, "gx", "gy"),
            P(None, "gx", "gy"),
            P(None, "gx", "gy"),
            P(None, "gx", "gy"),
            P(None, "gx", "gy"),
            P(None, "gx", "gy"),
        ),
        check_vma=False,
    )
```

```python
import functools
import jax
import jax.numpy as jnp
from jax import lax
from jax.experimental import pallas as pl
from jax.experimental.pallas import tpu as pltpu
from jax.sharding import PartitionSpec as P


STEPS = 2
START = 20


SMOOTHING = 0.5
BETA_ONE = 0.9
BETA_TWO = 0.99
LEARN_RATE = 0.01
EPSILON = 1e-08

LANES = 128
CHANNELS = 32
UNROLL = 4
GRADS_VMEM = 16 * 2**20
BOTH = ("gx", "gy")
f32 = jnp.float32
bf16 = jnp.bfloat16


def ring_order(chips):
    return list(range(0, chips, 2)) + list(range(chips - 1, 0, -2))


def send(x, move):
    n, peers = lax.axis_size("gx"), lax.axis_size("gy")
    pairs = []
    for g in range(n):
        for y in range(peers):
            to = move(g // 2, g % 2, y)
            if to is not None:
                pairs.append((g * peers + y, (to[0] * 2 + to[1]) * peers + to[2]))
    return lax.ppermute(x, BOTH, pairs)


def to_core(x):
    return send(x, lambda k, c, y: (k, 1 - c, y))


def to_ring(x, step):
    chips = lax.axis_size("gx") // 2
    order = ring_order(chips)
    at = {k: i for i, k in enumerate(order)}
    return send(x, lambda k, c, y: (order[(at[k] + step) % chips], c, y))


def to_gy(x, step):
    peers = lax.axis_size("gy")
    return send(x, lambda k, c, y: (k, c, (y + step) % peers))


def offsets(chips):
    out = [0]
    for d in range(1, chips // 2):
        out += [-d, d]
    return out + [chips // 2]


def chip_in_slot(gx, slot, chips):
    k = gx // 2
    at = jnp.where(k % 2 == 0, k // 2, chips - 1 - k // 2)
    i = (at + offsets(chips)[slot] + chips) % chips
    return jnp.where(i < chips // 2, 2 * i, 2 * chips - 1 - 2 * i)


def vmem(count):
    return [pl.BlockSpec(memory_space=pltpu.VMEM)] * count


SCALARS = pl.BlockSpec(memory_space=pltpu.SMEM)
SMALL = pltpu.CompilerParams(vmem_limit_bytes=20 * 2**20)


def cost(flops, size):
    return pl.CostEstimate(flops=flops, bytes_accessed=size, transcendentals=0)


def diagonal(small, times):
    size = small.shape[0] * times
    wide = jnp.concatenate([small.astype(f32)] * times, axis=1)
    full = jnp.concatenate([wide] * times, axis=0)
    row = lax.broadcasted_iota(jnp.int32, (size, size), 0) // small.shape[0]
    col = lax.broadcasted_iota(jnp.int32, (size, size), 1) // small.shape[0]
    return jnp.where(row == col, full, 0.0)


def fixed_kernel(
    chips, zl, info, b_output, target_a, target_b, w, b, o, wanted, w_in, w_out, w_back, bias, scale
):
    gx = info[0]
    x_count = target_a.shape[0]
    starts = [
        pl.multiple_of((2 * chip_in_slot(gx, s, chips) + gx % 2) * zl, zl) for s in range(chips)
    ]
    for side, ref in enumerate((target_a, target_b)):

        def one(x, carry):
            rows = jnp.concatenate([ref[x, pl.ds(z, zl), :] for z in starts], axis=0)
            rows = rows - b_output[0]
            high = rows.astype(bf16).astype(f32)
            both = jnp.concatenate([high, rows - high], axis=0)
            wanted[side * x_count + x] = both.T.astype(bf16)
            return carry

        lax.fori_loop(0, x_count, one, 0)
    times = w_in.shape[0] // w.shape[0]
    wide, line = w[...].astype(f32), o[...].astype(f32)
    w_in[...] = diagonal(0.5 * wide, times).astype(bf16)
    w_out[...] = diagonal(jnp.broadcast_to(line, wide.shape).T, times).astype(bf16)
    w_back[...] = diagonal(wide.T, times).astype(bf16)
    bias[...] = jnp.concatenate([0.5 * b[...]] * times, axis=1)
    scale[...] = jnp.concatenate([0.5 * line] * times, axis=1)


def fixed_parts(info, target, target_b, zl, w_hidden, b_hidden, w_output, b_output):
    chips = lax.axis_size("gx") // 2
    x_count, z_count, y_count = target.shape
    hidden = w_hidden.shape[1]
    width = zl * hidden
    square = jax.ShapeDtypeStruct((width, width), bf16)
    line = jax.ShapeDtypeStruct((1, width), f32)
    return pl.pallas_call(
        functools.partial(fixed_kernel, chips, zl),
        in_specs=[SCALARS, SCALARS] + vmem(5),
        out_specs=vmem(6),
        out_shape=[
            jax.ShapeDtypeStruct((2 * x_count, y_count, z_count), bf16),
            square,
            square,
            square,
            line,
            line,
        ],
        compiler_params=SMALL,
        cost_estimate=cost(0, 4 * 2**20),
    )(
        info,
        b_output,
        target,
        target_b,
        w_hidden,
        b_hidden[None],
        w_output[None],
    )


def lanes_kernel(plane, out):
    c, zl, _ = plane.shape
    per = LANES // c
    for t in range(zl // per):
        rows = jnp.concatenate([plane[:, t * per + j, :] for j in range(per)], axis=0)
        out[:, t * LANES : (t + 1) * LANES] = rows.T


def lanes_yz(plane):
    c, zl, y = plane.shape
    return pl.pallas_call(
        lanes_kernel,
        in_specs=vmem(1),
        out_specs=vmem(1)[0],
        out_shape=jax.ShapeDtypeStruct((y, zl * c), f32),
        compiler_params=SMALL,
        cost_estimate=cost(0, 2**18),
    )(plane)


def z_places(gx, gy, slot, chips, peers, zl, zs):
    z = (2 * chip_in_slot(gx, slot, chips) + gx % 2) * zl
    return (gy - z // zs + peers) % peers * zs + z % zs


def spread_xy_kernel(xy_a, xy_b, xy):
    c, x_count, _ = xy_a.shape

    def some(i, carry):
        for x in range(UNROLL):
            x += i * UNROLL
            for side, ref in enumerate((xy_a, xy_b)):
                xy[side * x_count + x] = jnp.concatenate([ref[:, x, :]] * (LANES // c), axis=0).T
        return carry

    lax.fori_loop(0, x_count // UNROLL, some, 0)


def spread_xy(xy_a, xy_b):
    _, x_count, y_count = xy_a.shape
    return pl.pallas_call(
        spread_xy_kernel,
        in_specs=vmem(2),
        out_specs=vmem(1)[0],
        out_shape=jax.ShapeDtypeStruct((2 * x_count, y_count, LANES), f32),
        compiler_params=SMALL,
        cost_estimate=cost(0, 3 * 2**20),
    )(xy_a, xy_b)


def spread_xz_kernel(chips, peers, zl, info, *refs):
    xzs, xz, held = refs[: 2 * peers], refs[2 * peers : -1], refs[-1]
    _, x_count, zs = xzs[0].shape

    def some(i, carry):
        for x in range(UNROLL):
            x += i * UNROLL
            for s in range(peers):
                for side in range(2):
                    held[s * zs : (s + 1) * zs, side * x_count + x, :] = xzs[2 * s + side][:, x, :].T
        return carry

    lax.fori_loop(0, x_count // UNROLL, some, 0)
    for p in range(chips):
        at = z_places(info[0], info[1], p, chips, peers, zl, zs)
        xz[p][...] = jnp.concatenate([held[at + j] for j in range(zl)], axis=1)


def spread_xz(info, xzs, zl):
    peers, chips = lax.axis_size("gy"), lax.axis_size("gx") // 2
    c, x_count, zs = xzs[0].shape
    return pl.pallas_call(
        functools.partial(spread_xz_kernel, chips, peers, zl),
        in_specs=[SCALARS] + vmem(len(xzs)),
        out_specs=vmem(chips),
        out_shape=[jax.ShapeDtypeStruct((2 * x_count, zl * c), f32)] * chips,
        scratch_shapes=[pltpu.VMEM((peers * zs, 2 * x_count, c), f32)],
        compiler_params=SMALL,
        cost_estimate=cost(0, 3 * 2**20),
    )(info, *xzs)


def collect_xy_kernel(part, xy_a, xy_b, *outs):
    c, x_count, _ = xy_a.shape

    def some(i, carry):
        for x in range(UNROLL):
            x += i * UNROLL
            for side, ref in enumerate((xy_a, xy_b)):
                rows = part[side * x_count + x].T
                total = sum(rows[j * c : (j + 1) * c] for j in range(LANES // c))
                outs[side][:, x, :] = total / ref[:, x, :]
        return carry

    lax.fori_loop(0, x_count // UNROLL, some, 0)


def collect_xy(part, xy_a, xy_b):
    return pl.pallas_call(
        collect_xy_kernel,
        in_specs=vmem(3),
        out_specs=vmem(2),
        out_shape=[jax.ShapeDtypeStruct(xy_a.shape, f32)] * 2,
        compiler_params=SMALL,
        cost_estimate=cost(0, 4 * 2**20),
    )(part, xy_a, xy_b)


def collect_xz_kernel(chips, peers, zl, info, *refs):
    parts, outs, held = refs[:chips], refs[chips : chips + 2 * peers], refs[chips + 2 * peers]
    c, x_count, zs = outs[0].shape
    held[...] = jnp.zeros_like(held)
    for p in range(chips):
        at = z_places(info[0], info[1], p, chips, peers, zl, zs)
        rows = parts[p][...]
        for j in range(zl):
            held[at + j] = rows[:, j * c : (j + 1) * c]

    def some(i, carry):
        for x in range(UNROLL):
            x += i * UNROLL
            for s in range(peers):
                for side in range(2):
                    outs[2 * s + side][:, x, :] = held[
                        s * zs : (s + 1) * zs, side * x_count + x, :
                    ].T
        return carry

    lax.fori_loop(0, x_count // UNROLL, some, 0)


def collect_xz(info, parts, shape, zl):
    peers, chips = lax.axis_size("gy"), lax.axis_size("gx") // 2
    c, x_count, zs = shape
    return pl.pallas_call(
        functools.partial(collect_xz_kernel, chips, peers, zl),
        in_specs=[SCALARS] + vmem(chips),
        out_specs=vmem(2 * peers),
        out_shape=[jax.ShapeDtypeStruct(shape, f32)] * (2 * peers),
        scratch_shapes=[pltpu.VMEM((peers * zs, 2 * x_count, c), f32)],
        compiler_params=SMALL,
        cost_estimate=cost(0, 4 * 2**20),
    )(info, *parts)


def grads_kernel(count, first, slot, w_in, w_out, w_back, bias, scale, wanted, xy, *refs):
    refs = list(refs)
    take = lambda k: [refs.pop(0) for _ in range(k)]
    xzs, yzs = take(count), take(count)
    before = None if first else take(1)[0]
    gxy = take(1)[0]
    gxzs, gyzs = take(count), take(count)
    pick, xz, yzb, gxz, gyz = refs
    step = pl.program_id(0)
    x_count, y_count, _ = xy.shape
    width = w_in.shape[0]
    z_count = wanted.shape[2] // 2
    zl = width // CHANNELS
    times = width // LANES

    @pl.when(step == 0)
    def _():
        row = lax.broadcasted_iota(jnp.int32, (2 * z_count, width), 0) % z_count
        col = lax.broadcasted_iota(jnp.int32, (2 * z_count, width), 1) // CHANNELS
        for j in range(count):
            pick[j, :width] = w_out[...]
            pick[j, width:] = jnp.where(row == (slot[0] + j) * zl + col, -1.0, 0.0).astype(bf16)
            yzb[j] = yzs[j][...]
        gyz[...] = jnp.zeros_like(gyz)

    for j in range(count):
        xz[j] = xzs[j][...]
    if first:
        gxy[...] = jnp.zeros_like(gxy)
    else:
        gxy[...] = before[...]

    def one_block(j, carry):
        yz = yzb[j]
        lines = [xz[j, x : x + 1, :] for x in range(x_count)]
        pairs = [jnp.concatenate([xy[x]] * times, axis=1) * yz for x in range(x_count)]
        features = jnp.concatenate([(g * r).astype(bf16) for g, r in zip(pairs, lines)], axis=0)
        half = jnp.dot(features, w_in[...], preferred_element_type=f32) + bias[...]
        t = jnp.tanh(half)
        up = 1.0 + t
        hidden = half * up
        slope = (up + hidden * (1.0 - t)) * scale[...]
        residual = jnp.dot(
            jnp.concatenate(
                [
                    hidden.astype(bf16),
                    jnp.concatenate([wanted[x] for x in range(x_count)], axis=0),
                ],
                axis=1,
            ),
            pick[j],
            preferred_element_type=f32,
        )
        back_hidden = (residual * slope).astype(bf16)
        back = jnp.dot(back_hidden, w_back[...], preferred_element_type=f32)
        total = None
        for x in range(x_count):
            b = back[x * y_count : (x + 1) * y_count] * pairs[x]
            gxz[j, x : x + 1, :] = jnp.sum(b, axis=0, keepdims=True)
            e = b * lines[x]
            gxy[x] += sum(e[:, h * LANES : (h + 1) * LANES] for h in range(times))
            total = e if total is None else total + e
        gyz[j] += total
        return carry

    lax.fori_loop(0, count, one_block, 0)
    for j in range(count):
        gxzs[j][...] = gxz[j]

    @pl.when(step == 1)
    def _():
        for j in range(count):
            gyzs[j][...] = gyz[j] / yzb[j]


def block_grads(slots, weights, wanted, xy, xzs, yzs, before):
    count = len(slots)
    rows, y_count, _ = xy.shape
    rows = rows // 2
    width = yzs[0].shape[1]

    def whole(a):
        return pl.BlockSpec(a.shape, lambda i: (0,) * a.ndim)

    side = pl.BlockSpec((rows, y_count, LANES), lambda i: (i, 0, 0))
    line = pl.BlockSpec((rows, width), lambda i: (i, 0))
    outs = pl.pallas_call(
        functools.partial(grads_kernel, count, before is None),
        grid=(2,),
        in_specs=[SCALARS]
        + [whole(w) for w in weights]
        + [side, side]
        + [line] * count
        + [whole(a) for a in yzs]
        + ([] if before is None else [side]),
        out_specs=[side] + [line] * count + [whole(a) for a in yzs],
        out_shape=[jax.ShapeDtypeStruct(xy.shape, f32)]
        + [jax.ShapeDtypeStruct((2 * rows, width), f32)] * count
        + [jax.ShapeDtypeStruct(a.shape, f32) for a in yzs],
        scratch_shapes=[
            pltpu.VMEM((count, width + wanted.shape[2], width), bf16),
            pltpu.VMEM((count, rows, width), f32),
            pltpu.VMEM((count, y_count, width), f32),
            pltpu.VMEM((count, rows, width), f32),
            pltpu.VMEM((count, y_count, width), f32),
        ],
        compiler_params=pltpu.CompilerParams(vmem_limit_bytes=GRADS_VMEM),
        cost_estimate=cost(12 * rows * y_count * count * width * width, count * 10 * 2**20),
    )(
        jnp.array(slots[:1], jnp.int32),
        *weights,
        wanted,
        xy,
        *[xzs[s] for s in slots],
        *yzs,
        *([] if before is None else [before]),
    )
    return outs[0], outs[1 : 1 + count], outs[1 + count :]


def near_sides(p, above, below, left, right):
    rows, cols = p.shape[1:]
    row = lax.broadcasted_iota(jnp.int32, p.shape, 1)
    col = lax.broadcasted_iota(jnp.int32, p.shape, 2)
    up = jnp.where(row == 0, above, pltpu.roll(p, 1, 1))
    down = jnp.where(row == rows - 1, below, pltpu.roll(p, rows - 1, 1))
    wide = p if cols % LANES == 0 else jnp.concatenate([p] * (LANES // cols), axis=2)
    back = pltpu.roll(wide, 1, 2)[:, :, :cols]
    ahead = pltpu.roll(wide, wide.shape[2] - 1, 2)[:, :, :cols]
    return up, down, jnp.where(col == 0, left, back), jnp.where(col == cols - 1, right, ahead)


def upright(ref, at, shape):
    c, rows, cols = shape
    line = ref[:, at : at + c * rows]
    return jnp.broadcast_to(line, (cols, c * rows)).T.reshape(shape)


def update(info, ends, count, plane, first, second, grad, borders, at_row, at_col, outs):
    above, below, left, right = borders
    p = plane[...]
    rows, cols = p.shape[1:]
    above = jnp.where(info[0] == 0, p[:, :1, :], above[:, :, at_row : at_row + cols])
    below = jnp.where(info[0] == ends[0], p[:, rows - 1 :, :], below[:, :, at_row : at_row + cols])
    left = jnp.where(info[1] == 0, p, upright(left, at_col, p.shape))
    right = jnp.where(info[1] == ends[1], p, upright(right, at_col, p.shape))
    up, down, back, ahead = near_sides(p, above, below, left, right)
    grad = grad + 2.0 * SMOOTHING * ((p - up) + (p - down) + (p - back) + (p - ahead))
    m = BETA_ONE * first[...] + (1.0 - BETA_ONE) * grad
    v = BETA_TWO * second[...] + (1.0 - BETA_TWO) * grad * grad
    corr_one = 1.0 - BETA_ONE**count
    corr_two = 1.0 - BETA_TWO**count
    outs[1][...] = m
    outs[2][...] = v
    outs[0][...] = p - LEARN_RATE * (m / corr_one) / (jnp.sqrt(v / corr_two) + EPSILON)


def update_one_kernel(ends, count, at_row, at_col, info, above, below, left, right, *refs):
    state, grads, outs = refs[:3], refs[3:-3], refs[-3:]
    grad = sum(g[...] for g in grads)
    borders = (above, below, left, right)
    update(info, ends, count, *state, grad, borders, at_row, at_col, outs)


def update_one(info, count, borders, state, grads, at_row, at_col):
    ends = (lax.axis_size("gx") - 1, lax.axis_size("gy") - 1)
    return pl.pallas_call(
        functools.partial(update_one_kernel, ends, count, at_row, at_col),
        in_specs=[SCALARS] + vmem(7 + len(grads)),
        out_specs=vmem(3),
        out_shape=[jax.ShapeDtypeStruct(a.shape, f32) for a in state],
        compiler_params=SMALL,
        cost_estimate=cost(0, 2 * 2**20),
    )(info, *borders, *state, *grads)


def update_yz_kernel(ends, count, info, above, below, left, right, plane, first, second, a, b, d, *refs):
    outs, lanes, held = refs[:3], refs[3], refs[4]
    c, zl, width = plane.shape
    per = LANES // c
    for t in range(zl // per):
        at = slice(t * LANES, (t + 1) * LANES)
        rows = (a[:, at] + b[:, at] + d[:, at]).T
        for j in range(per):
            held[:, t * per + j, :] = rows[j * c : (j + 1) * c]
    borders = (above, below, left, right)
    at_col = left.shape[1] - c * zl
    update(info, ends, count, plane, first, second, held[...], borders, width, at_col, outs)
    lanes_kernel(outs[0], lanes)


def update_yz(info, count, borders, state, parts):
    ends = (lax.axis_size("gx") - 1, lax.axis_size("gy") - 1)
    outs = pl.pallas_call(
        functools.partial(update_yz_kernel, ends, count),
        in_specs=[SCALARS] + vmem(10),
        out_specs=vmem(4),
        out_shape=[jax.ShapeDtypeStruct(a.shape, f32) for a in (*state, parts[0])],
        scratch_shapes=[pltpu.VMEM(state[0].shape, f32)],
        compiler_params=SMALL,
        cost_estimate=cost(0, 2 * 2**20),
    )(info, *borders, *state, *parts)
    return outs[:3], outs[3]


def edges_kernel(peers, info, xy, xz, yz, *outs):
    width = xy.shape[2]
    for ref, at in ((xy, 0), (yz, width), (xz, 2 * width)):
        rows, cols = ref.shape[1:]
        outs[0][:, :, at : at + cols] = ref[:, rows - 1 :, :]
        outs[1][:, :, at : at + cols] = ref[:, :1, :]
    at = 0
    for ref in (xy, xz, yz):
        c, rows, cols = ref.shape
        flat = ref[...].reshape(c * rows, cols).T
        last, first = flat[cols - 1 :], flat[:1]
        here = slice(at, at + c * rows)
        if peers == 2:
            outs[2][:, here] = jnp.where(info[1] == 0, last, first)
        else:
            outs[2][:, here] = last
            outs[3][:, here] = first
        at += c * rows


def borders(info, planes):
    n, peers = lax.axis_size("gx"), lax.axis_size("gy")
    c = planes[0].shape[0]
    row = jax.ShapeDtypeStruct((c, 1, sum(p.shape[2] for p in planes)), f32)
    col = jax.ShapeDtypeStruct((1, sum(c * p.shape[1] for p in planes)), f32)
    outs = pl.pallas_call(
        functools.partial(edges_kernel, peers),
        in_specs=[SCALARS] + vmem(3),
        out_specs=vmem(3 if peers == 2 else 4),
        out_shape=[row, row] + [col] * (1 if peers == 2 else 2),
        compiler_params=SMALL,
        cost_estimate=cost(0, 2**20),
    )(info, *planes)
    up = [(i, i + 1) for i in range(n - 1)]
    above = lax.ppermute(outs[0], "gx", up)
    below = lax.ppermute(outs[1], "gx", [(j, i) for i, j in up])
    if peers == 2:
        left = right = lax.ppermute(outs[2], "gy", [(0, 1), (1, 0)])
    else:
        up = [(i, i + 1) for i in range(peers - 1)]
        left = lax.ppermute(outs[2], "gy", up)
        right = lax.ppermute(outs[3], "gy", [(j, i) for i, j in up])
    return above, below, left, right


def per_device(
    target,
    plane_xy,
    plane_xz,
    plane_yz,
    first_xy,
    first_xz,
    first_yz,
    second_xy,
    second_xz,
    second_yz,
    w_hidden,
    b_hidden,
    w_output,
    b_output,
):
    peers = lax.axis_size("gy")
    info = jnp.stack([lax.axis_index("gx"), lax.axis_index("gy")]).astype(jnp.int32)
    zl = plane_yz.shape[1]
    lanes = lanes_yz(plane_yz)
    target_b = to_core(target)
    fixed = None

    chips = lax.axis_size("gx") // 2
    half = chips // 2
    slot = {o: i for i, o in enumerate(offsets(chips))}
    middle = lanes.shape[0] // 2

    for iteration in range(STEPS):
        back, ahead = {0: lanes}, {0: lanes}
        for d in range(1, half):
            back[d], ahead[d] = to_ring(back[d - 1], 1), to_ring(ahead[d - 1], -1)
        parts = to_ring(back[half - 1][:middle], 1), to_ring(ahead[half - 1][middle:], -1)
        far = jnp.concatenate(parts, axis=0)
        yzs = {0: lanes, half: far}
        for d in range(1, half):
            yzs[-d], yzs[d] = back[d], ahead[d]
        xy_b, xz_b = to_core(plane_xy), to_core(plane_xz)
        xzs = [plane_xz, xz_b]
        for s in range(1, peers):
            xz_y = to_gy(plane_xz, s)
            xzs += [xz_y, to_core(xz_y)]
        around = borders(info, (plane_xy, plane_xz, plane_yz))
        if fixed is None:
            fixed = fixed_parts(info, target, target_b, zl, w_hidden, b_hidden, w_output, b_output)
        wanted, weights = fixed[0], fixed[1:]
        xy = spread_xy(plane_xy, xy_b)
        xz = spread_xz(info, xzs, zl)

        order = [(0,), (-1,), (1,), (half,)] + [(-d, d) for d in range(half - 1, 1, -1)]
        part_xy, parts_xz, parts_yz = None, {}, {}
        send_ahead, send_back = None, None
        for group in order:
            part_xy, lines, blocks = block_grads(
                [slot[o] for o in group], weights, wanted, xy, xz, [yzs[o] for o in group], part_xy
            )
            for o, line, block in zip(group, lines, blocks):
                parts_xz[slot[o]], parts_yz[o] = line, block
        block = parts_yz[half]
        send_ahead, send_back = to_ring(block[:middle], 1), to_ring(block[middle:], -1)
        for d in range(half - 1, 0, -1):
            if d == half - 1:
                send_ahead = jnp.pad(send_ahead, ((0, middle), (0, 0)))
                send_back = jnp.pad(send_back, ((middle, 0), (0, 0)))
            send_ahead, send_back = parts_yz[d] + send_ahead, parts_yz[-d] + send_back
            send_ahead, send_back = to_ring(send_ahead, 1), to_ring(send_back, -1)

        pieces = collect_xz(info, [parts_xz[i] for i in range(chips)], plane_xz.shape, zl)
        grad_xy, far_xy = collect_xy(part_xy, plane_xy, xy_b)
        sides = [pieces[2 * s] + to_core(pieces[2 * s + 1]) for s in range(1, peers)]
        grads_xz = [to_gy(side, -s) for s, side in enumerate(sides, 1)]
        near_xz, far_xz = pieces[0], to_core(pieces[1])
        for extra in grads_xz[1:]:
            near_xz = near_xz + extra
        count = START + iteration + 1
        channels, rows, width = plane_xy.shape
        state = (plane_xz, first_xz, second_xz)
        plane_xz, first_xz, second_xz = update_one(
            info, count, around, state, (near_xz, far_xz, grads_xz[0]), 2 * width, channels * rows
        )
        state = (plane_xy, first_xy, second_xy)
        far_xy = to_core(far_xy)
        plane_xy, first_xy, second_xy = update_one(
            info, count, around, state, (grad_xy, far_xy), 0, 0
        )
        (plane_yz, first_yz, second_yz), lanes = update_yz(
            info, count, around, (plane_yz, first_yz, second_yz), (parts_yz[0], send_ahead, send_back)
        )
    return (
        plane_xy,
        plane_xz,
        plane_yz,
        first_xy,
        first_xz,
        first_yz,
        second_xy,
        second_xz,
        second_yz,
    )


def solution(mesh):
    return jax.shard_map(
        per_device,
        mesh=mesh,
        in_specs=(
            P("gx", None, "gy"),
            P(None, "gx", "gy"),
            P(None, "gx", "gy"),
            P(None, "gx", "gy"),
            P(None, "gx", "gy"),
            P(None, "gx", "gy"),
            P(None, "gx", "gy"),
            P(None, "gx", "gy"),
            P(None, "gx", "gy"),
            P(None, "gx", "gy"),
            P(),
            P(),
            P(),
            P(),
        ),
        out_specs=(
            P(None, "gx", "gy"),
            P(None, "gx", "gy"),
            P(None, "gx", "gy"),
            P(None, "gx", "gy"),
            P(None, "gx", "gy"),
            P(None, "gx", "gy"),
            P(None, "gx", "gy"),
            P(None, "gx", "gy"),
            P(None, "gx", "gy"),
        ),
        check_vma=False,
    )
```

```python
import functools
import jax
import jax.numpy as jnp
from jax import lax
from jax.experimental import pallas as pl
from jax.experimental.pallas import tpu as pltpu
from jax.sharding import PartitionSpec as P


STEPS = 2
START = 20


SMOOTHING = 0.5
BETA_ONE = 0.9
BETA_TWO = 0.99
LEARN_RATE = 0.01
EPSILON = 1e-08

LANES = 128
CHANNELS = 32
UNROLL = 4
GRADS_VMEM = 16 * 2**20
BOTH = ("gx", "gy")
f32 = jnp.float32
bf16 = jnp.bfloat16


def ring_order(chips):
    return list(range(0, chips, 2)) + list(range(chips - 1, 0, -2))


def send(x, move):
    n, peers = lax.axis_size("gx"), lax.axis_size("gy")
    pairs = []
    for g in range(n):
        for y in range(peers):
            to = move(g // 2, g % 2, y)
            if to is not None:
                pairs.append((g * peers + y, (to[0] * 2 + to[1]) * peers + to[2]))
    return lax.ppermute(x, BOTH, pairs)


def to_core(x):
    return send(x, lambda k, c, y: (k, 1 - c, y))


def to_ring(x, step):
    chips = lax.axis_size("gx") // 2
    order = ring_order(chips)
    at = {k: i for i, k in enumerate(order)}
    return send(x, lambda k, c, y: (order[(at[k] + step) % chips], c, y))


def to_gy(x, step):
    peers = lax.axis_size("gy")
    return send(x, lambda k, c, y: (k, c, (y + step) % peers))


def offsets(chips):
    out = [0]
    for d in range(1, chips // 2):
        out += [-d, d]
    return out + [chips // 2]


def chip_in_slot(gx, slot, chips):
    k = gx // 2
    at = jnp.where(k % 2 == 0, k // 2, chips - 1 - k // 2)
    i = (at + offsets(chips)[slot] + chips) % chips
    return jnp.where(i < chips // 2, 2 * i, 2 * chips - 1 - 2 * i)


def vmem(count):
    return [pl.BlockSpec(memory_space=pltpu.VMEM)] * count


SCALARS = pl.BlockSpec(memory_space=pltpu.SMEM)
SMALL = pltpu.CompilerParams(vmem_limit_bytes=20 * 2**20)


def cost(flops, size):
    return pl.CostEstimate(flops=flops, bytes_accessed=size, transcendentals=0)


def diagonal(small, times):
    size = small.shape[0] * times
    wide = jnp.concatenate([small.astype(f32)] * times, axis=1)
    full = jnp.concatenate([wide] * times, axis=0)
    row = lax.broadcasted_iota(jnp.int32, (size, size), 0) // small.shape[0]
    col = lax.broadcasted_iota(jnp.int32, (size, size), 1) // small.shape[0]
    return jnp.where(row == col, full, 0.0)


def fixed_kernel(
    chips, zl, info, b_output, target_a, target_b, w, b, o, wanted, w_in, w_out, w_back, bias, scale
):
    gx = info[0]
    x_count = target_a.shape[0]
    starts = [
        pl.multiple_of((2 * chip_in_slot(gx, s, chips) + gx % 2) * zl, zl) for s in range(chips)
    ]
    for side, ref in enumerate((target_a, target_b)):

        def one(x, carry):
            rows = jnp.concatenate([ref[x, pl.ds(z, zl), :] for z in starts], axis=0)
            rows = rows - b_output[0]
            high = rows.astype(bf16).astype(f32)
            both = jnp.concatenate([high, rows - high], axis=0)
            wanted[side * x_count + x] = both.T.astype(bf16)
            return carry

        lax.fori_loop(0, x_count, one, 0)
    times = w_in.shape[0] // w.shape[0]
    wide, line = w[...].astype(f32), o[...].astype(f32)
    w_in[...] = diagonal(0.5 * wide, times).astype(bf16)
    w_out[...] = diagonal(jnp.broadcast_to(line, wide.shape).T, times).astype(bf16)
    w_back[...] = diagonal(wide.T, times).astype(bf16)
    bias[...] = jnp.concatenate([0.5 * b[...]] * times, axis=1)
    scale[...] = jnp.concatenate([0.5 * line] * times, axis=1)


def fixed_parts(info, target, target_b, zl, w_hidden, b_hidden, w_output, b_output):
    chips = lax.axis_size("gx") // 2
    x_count, z_count, y_count = target.shape
    hidden = w_hidden.shape[1]
    width = zl * hidden
    square = jax.ShapeDtypeStruct((width, width), bf16)
    line = jax.ShapeDtypeStruct((1, width), f32)
    return pl.pallas_call(
        functools.partial(fixed_kernel, chips, zl),
        in_specs=[SCALARS, SCALARS] + vmem(5),
        out_specs=vmem(6),
        out_shape=[
            jax.ShapeDtypeStruct((2 * x_count, y_count, z_count), bf16),
            square,
            square,
            square,
            line,
            line,
        ],
        compiler_params=SMALL,
        cost_estimate=cost(0, 4 * 2**20),
    )(
        info,
        b_output,
        target,
        target_b,
        w_hidden,
        b_hidden[None],
        w_output[None],
    )


def lanes_kernel(plane, out):
    c, zl, _ = plane.shape
    per = LANES // c
    for t in range(zl // per):
        rows = jnp.concatenate([plane[:, t * per + j, :] for j in range(per)], axis=0)
        out[:, t * LANES : (t + 1) * LANES] = rows.T


def lanes_yz(plane):
    c, zl, y = plane.shape
    return pl.pallas_call(
        lanes_kernel,
        in_specs=vmem(1),
        out_specs=vmem(1)[0],
        out_shape=jax.ShapeDtypeStruct((y, zl * c), f32),
        compiler_params=SMALL,
        cost_estimate=cost(0, 2**18),
    )(plane)


def z_places(gx, gy, slot, chips, peers, zl, zs):
    z = (2 * chip_in_slot(gx, slot, chips) + gx % 2) * zl
    return (gy - z // zs + peers) % peers * zs + z % zs


def spread_xy_kernel(xy_a, xy_b, xy):
    c, x_count, _ = xy_a.shape

    def some(i, carry):
        for x in range(UNROLL):
            x += i * UNROLL
            for side, ref in enumerate((xy_a, xy_b)):
                xy[side * x_count + x] = jnp.concatenate([ref[:, x, :]] * (LANES // c), axis=0).T
        return carry

    lax.fori_loop(0, x_count // UNROLL, some, 0)


def spread_xy(xy_a, xy_b):
    _, x_count, y_count = xy_a.shape
    return pl.pallas_call(
        spread_xy_kernel,
        in_specs=vmem(2),
        out_specs=vmem(1)[0],
        out_shape=jax.ShapeDtypeStruct((2 * x_count, y_count, LANES), f32),
        compiler_params=SMALL,
        cost_estimate=cost(0, 3 * 2**20),
    )(xy_a, xy_b)


def spread_xz_kernel(chips, peers, zl, info, *refs):
    xzs, xz, held = refs[: 2 * peers], refs[2 * peers : -1], refs[-1]
    _, x_count, zs = xzs[0].shape

    def some(i, carry):
        for x in range(UNROLL):
            x += i * UNROLL
            for s in range(peers):
                for side in range(2):
                    held[s * zs : (s + 1) * zs, side * x_count + x, :] = xzs[2 * s + side][:, x, :].T
        return carry

    lax.fori_loop(0, x_count // UNROLL, some, 0)
    for p in range(chips):
        at = z_places(info[0], info[1], p, chips, peers, zl, zs)
        xz[p][...] = jnp.concatenate([held[at + j] for j in range(zl)], axis=1)


def spread_xz(info, xzs, zl):
    peers, chips = lax.axis_size("gy"), lax.axis_size("gx") // 2
    c, x_count, zs = xzs[0].shape
    return pl.pallas_call(
        functools.partial(spread_xz_kernel, chips, peers, zl),
        in_specs=[SCALARS] + vmem(len(xzs)),
        out_specs=vmem(chips),
        out_shape=[jax.ShapeDtypeStruct((2 * x_count, zl * c), f32)] * chips,
        scratch_shapes=[pltpu.VMEM((peers * zs, 2 * x_count, c), f32)],
        compiler_params=SMALL,
        cost_estimate=cost(0, 3 * 2**20),
    )(info, *xzs)


def collect_xy_kernel(part, xy_a, xy_b, *outs):
    c, x_count, _ = xy_a.shape

    def some(i, carry):
        for x in range(UNROLL):
            x += i * UNROLL
            for side, ref in enumerate((xy_a, xy_b)):
                rows = part[side * x_count + x].T
                total = sum(rows[j * c : (j + 1) * c] for j in range(LANES // c))
                outs[side][:, x, :] = total / ref[:, x, :]
        return carry

    lax.fori_loop(0, x_count // UNROLL, some, 0)


def collect_xy(part, xy_a, xy_b):
    return pl.pallas_call(
        collect_xy_kernel,
        in_specs=vmem(3),
        out_specs=vmem(2),
        out_shape=[jax.ShapeDtypeStruct(xy_a.shape, f32)] * 2,
        compiler_params=SMALL,
        cost_estimate=cost(0, 4 * 2**20),
    )(part, xy_a, xy_b)


def collect_xz_kernel(chips, peers, zl, info, *refs):
    parts, outs, held = refs[:chips], refs[chips : chips + 2 * peers], refs[chips + 2 * peers]
    c, x_count, zs = outs[0].shape
    held[...] = jnp.zeros_like(held)
    for p in range(chips):
        at = z_places(info[0], info[1], p, chips, peers, zl, zs)
        rows = parts[p][...]
        for j in range(zl):
            held[at + j] = rows[:, j * c : (j + 1) * c]

    def some(i, carry):
        for x in range(UNROLL):
            x += i * UNROLL
            for s in range(peers):
                for side in range(2):
                    outs[2 * s + side][:, x, :] = held[
                        s * zs : (s + 1) * zs, side * x_count + x, :
                    ].T
        return carry

    lax.fori_loop(0, x_count // UNROLL, some, 0)


def collect_xz(info, parts, shape, zl):
    peers, chips = lax.axis_size("gy"), lax.axis_size("gx") // 2
    c, x_count, zs = shape
    return pl.pallas_call(
        functools.partial(collect_xz_kernel, chips, peers, zl),
        in_specs=[SCALARS] + vmem(chips),
        out_specs=vmem(2 * peers),
        out_shape=[jax.ShapeDtypeStruct(shape, f32)] * (2 * peers),
        scratch_shapes=[pltpu.VMEM((peers * zs, 2 * x_count, c), f32)],
        compiler_params=SMALL,
        cost_estimate=cost(0, 4 * 2**20),
    )(info, *parts)


def grads_kernel(count, first, slot, w_in, w_out, w_back, bias, scale, wanted, xy, *refs):
    refs = list(refs)
    take = lambda k: [refs.pop(0) for _ in range(k)]
    xzs, yzs = take(count), take(count)
    before = None if first else take(1)[0]
    gxy = take(1)[0]
    gxzs, gyzs = take(count), take(count)
    pick, xz, yzb, gxz, gyz = refs
    step = pl.program_id(0)
    x_count, y_count, _ = xy.shape
    width = w_in.shape[0]
    z_count = wanted.shape[2] // 2
    zl = width // CHANNELS
    times = width // LANES

    @pl.when(step == 0)
    def _():
        row = lax.broadcasted_iota(jnp.int32, (2 * z_count, width), 0) % z_count
        col = lax.broadcasted_iota(jnp.int32, (2 * z_count, width), 1) // CHANNELS
        for j in range(count):
            pick[j, :width] = w_out[...]
            pick[j, width:] = jnp.where(row == (slot[0] + j) * zl + col, -1.0, 0.0).astype(bf16)
            yzb[j] = yzs[j][...]
        gyz[...] = jnp.zeros_like(gyz)

    for j in range(count):
        xz[j] = xzs[j][...]
    if first:
        gxy[...] = jnp.zeros_like(gxy)
    else:
        gxy[...] = before[...]

    def one_block(j, carry):
        yz = yzb[j]
        lines = [xz[j, x : x + 1, :] for x in range(x_count)]
        pairs = [jnp.concatenate([xy[x]] * times, axis=1) * yz for x in range(x_count)]
        features = jnp.concatenate([(g * r).astype(bf16) for g, r in zip(pairs, lines)], axis=0)
        half = jnp.dot(features, w_in[...], preferred_element_type=f32) + bias[...]
        t = jnp.tanh(half)
        up = 1.0 + t
        hidden = half * up
        slope = (up + hidden * (1.0 - t)) * scale[...]
        residual = jnp.dot(
            jnp.concatenate(
                [
                    hidden.astype(bf16),
                    jnp.concatenate([wanted[x] for x in range(x_count)], axis=0),
                ],
                axis=1,
            ),
            pick[j],
            preferred_element_type=f32,
        )
        back_hidden = (residual * slope).astype(bf16)
        back = jnp.dot(back_hidden, w_back[...], preferred_element_type=f32)
        total = None
        for x in range(x_count):
            b = back[x * y_count : (x + 1) * y_count] * pairs[x]
            gxz[j, x : x + 1, :] = jnp.sum(b, axis=0, keepdims=True)
            e = b * lines[x]
            gxy[x] += sum(e[:, h * LANES : (h + 1) * LANES] for h in range(times))
            total = e if total is None else total + e
        gyz[j] += total
        return carry

    lax.fori_loop(0, count, one_block, 0)
    for j in range(count):
        gxzs[j][...] = gxz[j]

    @pl.when(step == 1)
    def _():
        for j in range(count):
            gyzs[j][...] = gyz[j] / yzb[j]


def block_grads(slots, weights, wanted, xy, xzs, yzs, before):
    count = len(slots)
    rows, y_count, _ = xy.shape
    rows = rows // 2
    width = yzs[0].shape[1]

    def whole(a):
        return pl.BlockSpec(a.shape, lambda i: (0,) * a.ndim)

    side = pl.BlockSpec((rows, y_count, LANES), lambda i: (i, 0, 0))
    line = pl.BlockSpec((rows, width), lambda i: (i, 0))
    outs = pl.pallas_call(
        functools.partial(grads_kernel, count, before is None),
        grid=(2,),
        in_specs=[SCALARS]
        + [whole(w) for w in weights]
        + [side, side]
        + [line] * count
        + [whole(a) for a in yzs]
        + ([] if before is None else [side]),
        out_specs=[side] + [line] * count + [whole(a) for a in yzs],
        out_shape=[jax.ShapeDtypeStruct(xy.shape, f32)]
        + [jax.ShapeDtypeStruct((2 * rows, width), f32)] * count
        + [jax.ShapeDtypeStruct(a.shape, f32) for a in yzs],
        scratch_shapes=[
            pltpu.VMEM((count, width + wanted.shape[2], width), bf16),
            pltpu.VMEM((count, rows, width), f32),
            pltpu.VMEM((count, y_count, width), f32),
            pltpu.VMEM((count, rows, width), f32),
            pltpu.VMEM((count, y_count, width), f32),
        ],
        compiler_params=pltpu.CompilerParams(vmem_limit_bytes=GRADS_VMEM),
        cost_estimate=cost(12 * rows * y_count * count * width * width, count * 10 * 2**20),
    )(
        jnp.array(slots[:1], jnp.int32),
        *weights,
        wanted,
        xy,
        *[xzs[s] for s in slots],
        *yzs,
        *([] if before is None else [before]),
    )
    return outs[0], outs[1 : 1 + count], outs[1 + count :]


def near_sides(p, above, below, left, right):
    rows, cols = p.shape[1:]
    row = lax.broadcasted_iota(jnp.int32, p.shape, 1)
    col = lax.broadcasted_iota(jnp.int32, p.shape, 2)
    up = jnp.where(row == 0, above, pltpu.roll(p, 1, 1))
    down = jnp.where(row == rows - 1, below, pltpu.roll(p, rows - 1, 1))
    wide = p if cols % LANES == 0 else jnp.concatenate([p] * (LANES // cols), axis=2)
    back = pltpu.roll(wide, 1, 2)[:, :, :cols]
    ahead = pltpu.roll(wide, wide.shape[2] - 1, 2)[:, :, :cols]
    return up, down, jnp.where(col == 0, left, back), jnp.where(col == cols - 1, right, ahead)


def upright(ref, at, shape):
    c, rows, cols = shape
    line = ref[:, at : at + c * rows]
    return jnp.broadcast_to(line, (cols, c * rows)).T.reshape(shape)


def update(info, ends, count, plane, first, second, grad, borders, at_row, at_col, outs):
    chip, core, left, right = borders
    odd = info[0] % 2 == 1
    above, below = jnp.where(odd, core[...], chip[...]), jnp.where(odd, chip[...], core[...])
    p = plane[...]
    rows, cols = p.shape[1:]
    above = jnp.where(info[0] == 0, p[:, :1, :], above[:, :, at_row : at_row + cols])
    below = jnp.where(info[0] == ends[0], p[:, rows - 1 :, :], below[:, :, at_row : at_row + cols])
    left = jnp.where(info[1] == 0, p, upright(left, at_col, p.shape))
    right = jnp.where(info[1] == ends[1], p, upright(right, at_col, p.shape))
    up, down, back, ahead = near_sides(p, above, below, left, right)
    grad = grad + 2.0 * SMOOTHING * ((p - up) + (p - down) + (p - back) + (p - ahead))
    m = BETA_ONE * first[...] + (1.0 - BETA_ONE) * grad
    v = BETA_TWO * second[...] + (1.0 - BETA_TWO) * grad * grad
    corr_one = 1.0 - BETA_ONE**count
    corr_two = 1.0 - BETA_TWO**count
    outs[1][...] = m
    outs[2][...] = v
    outs[0][...] = p - LEARN_RATE * (m / corr_one) / (jnp.sqrt(v / corr_two) + EPSILON)


def update_one_kernel(ends, count, at_row, at_col, info, above, below, left, right, *refs):
    state, grads, outs = refs[:3], refs[3:-3], refs[-3:]
    grad = sum(g[...] for g in grads)
    borders = (above, below, left, right)
    update(info, ends, count, *state, grad, borders, at_row, at_col, outs)


def update_one(info, count, borders, state, grads, at_row, at_col):
    ends = (lax.axis_size("gx") - 1, lax.axis_size("gy") - 1)
    return pl.pallas_call(
        functools.partial(update_one_kernel, ends, count, at_row, at_col),
        in_specs=[SCALARS] + vmem(7 + len(grads)),
        out_specs=vmem(3),
        out_shape=[jax.ShapeDtypeStruct(a.shape, f32) for a in state],
        compiler_params=SMALL,
        cost_estimate=cost(0, 2 * 2**20),
    )(info, *borders, *state, *grads)


def update_yz_kernel(ends, count, info, above, below, left, right, plane, first, second, a, b, d, *refs):
    outs, lanes, held = refs[:3], refs[3], refs[4]
    c, zl, width = plane.shape
    per = LANES // c
    for t in range(zl // per):
        at = slice(t * LANES, (t + 1) * LANES)
        rows = (a[:, at] + b[:, at] + d[:, at]).T
        for j in range(per):
            held[:, t * per + j, :] = rows[j * c : (j + 1) * c]
    borders = (above, below, left, right)
    at_col = left.shape[1] - c * zl
    update(info, ends, count, plane, first, second, held[...], borders, width, at_col, outs)
    lanes_kernel(outs[0], lanes)


def update_yz(info, count, borders, state, parts):
    ends = (lax.axis_size("gx") - 1, lax.axis_size("gy") - 1)
    outs = pl.pallas_call(
        functools.partial(update_yz_kernel, ends, count),
        in_specs=[SCALARS] + vmem(10),
        out_specs=vmem(4),
        out_shape=[jax.ShapeDtypeStruct(a.shape, f32) for a in (*state, parts[0])],
        scratch_shapes=[pltpu.VMEM(state[0].shape, f32)],
        compiler_params=SMALL,
        cost_estimate=cost(0, 2 * 2**20),
    )(info, *borders, *state, *parts)
    return outs[:3], outs[3]


def edges_kernel(peers, info, xy, xz, yz, gate, *outs):
    width = xy.shape[2]
    for ref, at in ((xy, 0), (yz, width), (xz, 2 * width)):
        rows, cols = ref.shape[1:]
        last, first = ref[:, rows - 1 :, :], ref[:, :1, :]
        odd = info[0] % 2 == 1
        outs[0][:, :, at : at + cols] = jnp.where(odd, last, first)
        outs[1][:, :, at : at + cols] = jnp.where(odd, first, last)
    at = 0
    for ref in (xy, xz, yz):
        c, rows, cols = ref.shape
        flat = ref[...].reshape(c * rows, cols).T
        last, first = flat[cols - 1 :], flat[:1]
        here = slice(at, at + c * rows)
        if peers == 2:
            outs[2][:, here] = jnp.where(info[1] == 0, last, first)
        else:
            outs[2][:, here] = last
            outs[3][:, here] = first
        at += c * rows


def borders(info, planes, gate):
    n, peers = lax.axis_size("gx"), lax.axis_size("gy")
    c = planes[0].shape[0]
    row = jax.ShapeDtypeStruct((c, 1, sum(p.shape[2] for p in planes)), f32)
    col = jax.ShapeDtypeStruct((1, sum(c * p.shape[1] for p in planes)), f32)
    outs = pl.pallas_call(
        functools.partial(edges_kernel, peers),
        in_specs=[SCALARS] + vmem(3) + [pl.BlockSpec(memory_space=pl.ANY)],
        out_specs=vmem(3 if peers == 2 else 4),
        out_shape=[row, row] + [col] * (1 if peers == 2 else 2),
        compiler_params=SMALL,
        cost_estimate=cost(0, 2**20),
    )(info, *planes, gate)

    def next_chip(k, c, y):
        to = k + 1 if c == 1 else k - 1
        return (to, 1 - c, y) if 0 <= to < n // 2 else None

    chip, core = send(outs[0], next_chip), to_core(outs[1])
    if peers == 2:
        left = right = lax.ppermute(outs[2], "gy", [(0, 1), (1, 0)])
    else:
        up = [(i, i + 1) for i in range(peers - 1)]
        left = lax.ppermute(outs[2], "gy", up)
        right = lax.ppermute(outs[3], "gy", [(j, i) for i, j in up])
    return chip, core, left, right


def per_device(
    target,
    plane_xy,
    plane_xz,
    plane_yz,
    first_xy,
    first_xz,
    first_yz,
    second_xy,
    second_xz,
    second_yz,
    w_hidden,
    b_hidden,
    w_output,
    b_output,
):
    peers = lax.axis_size("gy")
    info = jnp.stack([lax.axis_index("gx"), lax.axis_index("gy")]).astype(jnp.int32)
    zl = plane_yz.shape[1]
    lanes = lanes_yz(plane_yz)
    target_b = to_core(target)
    fixed = None

    chips = lax.axis_size("gx") // 2
    half = chips // 2
    slot = {o: i for i, o in enumerate(offsets(chips))}
    middle = lanes.shape[0] // 2

    for iteration in range(STEPS):
        back, ahead = {0: lanes}, {0: lanes}
        for d in range(1, half):
            back[d], ahead[d] = to_ring(back[d - 1], 1), to_ring(ahead[d - 1], -1)
        parts = to_ring(back[half - 1][:middle], 1), to_ring(ahead[half - 1][middle:], -1)
        far = jnp.concatenate(parts, axis=0)
        yzs = {0: lanes, half: far}
        for d in range(1, half):
            yzs[-d], yzs[d] = back[d], ahead[d]
        xy_b, xz_b = to_core(plane_xy), to_core(plane_xz)
        xzs = [plane_xz, xz_b]
        for s in range(1, peers):
            xz_y = to_gy(plane_xz, s)
            xzs += [xz_y, to_core(xz_y)]
        if fixed is None:
            fixed = fixed_parts(info, target, target_b, zl, w_hidden, b_hidden, w_output, b_output)
        wanted, weights = fixed[0], fixed[1:]
        xy = spread_xy(plane_xy, xy_b)
        xz = spread_xz(info, xzs, zl)

        order = [(0,), (-1,), (1,), (half,)] + [(-d, d) for d in range(half - 1, 1, -1)]
        part_xy, parts_xz, parts_yz = None, {}, {}
        send_ahead, send_back = None, None
        for group in order:
            part_xy, lines, blocks = block_grads(
                [slot[o] for o in group], weights, wanted, xy, xz, [yzs[o] for o in group], part_xy
            )
            for o, line, block in zip(group, lines, blocks):
                parts_xz[slot[o]], parts_yz[o] = line, block
            if group == (1,):
                around = borders(info, (plane_xy, plane_xz, plane_yz), lines[0])
        block = parts_yz[half]
        send_ahead, send_back = to_ring(block[:middle], 1), to_ring(block[middle:], -1)
        for d in range(half - 1, 0, -1):
            if d == half - 1:
                send_ahead = jnp.pad(send_ahead, ((0, middle), (0, 0)))
                send_back = jnp.pad(send_back, ((middle, 0), (0, 0)))
            send_ahead, send_back = parts_yz[d] + send_ahead, parts_yz[-d] + send_back
            send_ahead, send_back = to_ring(send_ahead, 1), to_ring(send_back, -1)

        pieces = collect_xz(info, [parts_xz[i] for i in range(chips)], plane_xz.shape, zl)
        grad_xy, far_xy = collect_xy(part_xy, plane_xy, xy_b)
        sides = [pieces[2 * s] + to_core(pieces[2 * s + 1]) for s in range(1, peers)]
        grads_xz = [to_gy(side, -s) for s, side in enumerate(sides, 1)]
        near_xz, far_xz = pieces[0], to_core(pieces[1])
        for extra in grads_xz[1:]:
            near_xz = near_xz + extra
        count = START + iteration + 1
        channels, rows, width = plane_xy.shape
        state = (plane_xz, first_xz, second_xz)
        plane_xz, first_xz, second_xz = update_one(
            info, count, around, state, (near_xz, far_xz, grads_xz[0]), 2 * width, channels * rows
        )
        state = (plane_xy, first_xy, second_xy)
        far_xy = to_core(far_xy)
        plane_xy, first_xy, second_xy = update_one(
            info, count, around, state, (grad_xy, far_xy), 0, 0
        )
        (plane_yz, first_yz, second_yz), lanes = update_yz(
            info, count, around, (plane_yz, first_yz, second_yz), (parts_yz[0], send_ahead, send_back)
        )
    return (
        plane_xy,
        plane_xz,
        plane_yz,
        first_xy,
        first_xz,
        first_yz,
        second_xy,
        second_xz,
        second_yz,
    )


def solution(mesh):
    return jax.shard_map(
        per_device,
        mesh=mesh,
        in_specs=(
            P("gx", None, "gy"),
            P(None, "gx", "gy"),
            P(None, "gx", "gy"),
            P(None, "gx", "gy"),
            P(None, "gx", "gy"),
            P(None, "gx", "gy"),
            P(None, "gx", "gy"),
            P(None, "gx", "gy"),
            P(None, "gx", "gy"),
            P(None, "gx", "gy"),
            P(),
            P(),
            P(),
            P(),
        ),
        out_specs=(
            P(None, "gx", "gy"),
            P(None, "gx", "gy"),
            P(None, "gx", "gy"),
            P(None, "gx", "gy"),
            P(None, "gx", "gy"),
            P(None, "gx", "gy"),
            P(None, "gx", "gy"),
            P(None, "gx", "gy"),
            P(None, "gx", "gy"),
        ),
        check_vma=False,
    )
```

```python
import functools
import jax
import jax.numpy as jnp
from jax import lax
from jax.experimental import pallas as pl
from jax.experimental.pallas import tpu as pltpu
from jax.sharding import PartitionSpec as P


STEPS = 2
START = 20


SMOOTHING = 0.5
BETA_ONE = 0.9
BETA_TWO = 0.99
LEARN_RATE = 0.01
EPSILON = 1e-08

LANES = 128
CHANNELS = 32
UNROLL = 4
GRADS_VMEM = 16 * 2**20
BOTH = ("gx", "gy")
f32 = jnp.float32
bf16 = jnp.bfloat16


def ring_order(chips):
    return list(range(0, chips, 2)) + list(range(chips - 1, 0, -2))


def send(x, move):
    n, peers = lax.axis_size("gx"), lax.axis_size("gy")
    pairs = []
    for g in range(n):
        for y in range(peers):
            to = move(g // 2, g % 2, y)
            if to is not None:
                pairs.append((g * peers + y, (to[0] * 2 + to[1]) * peers + to[2]))
    return lax.ppermute(x, BOTH, pairs)


def to_core(x):
    return send(x, lambda k, c, y: (k, 1 - c, y))


def to_ring(x, step):
    chips = lax.axis_size("gx") // 2
    order = ring_order(chips)
    at = {k: i for i, k in enumerate(order)}
    return send(x, lambda k, c, y: (order[(at[k] + step) % chips], c, y))


def to_gy(x, step):
    peers = lax.axis_size("gy")
    return send(x, lambda k, c, y: (k, c, (y + step) % peers))


def offsets(chips):
    out = [0]
    for d in range(1, chips // 2):
        out += [-d, d]
    return out + [chips // 2]


def chip_in_slot(gx, slot, chips):
    k = gx // 2
    at = jnp.where(k % 2 == 0, k // 2, chips - 1 - k // 2)
    i = (at + offsets(chips)[slot] + chips) % chips
    return jnp.where(i < chips // 2, 2 * i, 2 * chips - 1 - 2 * i)


def vmem(count):
    return [pl.BlockSpec(memory_space=pltpu.VMEM)] * count


SCALARS = pl.BlockSpec(memory_space=pltpu.SMEM)
SMALL = pltpu.CompilerParams(vmem_limit_bytes=20 * 2**20)


def cost(flops, size):
    return pl.CostEstimate(flops=flops, bytes_accessed=size, transcendentals=0)


def diagonal(small, times):
    size = small.shape[0] * times
    wide = jnp.concatenate([small.astype(f32)] * times, axis=1)
    full = jnp.concatenate([wide] * times, axis=0)
    row = lax.broadcasted_iota(jnp.int32, (size, size), 0) // small.shape[0]
    col = lax.broadcasted_iota(jnp.int32, (size, size), 1) // small.shape[0]
    return jnp.where(row == col, full, 0.0)


def fixed_kernel(
    chips, zl, info, b_output, target_a, target_b, w, b, o, wanted, w_in, w_out, w_back, bias, scale
):
    gx = info[0]
    x_count = target_a.shape[0]
    starts = [
        pl.multiple_of((2 * chip_in_slot(gx, s, chips) + gx % 2) * zl, zl) for s in range(chips)
    ]
    for side, ref in enumerate((target_a, target_b)):

        def one(x, carry):
            rows = jnp.concatenate([ref[x, pl.ds(z, zl), :] for z in starts], axis=0)
            rows = rows - b_output[0]
            high = rows.astype(bf16).astype(f32)
            both = jnp.concatenate([high, rows - high], axis=0)
            wanted[side * x_count + x] = both.T.astype(bf16)
            return carry

        lax.fori_loop(0, x_count, one, 0)
    times = w_in.shape[0] // w.shape[0]
    wide, line = w[...].astype(f32), o[...].astype(f32)
    w_in[...] = diagonal(0.5 * wide, times).astype(bf16)
    w_out[...] = diagonal(jnp.broadcast_to(line, wide.shape).T, times).astype(bf16)
    w_back[...] = diagonal(wide.T, times).astype(bf16)
    bias[...] = jnp.concatenate([0.5 * b[...]] * times, axis=1)
    scale[...] = jnp.concatenate([0.5 * line] * times, axis=1)


def fixed_parts(info, target, target_b, zl, w_hidden, b_hidden, w_output, b_output):
    chips = lax.axis_size("gx") // 2
    x_count, z_count, y_count = target.shape
    hidden = w_hidden.shape[1]
    width = zl * hidden
    square = jax.ShapeDtypeStruct((width, width), bf16)
    line = jax.ShapeDtypeStruct((1, width), f32)
    return pl.pallas_call(
        functools.partial(fixed_kernel, chips, zl),
        in_specs=[SCALARS, SCALARS] + vmem(5),
        out_specs=vmem(6),
        out_shape=[
            jax.ShapeDtypeStruct((2 * x_count, y_count, z_count), bf16),
            square,
            square,
            square,
            line,
            line,
        ],
        compiler_params=SMALL,
        cost_estimate=cost(0, 4 * 2**20),
    )(
        info,
        b_output,
        target,
        target_b,
        w_hidden,
        b_hidden[None],
        w_output[None],
    )


def lanes_kernel(plane, out):
    c, zl, _ = plane.shape
    per = LANES // c
    for t in range(zl // per):
        rows = jnp.concatenate([plane[:, t * per + j, :] for j in range(per)], axis=0)
        out[:, t * LANES : (t + 1) * LANES] = rows.T


def lanes_yz(plane):
    c, zl, y = plane.shape
    return pl.pallas_call(
        lanes_kernel,
        in_specs=vmem(1),
        out_specs=vmem(1)[0],
        out_shape=jax.ShapeDtypeStruct((y, zl * c), f32),
        compiler_params=SMALL,
        cost_estimate=cost(0, 2**18),
    )(plane)


def z_places(gx, gy, slot, chips, peers, zl, zs):
    z = (2 * chip_in_slot(gx, slot, chips) + gx % 2) * zl
    return (gy - z // zs + peers) % peers * zs + z % zs


def spread_xy_kernel(xy_a, xy_b, xy):
    c, x_count, _ = xy_a.shape

    def some(i, carry):
        for x in range(UNROLL):
            x += i * UNROLL
            for side, ref in enumerate((xy_a, xy_b)):
                xy[side * x_count + x] = jnp.concatenate([ref[:, x, :]] * (LANES // c), axis=0).T
        return carry

    lax.fori_loop(0, x_count // UNROLL, some, 0)


def spread_xy(xy_a, xy_b):
    _, x_count, y_count = xy_a.shape
    return pl.pallas_call(
        spread_xy_kernel,
        in_specs=vmem(2),
        out_specs=vmem(1)[0],
        out_shape=jax.ShapeDtypeStruct((2 * x_count, y_count, LANES), f32),
        compiler_params=SMALL,
        cost_estimate=cost(0, 3 * 2**20),
    )(xy_a, xy_b)


def spread_xz_kernel(chips, peers, zl, info, *refs):
    xzs, xz, held = refs[: 2 * peers], refs[2 * peers : -1], refs[-1]
    _, x_count, zs = xzs[0].shape

    def some(i, carry):
        for x in range(UNROLL):
            x += i * UNROLL
            for s in range(peers):
                for side in range(2):
                    held[s * zs : (s + 1) * zs, side * x_count + x, :] = xzs[2 * s + side][:, x, :].T
        return carry

    lax.fori_loop(0, x_count // UNROLL, some, 0)
    for p in range(chips):
        at = z_places(info[0], info[1], p, chips, peers, zl, zs)
        xz[p][...] = jnp.concatenate([held[at + j] for j in range(zl)], axis=1)


def spread_xz(info, xzs, zl):
    peers, chips = lax.axis_size("gy"), lax.axis_size("gx") // 2
    c, x_count, zs = xzs[0].shape
    return pl.pallas_call(
        functools.partial(spread_xz_kernel, chips, peers, zl),
        in_specs=[SCALARS] + vmem(len(xzs)),
        out_specs=vmem(chips),
        out_shape=[jax.ShapeDtypeStruct((2 * x_count, zl * c), f32)] * chips,
        scratch_shapes=[pltpu.VMEM((peers * zs, 2 * x_count, c), f32)],
        compiler_params=SMALL,
        cost_estimate=cost(0, 3 * 2**20),
    )(info, *xzs)


def collect_xy_kernel(part, xy_a, xy_b, *outs):
    c, x_count, _ = xy_a.shape

    def some(i, carry):
        for x in range(UNROLL):
            x += i * UNROLL
            for side, ref in enumerate((xy_a, xy_b)):
                rows = part[side * x_count + x].T
                total = sum(rows[j * c : (j + 1) * c] for j in range(LANES // c))
                outs[side][:, x, :] = total / ref[:, x, :]
        return carry

    lax.fori_loop(0, x_count // UNROLL, some, 0)


def collect_xy(part, xy_a, xy_b):
    return pl.pallas_call(
        collect_xy_kernel,
        in_specs=vmem(3),
        out_specs=vmem(2),
        out_shape=[jax.ShapeDtypeStruct(xy_a.shape, f32)] * 2,
        compiler_params=SMALL,
        cost_estimate=cost(0, 4 * 2**20),
    )(part, xy_a, xy_b)


def collect_xz_kernel(chips, peers, zl, info, *refs):
    parts, outs, held = refs[:chips], refs[chips : chips + 2 * peers], refs[chips + 2 * peers]
    c, x_count, zs = outs[0].shape
    half = x_count // 2
    held[...] = jnp.zeros_like(held)
    for p in range(chips):
        at = z_places(info[0], info[1], p, chips, peers, zl, zs)
        rows = parts[p][...]
        for j in range(zl):
            held[at + j] = rows[:, j * c : (j + 1) * c]

    def turned(s, side, x):
        return held[s * zs : (s + 1) * zs, side * x_count + x, :].T

    def some(i, carry):
        for x in range(UNROLL // 2):
            x += i * (UNROLL // 2)
            for side in range(2):
                for far in (0, half):
                    outs[side][:, x + far, :] = turned(0, side, x + far)
                for s in range(1, peers):
                    pair = turned(s, side, x), turned(s, side, x + half)
                    outs[2 * s + side][:, x, :] = jnp.concatenate(pair, axis=1)
        return carry

    lax.fori_loop(0, half // (UNROLL // 2), some, 0)


def collect_xz(info, parts, shape, zl):
    peers, chips = lax.axis_size("gy"), lax.axis_size("gx") // 2
    c, x_count, zs = shape
    return pl.pallas_call(
        functools.partial(collect_xz_kernel, chips, peers, zl),
        in_specs=[SCALARS] + vmem(chips),
        out_specs=vmem(2 * peers),
        out_shape=[jax.ShapeDtypeStruct(shape, f32)] * 2
        + [jax.ShapeDtypeStruct((c, x_count // 2, 2 * zs), f32)] * (2 * peers - 2),
        scratch_shapes=[pltpu.VMEM((peers * zs, 2 * x_count, c), f32)],
        compiler_params=SMALL,
        cost_estimate=cost(0, 4 * 2**20),
    )(info, *parts)


def grads_kernel(count, first, slot, w_in, w_out, w_back, bias, scale, wanted, xy, *refs):
    refs = list(refs)
    take = lambda k: [refs.pop(0) for _ in range(k)]
    xzs, yzs = take(count), take(count)
    before = None if first else take(1)[0]
    gxy = take(1)[0]
    gxzs, gyzs = take(count), take(count)
    pick, xz, yzb, gxz, gyz = refs
    step = pl.program_id(0)
    x_count, y_count, _ = xy.shape
    width = w_in.shape[0]
    z_count = wanted.shape[2] // 2
    zl = width // CHANNELS
    times = width // LANES

    @pl.when(step == 0)
    def _():
        row = lax.broadcasted_iota(jnp.int32, (2 * z_count, width), 0) % z_count
        col = lax.broadcasted_iota(jnp.int32, (2 * z_count, width), 1) // CHANNELS
        for j in range(count):
            pick[j, :width] = w_out[...]
            pick[j, width:] = jnp.where(row == (slot[0] + j) * zl + col, -1.0, 0.0).astype(bf16)
            yzb[j] = yzs[j][...]
        gyz[...] = jnp.zeros_like(gyz)

    for j in range(count):
        xz[j] = xzs[j][...]
    if first:
        gxy[...] = jnp.zeros_like(gxy)
    else:
        gxy[...] = before[...]

    def one_block(j, carry):
        yz = yzb[j]
        lines = [xz[j, x : x + 1, :] for x in range(x_count)]
        pairs = [jnp.concatenate([xy[x]] * times, axis=1) * yz for x in range(x_count)]
        features = jnp.concatenate([(g * r).astype(bf16) for g, r in zip(pairs, lines)], axis=0)
        half = jnp.dot(features, w_in[...], preferred_element_type=f32) + bias[...]
        t = jnp.tanh(half)
        up = 1.0 + t
        hidden = half * up
        slope = (up + hidden * (1.0 - t)) * scale[...]
        residual = jnp.dot(
            jnp.concatenate(
                [
                    hidden.astype(bf16),
                    jnp.concatenate([wanted[x] for x in range(x_count)], axis=0),
                ],
                axis=1,
            ),
            pick[j],
            preferred_element_type=f32,
        )
        back_hidden = (residual * slope).astype(bf16)
        back = jnp.dot(back_hidden, w_back[...], preferred_element_type=f32)
        total = None
        for x in range(x_count):
            b = back[x * y_count : (x + 1) * y_count] * pairs[x]
            gxz[j, x : x + 1, :] = jnp.sum(b, axis=0, keepdims=True)
            e = b * lines[x]
            gxy[x] += sum(e[:, h * LANES : (h + 1) * LANES] for h in range(times))
            total = e if total is None else total + e
        gyz[j] += total
        return carry

    lax.fori_loop(0, count, one_block, 0)
    for j in range(count):
        gxzs[j][...] = gxz[j]

    @pl.when(step == 1)
    def _():
        for j in range(count):
            gyzs[j][...] = gyz[j] / yzb[j]


def block_grads(slots, weights, wanted, xy, xzs, yzs, before):
    count = len(slots)
    rows, y_count, _ = xy.shape
    rows = rows // 2
    width = yzs[0].shape[1]

    def whole(a):
        return pl.BlockSpec(a.shape, lambda i: (0,) * a.ndim)

    side = pl.BlockSpec((rows, y_count, LANES), lambda i: (i, 0, 0))
    line = pl.BlockSpec((rows, width), lambda i: (i, 0))
    outs = pl.pallas_call(
        functools.partial(grads_kernel, count, before is None),
        grid=(2,),
        in_specs=[SCALARS]
        + [whole(w) for w in weights]
        + [side, side]
        + [line] * count
        + [whole(a) for a in yzs]
        + ([] if before is None else [side]),
        out_specs=[side] + [line] * count + [whole(a) for a in yzs],
        out_shape=[jax.ShapeDtypeStruct(xy.shape, f32)]
        + [jax.ShapeDtypeStruct((2 * rows, width), f32)] * count
        + [jax.ShapeDtypeStruct(a.shape, f32) for a in yzs],
        scratch_shapes=[
            pltpu.VMEM((count, width + wanted.shape[2], width), bf16),
            pltpu.VMEM((count, rows, width), f32),
            pltpu.VMEM((count, y_count, width), f32),
            pltpu.VMEM((count, rows, width), f32),
            pltpu.VMEM((count, y_count, width), f32),
        ],
        compiler_params=pltpu.CompilerParams(vmem_limit_bytes=GRADS_VMEM),
        cost_estimate=cost(12 * rows * y_count * count * width * width, count * 10 * 2**20),
    )(
        jnp.array(slots[:1], jnp.int32),
        *weights,
        wanted,
        xy,
        *[xzs[s] for s in slots],
        *yzs,
        *([] if before is None else [before]),
    )
    return outs[0], outs[1 : 1 + count], outs[1 + count :]


def near_sides(p, above, below, left, right):
    rows, cols = p.shape[1:]
    row = lax.broadcasted_iota(jnp.int32, p.shape, 1)
    col = lax.broadcasted_iota(jnp.int32, p.shape, 2)
    up = jnp.where(row == 0, above, pltpu.roll(p, 1, 1))
    down = jnp.where(row == rows - 1, below, pltpu.roll(p, rows - 1, 1))
    wide = p if cols % LANES == 0 else jnp.concatenate([p] * (LANES // cols), axis=2)
    back = pltpu.roll(wide, 1, 2)[:, :, :cols]
    ahead = pltpu.roll(wide, wide.shape[2] - 1, 2)[:, :, :cols]
    return up, down, jnp.where(col == 0, left, back), jnp.where(col == cols - 1, right, ahead)


def upright(ref, at, shape):
    c, rows, cols = shape
    line = ref[:, at : at + c * rows]
    return jnp.broadcast_to(line, (cols, c * rows)).T.reshape(shape)


def update(info, ends, count, plane, first, second, grad, borders, at_row, at_col, outs):
    chip, core, left, right = borders
    odd = info[0] % 2 == 1
    above, below = jnp.where(odd, core[...], chip[...]), jnp.where(odd, chip[...], core[...])
    p = plane[...]
    rows, cols = p.shape[1:]
    above = jnp.where(info[0] == 0, p[:, :1, :], above[:, :, at_row : at_row + cols])
    below = jnp.where(info[0] == ends[0], p[:, rows - 1 :, :], below[:, :, at_row : at_row + cols])
    left = jnp.where(info[1] == 0, p, upright(left, at_col, p.shape))
    right = jnp.where(info[1] == ends[1], p, upright(right, at_col, p.shape))
    up, down, back, ahead = near_sides(p, above, below, left, right)
    grad = grad + 2.0 * SMOOTHING * ((p - up) + (p - down) + (p - back) + (p - ahead))
    m = BETA_ONE * first[...] + (1.0 - BETA_ONE) * grad
    v = BETA_TWO * second[...] + (1.0 - BETA_TWO) * grad * grad
    corr_one = 1.0 - BETA_ONE**count
    corr_two = 1.0 - BETA_TWO**count
    outs[1][...] = m
    outs[2][...] = v
    outs[0][...] = p - LEARN_RATE * (m / corr_one) / (jnp.sqrt(v / corr_two) + EPSILON)


def update_one_kernel(ends, count, at_row, at_col, info, above, below, left, right, *refs):
    state, grads, outs = refs[:3], refs[3:-3], refs[-3:]
    grad = 0.0
    for ref in grads:
        g = ref[...]
        if g.shape != state[0].shape:
            wide = g.shape[2] // 2
            g = jnp.concatenate([g[:, :, :wide], g[:, :, wide:]], axis=1)
        grad = grad + g
    borders = (above, below, left, right)
    update(info, ends, count, *state, grad, borders, at_row, at_col, outs)


def update_one(info, count, borders, state, grads, at_row, at_col):
    ends = (lax.axis_size("gx") - 1, lax.axis_size("gy") - 1)
    return pl.pallas_call(
        functools.partial(update_one_kernel, ends, count, at_row, at_col),
        in_specs=[SCALARS] + vmem(7 + len(grads)),
        out_specs=vmem(3),
        out_shape=[jax.ShapeDtypeStruct(a.shape, f32) for a in state],
        compiler_params=SMALL,
        cost_estimate=cost(0, 2 * 2**20),
    )(info, *borders, *state, *grads)


def update_yz_kernel(ends, count, info, above, below, left, right, plane, first, second, a, b, d, *refs):
    outs, lanes, held = refs[:3], refs[3], refs[4]
    c, zl, width = plane.shape
    per = LANES // c
    for t in range(zl // per):
        at = slice(t * LANES, (t + 1) * LANES)
        rows = (a[:, at] + b[:, at] + d[:, at]).T
        for j in range(per):
            held[:, t * per + j, :] = rows[j * c : (j + 1) * c]
    borders = (above, below, left, right)
    at_col = left.shape[1] - c * zl
    update(info, ends, count, plane, first, second, held[...], borders, width, at_col, outs)
    lanes_kernel(outs[0], lanes)


def update_yz(info, count, borders, state, parts):
    ends = (lax.axis_size("gx") - 1, lax.axis_size("gy") - 1)
    outs = pl.pallas_call(
        functools.partial(update_yz_kernel, ends, count),
        in_specs=[SCALARS] + vmem(10),
        out_specs=vmem(4),
        out_shape=[jax.ShapeDtypeStruct(a.shape, f32) for a in (*state, parts[0])],
        scratch_shapes=[pltpu.VMEM(state[0].shape, f32)],
        compiler_params=SMALL,
        cost_estimate=cost(0, 2 * 2**20),
    )(info, *borders, *state, *parts)
    return outs[:3], outs[3]


def edges_kernel(peers, info, xy, xz, yz, gate, *outs):
    width = xy.shape[2]
    for ref, at in ((xy, 0), (yz, width), (xz, 2 * width)):
        rows, cols = ref.shape[1:]
        last, first = ref[:, rows - 1 :, :], ref[:, :1, :]
        odd = info[0] % 2 == 1
        outs[0][:, :, at : at + cols] = jnp.where(odd, last, first)
        outs[1][:, :, at : at + cols] = jnp.where(odd, first, last)
    at = 0
    for ref in (xy, xz, yz):
        c, rows, cols = ref.shape
        flat = ref[...].reshape(c * rows, cols).T
        last, first = flat[cols - 1 :], flat[:1]
        here = slice(at, at + c * rows)
        if peers == 2:
            outs[2][:, here] = jnp.where(info[1] == 0, last, first)
        else:
            outs[2][:, here] = last
            outs[3][:, here] = first
        at += c * rows


def borders(info, planes, gate):
    n, peers = lax.axis_size("gx"), lax.axis_size("gy")
    c = planes[0].shape[0]
    row = jax.ShapeDtypeStruct((c, 1, sum(p.shape[2] for p in planes)), f32)
    col = jax.ShapeDtypeStruct((1, sum(c * p.shape[1] for p in planes)), f32)
    outs = pl.pallas_call(
        functools.partial(edges_kernel, peers),
        in_specs=[SCALARS] + vmem(3) + [pl.BlockSpec(memory_space=pl.ANY)],
        out_specs=vmem(3 if peers == 2 else 4),
        out_shape=[row, row] + [col] * (1 if peers == 2 else 2),
        compiler_params=SMALL,
        cost_estimate=cost(0, 2**20),
    )(info, *planes, gate)

    def next_chip(k, c, y):
        to = k + 1 if c == 1 else k - 1
        return (to, 1 - c, y) if 0 <= to < n // 2 else None

    chip, core = send(outs[0], next_chip), to_core(outs[1])
    if peers == 2:
        left = right = lax.ppermute(outs[2], "gy", [(0, 1), (1, 0)])
    else:
        up = [(i, i + 1) for i in range(peers - 1)]
        left = lax.ppermute(outs[2], "gy", up)
        right = lax.ppermute(outs[3], "gy", [(j, i) for i, j in up])
    return chip, core, left, right


def per_device(
    target,
    plane_xy,
    plane_xz,
    plane_yz,
    first_xy,
    first_xz,
    first_yz,
    second_xy,
    second_xz,
    second_yz,
    w_hidden,
    b_hidden,
    w_output,
    b_output,
):
    peers = lax.axis_size("gy")
    info = jnp.stack([lax.axis_index("gx"), lax.axis_index("gy")]).astype(jnp.int32)
    zl = plane_yz.shape[1]
    lanes = lanes_yz(plane_yz)
    target_b = to_core(target)
    fixed = None

    chips = lax.axis_size("gx") // 2
    half = chips // 2
    slot = {o: i for i, o in enumerate(offsets(chips))}
    middle = lanes.shape[0] // 2

    for iteration in range(STEPS):
        back, ahead = {0: lanes}, {0: lanes}
        for d in range(1, half):
            back[d], ahead[d] = to_ring(back[d - 1], 1), to_ring(ahead[d - 1], -1)
        parts = to_ring(back[half - 1][:middle], 1), to_ring(ahead[half - 1][middle:], -1)
        far = jnp.concatenate(parts, axis=0)
        yzs = {0: lanes, half: far}
        for d in range(1, half):
            yzs[-d], yzs[d] = back[d], ahead[d]
        xy_b, xz_b = to_core(plane_xy), to_core(plane_xz)
        xzs = [plane_xz, xz_b]
        for s in range(1, peers):
            xz_y = to_gy(plane_xz, s)
            xzs += [xz_y, to_core(xz_y)]
        if fixed is None:
            fixed = fixed_parts(info, target, target_b, zl, w_hidden, b_hidden, w_output, b_output)
        wanted, weights = fixed[0], fixed[1:]
        xy = spread_xy(plane_xy, xy_b)
        xz = spread_xz(info, xzs, zl)

        order = [(0,), (-1,), (1,), (half,)] + [(-d, d) for d in range(half - 1, 1, -1)]
        part_xy, parts_xz, parts_yz = None, {}, {}
        send_ahead, send_back = None, None
        for group in order:
            part_xy, lines, blocks = block_grads(
                [slot[o] for o in group], weights, wanted, xy, xz, [yzs[o] for o in group], part_xy
            )
            for o, line, block in zip(group, lines, blocks):
                parts_xz[slot[o]], parts_yz[o] = line, block
            if group == (1,):
                around = borders(info, (plane_xy, plane_xz, plane_yz), lines[0])
        block = parts_yz[half]
        send_ahead, send_back = to_ring(block[:middle], 1), to_ring(block[middle:], -1)
        for d in range(half - 1, 0, -1):
            if d == half - 1:
                send_ahead = jnp.pad(send_ahead, ((0, middle), (0, 0)))
                send_back = jnp.pad(send_back, ((middle, 0), (0, 0)))
            send_ahead, send_back = parts_yz[d] + send_ahead, parts_yz[-d] + send_back
            send_ahead, send_back = to_ring(send_ahead, 1), to_ring(send_back, -1)

        pieces = collect_xz(info, [parts_xz[i] for i in range(chips)], plane_xz.shape, zl)
        grad_xy, far_xy = collect_xy(part_xy, plane_xy, xy_b)
        sides = [pieces[2 * s] + to_core(pieces[2 * s + 1]) for s in range(1, peers)]
        grads_xz = [to_gy(side, -s) for s, side in enumerate(sides, 1)]
        far_xz, across_xz = to_core(pieces[1]), grads_xz[0]
        for extra in grads_xz[1:]:
            across_xz = across_xz + extra
        count = START + iteration + 1
        channels, rows, width = plane_xy.shape
        state = (plane_xz, first_xz, second_xz)
        plane_xz, first_xz, second_xz = update_one(
            info, count, around, state, (pieces[0], far_xz, across_xz), 2 * width, channels * rows
        )
        state = (plane_xy, first_xy, second_xy)
        far_xy = to_core(far_xy)
        plane_xy, first_xy, second_xy = update_one(
            info, count, around, state, (grad_xy, far_xy), 0, 0
        )
        (plane_yz, first_yz, second_yz), lanes = update_yz(
            info, count, around, (plane_yz, first_yz, second_yz), (parts_yz[0], send_ahead, send_back)
        )
    return (
        plane_xy,
        plane_xz,
        plane_yz,
        first_xy,
        first_xz,
        first_yz,
        second_xy,
        second_xz,
        second_yz,
    )


def solution(mesh):
    return jax.shard_map(
        per_device,
        mesh=mesh,
        in_specs=(
            P("gx", None, "gy"),
            P(None, "gx", "gy"),
            P(None, "gx", "gy"),
            P(None, "gx", "gy"),
            P(None, "gx", "gy"),
            P(None, "gx", "gy"),
            P(None, "gx", "gy"),
            P(None, "gx", "gy"),
            P(None, "gx", "gy"),
            P(None, "gx", "gy"),
            P(),
            P(),
            P(),
            P(),
        ),
        out_specs=(
            P(None, "gx", "gy"),
            P(None, "gx", "gy"),
            P(None, "gx", "gy"),
            P(None, "gx", "gy"),
            P(None, "gx", "gy"),
            P(None, "gx", "gy"),
            P(None, "gx", "gy"),
            P(None, "gx", "gy"),
            P(None, "gx", "gy"),
        ),
        check_vma=False,
    )
```
